32 devices in a mesh: fsdp: 2 (over x), ctx: 4 (over z), tp: 4 (over y, core).
Axes of the slice: x: 2, y: 2, z: 4, core: 2. Of those that a mesh axis runs over, the one named last changes fastest.
Arguments:
- hidden: bfloat16 [2, 4096, 768], P('fsdp', 'ctx'), may hold values from -6 to 6
- prefix: int32 [2], P('fsdp'), may hold values from 0 to 1024, as said below
- w_qkv: bfloat16 [768, 3, 768], P('fsdp', None, 'tp'), may hold values from -0.21875 to 0.21875
- b_qkv: bfloat16 [3, 12, 64], P(None, 'tp', 'fsdp'), may hold values from -3 to 3
- w_out: bfloat16 [768, 768], P('tp', 'fsdp'), may hold values from -1.75 to 1.75
- b_out: bfloat16 [768], P('fsdp'), may hold values from -2 to 2
- w_up: bfloat16 [768, 3072], P('fsdp', 'tp'), may hold values from -0.21875 to 0.21875
- b_up: bfloat16 [48, 64], P('tp', 'fsdp'), may hold values from -3 to 3
- w_down: bfloat16 [3072, 768], P('tp', 'fsdp'), may hold values from -0.109375 to 0.109375
- b_down: bfloat16 [768], P('fsdp'), may hold values from -2 to 2
- ln1_gain: bfloat16 [768], P('fsdp'), may hold values from 0.5 to 1.5
- ln1_shift: bfloat16 [768], P('fsdp'), may hold values from -2 to 2
- ln2_gain: bfloat16 [768], P('fsdp'), may hold values from 0.5 to 1.5
- ln2_shift: bfloat16 [768], P('fsdp'), may hold values from -2 to 2
- cotangent: bfloat16 [2, 4096, 768], P('fsdp', 'ctx'), may hold values from -6 to 6
Outputs:
- result: bfloat16 [2, 4096, 768], P('fsdp', 'ctx')
- grad_hidden: float32 [2, 4096, 768], P('fsdp', 'ctx')
- grad_w_qkv: float32 [768, 3, 768], P('fsdp', None, 'tp')
- grad_b_qkv: float32 [3, 12, 64], P(None, 'tp', 'fsdp')
- grad_w_out: float32 [768, 768], P('tp', 'fsdp')
- grad_b_out: float32 [768], P('fsdp')
- grad_w_up: float32 [768, 3072], P('fsdp', 'tp')
- grad_b_up: float32 [48, 64], P('tp', 'fsdp')
- grad_w_down: float32 [3072, 768], P('tp', 'fsdp')
- grad_b_down: float32 [768], P('fsdp')
- grad_ln1_gain: float32 [768], P('fsdp')
- grad_ln1_shift: float32 [768], P('fsdp')
- grad_ln2_gain: float32 [768], P('fsdp')
- grad_ln2_shift: float32 [768], P('fsdp')
The draws below stay inside these ranges and needn't reach their ends.
Inputs may be any that keep to these rules, and one draw needn't show every extreme that they name: One sequence has a prefix of exactly 1024 positions.
All inputs are finite; a program needn't handle non-finite values.
Results may differ from the reference program's by a relative error of at most 0.012.
The reference program's roundings to bfloat16 on the way count: a program that leaves them out, or rounds other values in their place, can miss the bound.
Values may be sent and summed in bfloat16 or wider, within the bound.
No kernel may reach another device: no remote copies, remote signals or barrier semaphores. Data moves between devices by JAX's collectives and lax.ppermute only.
A program may use at most 192 MiB of HBM per device.

```python
from functools import partial
import jax
import jax.numpy as jnp
from jax import lax

D = 768
HEADS = 12
HD = 64
FF = 3072
BLOCK = 16
SEQ_LEN = 2048
SEQS = 2
FF_ROWS = 48


def draw_prefix(key, part):
    value_key = jax.random.fold_in(key, 101)
    place_key = jax.random.fold_in(key, 202)
    values = jax.random.randint(value_key, (SEQS,), 0, SEQ_LEN // 2 + 1, dtype=jnp.int32)
    chosen = jax.random.randint(place_key, (), 0, SEQS, dtype=jnp.int32)
    places = jnp.arange(SEQS, dtype=jnp.int32)
    return jnp.where(places == chosen, jnp.int32(SEQ_LEN // 2), values)


def shard_levels(rng, shape, pieces, smallest, high):
    factor_of = 1.0
    for axis_at, shards_of in pieces:
        heights = jax.random.uniform(jax.random.fold_in(jax.random.fold_in(rng, 6), axis_at), (shards_of,), jnp.float32, smallest / len(pieces), high / len(pieces))
        factor_of = factor_of * jnp.repeat(jnp.exp(heights), shape[axis_at] // shards_of).reshape((-1,) + (1,) * (len(shape) - 1 - axis_at))
    return factor_of


def bell_draw(key, dims, spread, bound, pieces=(), held_as=jnp.bfloat16):
    drawn = jax.random.normal(key, dims, jnp.float32) * spread
    if len(pieces) > 0:
        drawn = shard_levels(key, dims, pieces, -0.22, 0.18) * drawn
    return jnp.clip(drawn, min=-bound, max=bound).astype(held_as)


def setup_inputs(seed: int = 0) -> dict:
    streams_of = jax.random.split(jax.random.key(seed), 16)
    return {
        "hidden": bell_draw(streams_of[0], (SEQS, 2 * SEQ_LEN, D), 1.0, 6.0, ((0, 2), (1, 4))),
        "prefix": draw_prefix(jax.random.fold_in(streams_of[15], 71), 0),
        "w_qkv": bell_draw(streams_of[2], (D, 3, D), D ** -0.5, 0.21875, ((0, 2), (2, 4))),
        "b_qkv": bell_draw(streams_of[3], (3, HEADS, HD), 0.5, 3.0, ((1, 4), (2, 2))),
        "w_out": bell_draw(streams_of[4], (D, D), HEADS ** -0.5, 1.75, ((0, 4), (1, 2))),
        "b_out": bell_draw(streams_of[5], (D,), 0.3, 2.0, ((0, 2),)),
        "w_up": bell_draw(streams_of[6], (D, FF), D ** -0.5, 0.21875, ((0, 2), (1, 4))),
        "b_up": bell_draw(streams_of[7], (FF_ROWS, HD), 0.5, 3.0, ((0, 4), (1, 2))),
        "w_down": bell_draw(streams_of[8], (FF, D), FF ** -0.5, 0.109375, ((0, 4), (1, 2))),
        "b_down": bell_draw(streams_of[9], (D,), 0.3, 2.0, ((0, 2),)),
        "ln1_gain": jnp.clip(1.0 + 0.1 * jax.random.normal(streams_of[10], (D,), jnp.float32), 0.5, 1.5).astype(jnp.bfloat16),
        "ln1_shift": bell_draw(streams_of[11], (D,), 0.3, 2.0, ((0, 2),)),
        "ln2_gain": jnp.clip(1.0 + 0.1 * jax.random.normal(streams_of[12], (D,), jnp.float32), 0.5, 1.5).astype(jnp.bfloat16),
        "ln2_shift": bell_draw(streams_of[13], (D,), 0.3, 2.0, ((0, 2),)),
        "cotangent": bell_draw(streams_of[14], (SEQS, 2 * SEQ_LEN, D), 1.0, 6.0, ((0, 2), (1, 4))),
    }


epsilon = 1e-05
HIGH = lax.Precision.HIGHEST

@jax.custom_vjp
def low(v):
    return lax.optimization_barrier(v.astype(jnp.bfloat16)).astype(jnp.float32)

@jax.custom_vjp
def low_back(v):
    return v

def low_keep(v):
    return (low(v), None)

def low_pass(kept, grad):
    return (grad,)

def back_keep(v):
    return (v, None)

def back_low(kept, grad):
    return (low(grad),)
low.defvjp(low_keep, low_pass)
low_back.defvjp(back_keep, back_low)

def norm_rows(values, gain_value, shift_value):
    row_mean = lax.optimization_barrier(jnp.mean(values, axis=-1, keepdims=True))
    centered = values - row_mean
    variance = lax.optimization_barrier(jnp.mean(centered * centered, axis=-1, keepdims=True))
    return centered * lax.rsqrt(variance + epsilon) * gain_value + shift_value

def rotate(values, cosine, sine_value):
    half_width = values.shape[-1] // 2
    first_half = values[..., :half_width]
    second = values[..., half_width:]
    return jnp.concatenate([first_half * cosine - second * sine_value, second * cosine + first_half * sine_value], axis=-1)

def angles(positions):
    half_width = HD // 2
    frequency = jnp.power(jnp.float32(10000.0), -2.0 * jnp.arange(half_width, dtype=jnp.float32) / HD)
    angle_rows = positions.astype(jnp.float32)[:, None] * frequency[None, :]
    return (jnp.cos(angle_rows)[:, None, :], jnp.sin(angle_rows)[:, None, :])

def visible(query_rows, key_rows, prefix_len):
    q_noisy = query_rows < SEQ_LEN
    k_noisy = key_rows < SEQ_LEN
    q_place = jnp.where(q_noisy, query_rows, query_rows - SEQ_LEN)
    k_place = jnp.where(k_noisy, key_rows, key_rows - SEQ_LEN)
    q_block = (q_place // BLOCK)[:, None]
    k_block = (k_place // BLOCK)[None, :]
    q_flag = q_noisy[:, None]
    k_flag = k_noisy[None, :]
    same_block = q_flag & k_flag & (q_block == k_block)
    earlier = q_flag & ~k_flag & (k_block < q_block)
    causal = ~q_flag & ~k_flag & (k_block <= q_block)
    opened = ~k_flag & (k_place[None, :] < prefix_len)
    return same_block | earlier | causal | opened

def apply_layer(values, w_qkv, b_qkv, w_out, b_out, w_up, b_up, w_down, b_down, gain_one, shift_one, gain_two, shift_two, allowed, cosine, sine_value):
    row_count = values.shape[0]
    normed = low(norm_rows(values, gain_one, shift_one))
    projected = jnp.einsum('nd,dcj->ncj', normed, w_qkv, precision=HIGH) + b_qkv.reshape(3, D)
    projected = low_back(projected)
    queries = low(rotate(projected[:, 0].reshape(row_count, HEADS, HD), cosine, sine_value))
    key_heads = low(rotate(projected[:, 1].reshape(row_count, HEADS, HD), cosine, sine_value))
    value_heads = low(projected[:, 2].reshape(row_count, HEADS, HD))
    score_scale = HD ** (-0.5)

    def one_head(head_item):
        query_head, key_head, value_head = head_item
        scores = low_back(jnp.dot(query_head, key_head.T, precision=HIGH) * score_scale)
        scores = jnp.where(allowed, scores, -1e+30)
        row_top = lax.optimization_barrier(jnp.max(scores, axis=-1, keepdims=True))
        weights = jnp.exp(scores - row_top)
        probs = weights / lax.optimization_barrier(jnp.sum(weights, axis=-1, keepdims=True))
        return jnp.dot(low(probs), value_head, precision=HIGH)
    heads_out = lax.map(jax.checkpoint(one_head), (jnp.transpose(queries, (1, 0, 2)), jnp.transpose(key_heads, (1, 0, 2)), jnp.transpose(value_heads, (1, 0, 2))))
    attended = jnp.transpose(heads_out, (1, 0, 2)).reshape(row_count, D)
    attended = low(low_back(attended))
    branch = low_back(jnp.dot(attended, w_out, precision=HIGH) + b_out)
    middle = values + branch
    normed_two = low(norm_rows(middle, gain_two, shift_two))
    pre_act = low_back(jnp.dot(normed_two, w_up, precision=HIGH) + b_up.reshape(FF))
    activated = low(jax.nn.gelu(pre_act, approximate=False))
    mlp_out = low_back(jnp.dot(activated, w_down, precision=HIGH) + b_down)
    return middle + mlp_out

def reference(hidden, prefix, w_qkv, b_qkv, w_out, b_out, w_up, b_up, w_down, b_down, ln1_gain, ln1_shift, ln2_gain, ln2_shift, cotangent):
    params = tuple((p.astype(jnp.float32) for p in (w_qkv, b_qkv, w_out, b_out, w_up, b_up, w_down, b_down, ln1_gain, ln1_shift, ln2_gain, ln2_shift)))
    row_ids = jnp.arange(2 * SEQ_LEN, dtype=jnp.int32)
    positions = jnp.where(row_ids < SEQ_LEN, row_ids, row_ids - SEQ_LEN)
    cosine, sine_value = angles(positions)

    def scan_step(totals, scan_item):
        seq_values, seq_grad, seq_prefix = scan_item
        allowed = visible(row_ids, row_ids, seq_prefix)
        layer_fn = partial(apply_layer, allowed=allowed, cosine=cosine, sine_value=sine_value)
        seq_out, pull_back = jax.vjp(layer_fn, seq_values, *params)
        grads = pull_back(seq_grad)
        totals = tuple((t + g for t, g in zip(totals, grads[1:])))
        return (totals, (seq_out.astype(jnp.bfloat16), grads[0]))
    initial = tuple((jnp.zeros_like(p) for p in params))
    totals, (outputs, grad_input) = lax.scan(scan_step, initial, (hidden.astype(jnp.float32), cotangent.astype(jnp.float32), prefix))
    return (outputs, grad_input, totals[0], totals[1], totals[2], totals[3], totals[4], totals[5], totals[6], totals[7], totals[8], totals[9], totals[10], totals[11])
```

```python
import functools
import jax
import jax.numpy as jnp
from jax import lax
from jax.experimental import pallas as pl
from jax.experimental.pallas import tpu as pltpu
from jax.sharding import PartitionSpec as P

HD = 64
BLOCK = 16
TILE = 256
LOG2E = 1.4426950408889634
NEG = -1e30


def stack_heads(rows, heads):
    lane = lax.broadcasted_iota(jnp.int32, rows.shape, 1) // HD
    return jnp.concatenate([jnp.where(lane == h, rows, jnp.zeros_like(rows)) for h in range(heads)], axis=0)


def tile_plan(sc_ref, i, tiles):
    z, s, pfx = sc_ref[0], sc_ref[1], sc_ref[2]
    half = sc_ref[3]
    noisy = z < half
    late = lax.rem(z, half)
    place = late * tiles + (i ^ s)
    below = i ^ s
    full_f = late * tiles
    plain = below + full_f
    opened = jnp.where(late == 0, (pfx + TILE - 1) // TILE, 0)
    top = jnp.maximum(below + 1, opened)
    masked = top - below
    total = plain + masked + noisy.astype(jnp.int32)

    def address(slot):
        near = tiles + (slot ^ s)
        far = 2 * tiles + (slot - below)
        edge = tiles + (((slot - plain + below) & (tiles - 1)) ^ s)
        own = i
        at = jnp.where(slot < below, near, jnp.where(slot < plain, far, jnp.where(slot < plain + masked, edge, own)))
        return pl.multiple_of(at * TILE, TILE)

    def mask_terms(slot):
        is_own = slot >= plain + masked
        tile_at = slot - plain + below
        return is_own, tile_at

    return noisy, late, below, plain, masked, total, address, mask_terms, pfx


def allowed(q_pos, k_pos, q_tile, k_tile, is_own, noisy, prefix):
    qb = q_tile * (TILE // BLOCK) + q_pos // BLOCK
    kb = k_tile * (TILE // BLOCK) + k_pos // BLOCK
    step = jnp.where(noisy, 0, 1)
    seen = (kb < qb + step) | (k_tile * TILE + k_pos < prefix)
    return seen


def fwd_kernel(tiles, heads, sc_ref, q_ref, k_ref, v_ref, o_ref, lse_ref, sbuf, mbuf, lbuf, acc):
    i = pl.program_id(0)
    noisy, late, below, plain, masked, total, address, mask_terms, pfx = tile_plan(sc_ref, i, tiles)
    width = heads * HD
    qs = stack_heads(q_ref[...], heads)
    mbuf[...] = jnp.full_like(mbuf, NEG)
    lbuf[...] = jnp.zeros_like(lbuf)
    acc[...] = jnp.zeros_like(acc)

    def score(slot):
        k = k_ref[pl.ds(address(slot), TILE), :]
        return lax.dot_general(qs, k, (((1,), (1,)), ((), ())), preferred_element_type=jnp.float32)

    def keep(slot, s):
        sbuf[slot] = s
        mbuf[...] = jnp.maximum(mbuf[...], jnp.maximum(s[:, :128], s[:, 128:]))

    def plain_step(slot, carry):
        keep(slot, score(slot))
        return carry

    lax.fori_loop(0, plain, plain_step, 0)
    q_pos = lax.broadcasted_iota(jnp.int32, (heads * TILE, TILE), 0) & (TILE - 1)
    k_pos = lax.broadcasted_iota(jnp.int32, (heads * TILE, TILE), 1)
    prefix = jnp.where(late == 0, pfx, 0)

    def edge_step(slot, carry):
        s = score(slot)
        seen = allowed(q_pos, k_pos, below, slot - plain + below, None, noisy, prefix)
        keep(slot, jnp.where(seen, s, NEG))
        return carry

    lax.fori_loop(plain, plain + masked, edge_step, 0)

    @pl.when(noisy)
    def _():
        slot = plain + masked
        s = score(slot)
        keep(slot, jnp.where(q_pos // BLOCK == k_pos // BLOCK, s, NEG))

    top = jnp.max(mbuf[...], axis=1, keepdims=True) * LOG2E
    mbuf[...] = jnp.broadcast_to(top, mbuf.shape)

    def sum_step(slot, carry):
        v = v_ref[pl.ds(address(slot), TILE), :]
        m = mbuf[...]
        s = sbuf[slot]
        p0 = jnp.exp2(s[:, :128] * LOG2E - m)
        p1 = jnp.exp2(s[:, 128:] * LOG2E - m)
        lbuf[...] += p0 + p1
        p = jnp.concatenate([p0, p1], axis=1).astype(jnp.bfloat16)
        acc[...] += jnp.dot(p, v, preferred_element_type=jnp.float32)
        return carry

    lax.fori_loop(0, total, sum_step, 0)
    norm = jnp.sum(lbuf[...], axis=1, keepdims=True)
    out = acc[...] * (1.0 / norm)
    lane = lax.broadcasted_iota(jnp.int32, (TILE, width), 1) // HD
    picked = out[:TILE]
    for h in range(1, heads):
        picked = jnp.where(lane == h, out[h * TILE : (h + 1) * TILE], picked)
    o_ref[...] = picked.astype(o_ref.dtype)
    lse = jnp.broadcast_to(top + jnp.log2(norm), (heads * TILE, 128))
    lse_ref[0] = jnp.concatenate([lse[h * TILE : (h + 1) * TILE].T[:1] for h in range(heads)] + [jnp.zeros((8 - heads, TILE), jnp.float32)], axis=0)


def attention(scalars, q, k, v):
    rows, width = q.shape
    tiles, heads = rows // TILE, width // HD
    whole = lambda i, sc: (0, 0)
    slots = 2 * tiles + 1
    return pl.pallas_call(
        functools.partial(fwd_kernel, tiles, heads),
        name="attn_fwd",
        out_shape=(jax.ShapeDtypeStruct((rows, width), jnp.bfloat16), jax.ShapeDtypeStruct((tiles, 8, TILE), jnp.float32)),
        grid_spec=pltpu.PrefetchScalarGridSpec(
            num_scalar_prefetch=1,
            grid=(tiles,),
            in_specs=[
                pl.BlockSpec((TILE, width), lambda i, sc: (i, 0)),
                pl.BlockSpec(k.shape, whole),
                pl.BlockSpec(v.shape, whole),
            ],
            out_specs=[
                pl.BlockSpec((TILE, width), lambda i, sc: (i, 0)),
                pl.BlockSpec((1, 8, TILE), lambda i, sc: (i, 0, 0)),
            ],
            scratch_shapes=[
                pltpu.VMEM((slots, heads * TILE, TILE), jnp.float32),
                pltpu.VMEM((heads * TILE, 128), jnp.float32),
                pltpu.VMEM((heads * TILE, 128), jnp.float32),
                pltpu.VMEM((heads * TILE, width), jnp.float32),
            ],
        ),
        compiler_params=pltpu.CompilerParams(dimension_semantics=("arbitrary",), vmem_limit_bytes=48 << 20),
        cost_estimate=pl.CostEstimate(flops=12_000_000_000, bytes_accessed=4_000_000, transcendentals=0),
    )(scalars, q, k, v)


def bwd_kernel(tiles, heads, sc_ref, q_ref, o_ref, g_ref, lse_ref, k_ref, v_ref, dq_ref, dk_ref, dv_ref, dqt, st, gt, lse_s, del_s, qs_s, gs_s):
    i = pl.program_id(0)
    noisy, late, below, plain, masked, total, address, mask_terms, pfx = tile_plan(sc_ref, i, tiles)
    width = heads * HD

    @pl.when(i == 0)
    def _():
        dk_ref[...] = jnp.zeros_like(dk_ref)
        dv_ref[...] = jnp.zeros_like(dv_ref)

    q = q_ref[...]
    g = g_ref[...]
    qs_s[...] = stack_heads(q, heads)
    gs_s[...] = stack_heads(g, heads)
    q_t = q.astype(jnp.float32).T
    g_t = g.astype(jnp.float32).T
    prod = (o_ref[...].astype(jnp.float32) * g.astype(jnp.float32)).T
    head_of = lax.broadcasted_iota(jnp.int32, (width, TILE), 0) // HD
    for h in range(heads):
        cols = slice(h * TILE, (h + 1) * TILE)
        st[:, cols] = jnp.where(head_of == h, q_t, 0.0).astype(jnp.bfloat16)
        gt[:, cols] = jnp.where(head_of == h, g_t, 0.0).astype(jnp.bfloat16)
        del_s[:, cols] = jnp.sum(prod[h * HD : (h + 1) * HD], axis=0, keepdims=True)
        lse_s[:, cols] = lse_ref[0, h : h + 1, :]
    dqt[...] = jnp.zeros_like(dqt)

    def step(slot, mask):
        at = address(slot)
        k = k_ref[pl.ds(at, TILE), :]
        v = v_ref[pl.ds(at, TILE), :]
        s = jnp.dot(k, st[...], preferred_element_type=jnp.float32)
        p = jnp.exp2(s * LOG2E - lse_s[...])
        if mask is not None:
            p = jnp.where(mask, p, 0.0)
        dp = jnp.dot(v, gt[...], preferred_element_type=jnp.float32)
        ds = (p * (dp - del_s[...])).astype(jnp.bfloat16)
        p = p.astype(jnp.bfloat16)
        dv_ref[pl.ds(at, TILE), :] += jnp.dot(p, gs_s[...], preferred_element_type=jnp.float32)
        dk_ref[pl.ds(at, TILE), :] += jnp.dot(ds, qs_s[...], preferred_element_type=jnp.float32)
        dqt[...] += lax.dot_general(k, ds, (((0,), (0,)), ((), ())), preferred_element_type=jnp.float32)

    def plain_step(slot, carry):
        step(slot, None)
        return carry

    lax.fori_loop(0, plain, plain_step, 0)
    k_pos = lax.broadcasted_iota(jnp.int32, (TILE, heads * TILE), 0)
    q_pos = lax.broadcasted_iota(jnp.int32, (TILE, heads * TILE), 1) & (TILE - 1)
    prefix = jnp.where(late == 0, pfx, 0)

    def edge_step(slot, carry):
        step(slot, allowed(q_pos, k_pos, below, slot - plain + below, None, noisy, prefix))
        return carry

    lax.fori_loop(plain, plain + masked, edge_step, 0)

    @pl.when(noisy)
    def _():
        step(plain + masked, q_pos // BLOCK == k_pos // BLOCK)

    dq_t = jnp.where(head_of == 0, dqt[:, :TILE], 0.0)
    for h in range(1, heads):
        dq_t = jnp.where(head_of == h, dqt[:, h * TILE : (h + 1) * TILE], dq_t)
    dq_ref[...] = dq_t.T * (HD**-0.5)


def attention_grads(scalars, q, o, g, lse, k, v):
    rows, width = q.shape
    tiles, heads = rows // TILE, width // HD
    whole = lambda i, sc: (0, 0)
    tile = pl.BlockSpec((TILE, width), lambda i, sc: (i, 0))
    return pl.pallas_call(
        functools.partial(bwd_kernel, tiles, heads),
        name="attn_bwd",
        out_shape=(
            jax.ShapeDtypeStruct((rows, width), jnp.float32),
            jax.ShapeDtypeStruct(k.shape, jnp.float32),
            jax.ShapeDtypeStruct(v.shape, jnp.float32),
        ),
        grid_spec=pltpu.PrefetchScalarGridSpec(
            num_scalar_prefetch=1,
            grid=(tiles,),
            in_specs=[
                tile,
                tile,
                tile,
                pl.BlockSpec((1, 8, TILE), lambda i, sc: (i, 0, 0)),
                pl.BlockSpec(k.shape, whole),
                pl.BlockSpec(v.shape, whole),
            ],
            out_specs=[tile, pl.BlockSpec(k.shape, whole), pl.BlockSpec(v.shape, whole)],
            scratch_shapes=[
                pltpu.VMEM((width, heads * TILE), jnp.float32),
                pltpu.VMEM((width, heads * TILE), jnp.bfloat16),
                pltpu.VMEM((width, heads * TILE), jnp.bfloat16),
                pltpu.VMEM((1, heads * TILE), jnp.float32),
                pltpu.VMEM((1, heads * TILE), jnp.float32),
                pltpu.VMEM((heads * TILE, width), jnp.bfloat16),
                pltpu.VMEM((heads * TILE, width), jnp.bfloat16),
            ],
        ),
        compiler_params=pltpu.CompilerParams(dimension_semantics=("arbitrary",), vmem_limit_bytes=48 << 20),
        cost_estimate=pl.CostEstimate(flops=30_000_000_000, bytes_accessed=12_000_000, transcendentals=0),
    )(scalars, q, o, g, lse, k, v)


epsilon = 1e-05
PAIR = [(0, 1), (1, 0)]


def low(values):
    return values.astype(jnp.bfloat16)


def wide(values):
    return values.astype(jnp.float32)


def dot(a, b, ca=1, cb=0):
    return lax.dot_general(a, b, (((ca,), (cb,)), ((), ())), preferred_element_type=jnp.float32)


def row_stats(values):
    mean = jnp.mean(values, axis=-1, keepdims=True)
    centered = values - mean
    variance = jnp.mean(centered * centered, axis=-1, keepdims=True)
    return mean, lax.rsqrt(variance + epsilon)


def normalize(values, gain, shift):
    mean, scale = row_stats(values)
    return (values - mean) * scale * gain + shift


def norm_grad(grad, values, gain):
    mean, scale = row_stats(values)
    unit = (values - mean) * scale
    weighted = grad * gain
    return scale * (weighted - jnp.mean(weighted, axis=-1, keepdims=True) - unit * jnp.mean(weighted * unit, axis=-1, keepdims=True))


def rotate(values, cosine, sine):
    rows, width = values.shape
    split = values.reshape(rows, width // HD, HD)
    first, second = split[..., : HD // 2], split[..., HD // 2 :]
    return jnp.concatenate([first * cosine - second * sine, second * cosine + first * sine], axis=-1).reshape(rows, width)


def angles(positions):
    half_width = HD // 2
    frequency = jnp.power(jnp.float32(10000.0), -2.0 * jnp.arange(half_width, dtype=jnp.float32) / HD)
    angle_rows = wide(positions)[:, None] * frequency[None, :]
    return (jnp.cos(angle_rows)[:, None, :], jnp.sin(angle_rows)[:, None, :])


def swap_core(values):
    return lax.ppermute(values, "tp", [(i, i ^ 1) for i in range(4)])


def swap_y(values):
    return lax.ppermute(values, "tp", [(i, i ^ 2) for i in range(4)])


def hop(values, pairs):
    return lax.ppermute(values, "ctx", pairs)


def pick(parts, index):
    return lax.dynamic_index_in_dim(parts, index, 0, keepdims=False)


def ordered(first, second, flip):
    return jnp.where(flip == 0, jnp.stack([first, second]), jnp.stack([second, first]))


def sum_ctx(values, z):
    near, far = z & 1, z >> 1
    near_pairs, far_pairs = [(i, i ^ 1) for i in range(4)], [(i, i ^ 2) for i in range(4)]
    rows, cols = values.shape
    halves = values.reshape(2, rows // 2, cols)
    half = pick(halves, near) + wide(hop(low(pick(halves, 1 - near)), near_pairs))
    quarters = half.reshape(2, rows // 4, cols)
    quarter = low(pick(quarters, far) + wide(hop(low(pick(quarters, 1 - far)), far_pairs)))
    half = ordered(quarter, hop(quarter, far_pairs), far).reshape(rows // 2, cols)
    return wide(ordered(half, hop(half, near_pairs), near).reshape(rows, cols))


def body(
    hidden,
    prefix,
    w_qkv,
    b_qkv,
    w_out,
    b_out,
    w_up,
    b_up,
    w_down,
    b_down,
    ln1_gain,
    ln1_shift,
    ln2_gain,
    ln2_shift,
    cotangent,
):
    members = lax.axis_size("fsdp")
    paired = members == 2
    z = lax.axis_index("ctx")
    t = lax.axis_index("tp")
    half_ctx = lax.axis_size("ctx") // 2
    core, side = t & 1, t >> 1
    turn = 2 * core + side
    f = lax.axis_index("fsdp") if paired else jnp.int32(0)
    rows, width = hidden.shape[1], hidden.shape[2]
    local = w_qkv.shape[2]
    units = w_up.shape[1]
    tiles = rows // TILE
    half, quarter = rows // 2, rows // 4
    part = width // 2

    def turned(values):
        grid = values.reshape(tiles, TILE, 2, part)
        near = lax.dynamic_index_in_dim(grid, f, 2, keepdims=False)
        far = lax.dynamic_index_in_dim(grid, 1 - f, 2, keepdims=False)
        both = jnp.concatenate([near, far], axis=-1)
        return jnp.concatenate([pick(both, j ^ turn) for j in range(tiles)], axis=0)

    def unturned(values):
        grid = values.reshape(tiles, TILE, width)
        grid = jnp.concatenate([pick(grid, j ^ turn) for j in range(tiles)], axis=0)
        return jnp.where(f == 0, grid, jnp.concatenate([grid[:, part:], grid[:, :part]], axis=1))

    def gathered(values, axis):
        if paired:
            return jnp.concatenate([values, lax.ppermute(values, "fsdp", PAIR)], axis=axis)
        return lax.all_gather(values, "fsdp", axis=axis, tiled=True)

    small = jnp.concatenate(
        [v.reshape(-1) for v in (ln1_gain, ln1_shift, b_qkv, b_out, ln2_gain, ln2_shift, b_up, b_down)]
    )
    if paired:
        own_small, other_small = small, lax.ppermute(small, "fsdp", PAIR)
        pieces = [own_small, other_small]
    else:
        pieces = list(lax.all_gather(small, "fsdp", axis=0, tiled=False))
    sizes = [v.size for v in (ln1_gain, ln1_shift, b_qkv, b_out, ln2_gain, ln2_shift, b_up, b_down)]
    starts = [sum(sizes[:n]) for n in range(len(sizes))]

    def vector(n):
        return wide(jnp.concatenate([p[starts[n] : starts[n] + sizes[n]] for p in pieces]))

    def folded(n, shape):
        parts = [p[starts[n] : starts[n] + sizes[n]].reshape(shape) for p in pieces]
        if paired:
            parts = [jnp.where(f == 0, parts[0], parts[1]), jnp.where(f == 0, parts[1], parts[0])]
        return wide(jnp.concatenate(parts, axis=-1)).reshape(-1)

    gain_one, shift_one = vector(0), vector(1)
    bias_qkv = folded(2, b_qkv.shape)
    bias_out, gain_two, shift_two = vector(3), vector(4), vector(5)
    bias_up = folded(6, b_up.shape)
    bias_down = vector(7)

    full_qkv = gathered(w_qkv.reshape(w_qkv.shape[0], 3 * local), 0)
    values_low = turned(hidden[0])

    own_quarter = values_low[:quarter]
    near_quarter = hop(own_quarter, [(i + half_ctx, i) for i in range(half_ctx)])
    near_quarter = jnp.where(z >= half_ctx, own_quarter, near_quarter)
    far_quarter = hop(own_quarter, [(2, 1)]) + hop(own_quarter, [(2, 3)])

    def spread(values):
        pair = jnp.concatenate([values, swap_y(values)], axis=0)
        return [pair, swap_core(pair)]

    seen_low = jnp.concatenate(spread(near_quarter) + spread(far_quarter), axis=0)

    full_out = gathered(w_out, 1)
    full_up = gathered(w_up, 0)
    full_down = gathered(w_down, 1)

    values = wide(values_low)
    upstream_low = turned(cotangent[0])

    tile_at = jnp.concatenate([jnp.full((TILE,), j, jnp.int32) ^ turn for j in range(tiles)])
    place = tile_at * TILE + (jnp.arange(rows, dtype=jnp.int32) & (TILE - 1))
    cos_own, sin_own = angles(place + (z % half_ctx) * rows)
    cos_far, sin_far = angles(place)
    cos_seen, sin_seen = jnp.concatenate([cos_own, cos_far]), jnp.concatenate([sin_own, sin_far])

    normed = low(normalize(values, gain_one, shift_one))
    projected = dot(normed, full_qkv) + bias_qkv
    score_scale = HD ** (-0.5)
    queries = low(rotate(projected[:, :local], cos_own, sin_own)) * jnp.bfloat16(score_scale)
    keys_own = low(rotate(projected[:, local : 2 * local], cos_own, sin_own))
    values_own = low(projected[:, 2 * local :])
    normed_seen = low(normalize(wide(seen_low), gain_one, shift_one))
    projected_seen = dot(normed_seen, full_qkv[:, local:]) + bias_qkv[local:]
    keys_seen = low(rotate(projected_seen[:, :local], cos_seen, sin_seen))
    values_seen = low(projected_seen[:, local:])
    keys_all = jnp.concatenate([keys_own, keys_seen], axis=0)
    values_all = jnp.concatenate([values_own, values_seen], axis=0)
    scalars = jnp.stack([z, turn, prefix[0], jnp.int32(half_ctx)]).astype(jnp.int32)
    attended, log_sums = attention(scalars, queries, keys_all, values_all)

    def reduced_half(first, second):
        return low(first + wide(swap_core(low(second))))

    def summed_half(first, second):
        mine = reduced_half(first, second)
        theirs = swap_y(mine)
        return wide(mine) + wide(jnp.concatenate([theirs[quarter:], theirs[:quarter]], axis=0))

    branch = summed_half(dot(attended[:half], full_out), dot(attended[half:], full_out))
    middle = values[:half] + branch + bias_out
    two_own = low(normalize(middle, gain_two, shift_two))
    two = (two_own, swap_core(two_own))
    dy = (upstream_low[:half], upstream_low[half:])
    acts, slopes = [], []
    for h in range(2):
        pre = dot(two[h], full_up) + bias_up
        cdf = 0.5 * (1.0 + lax.erf(pre * (2.0**-0.5)))
        acts.append(low(pre * cdf))
        slopes.append(cdf + pre * jnp.exp(-0.5 * pre * pre) * ((2.0 * jnp.pi) ** -0.5))
    grads_pre = [low(dot(dy[h], full_down, 1, 1) * slopes[h]) for h in range(2)]
    da_two = summed_half(dot(grads_pre[0], full_up, 1, 1), dot(grads_pre[1], full_up, 1, 1))
    dmid = wide(dy[0]) + norm_grad(da_two, middle, gain_two)
    dz_own = low(dmid)
    dz = (dz_own, swap_core(dz_own))
    grad_att = jnp.concatenate([low(dot(dz[h], full_out, 1, 1)) for h in range(2)], axis=0)

    down = summed_half(dot(acts[0], full_down), dot(acts[1], full_down))
    result_own = low(middle + down + bias_down)
    result = unturned(jnp.concatenate([result_own, swap_core(result_own)], axis=0))

    g_up = sum(dot(two[h], grads_pre[h], 0, 0) for h in range(2))
    g_down = sum(dot(dy[h], acts[h], 0, 0) for h in range(2))
    g_out = sum(dot(dz[h], attended[h * half : (h + 1) * half], 0, 0) for h in range(2))
    gb_up = sum(jnp.sum(wide(grads_pre[h]), axis=0) for h in range(2))
    gb_down = sum(jnp.sum(wide(dy[h]), axis=0) for h in range(2)) * 0.25
    gb_out = jnp.sum(wide(dz_own), axis=0) * 0.5

    def own_rows(values):
        if paired:
            return values[:part] + wide(lax.ppermute(low(values[part:]), "fsdp", PAIR))
        return lax.psum_scatter(values, "fsdp", scatter_dimension=0, tiled=True)

    def reduce_weights(values):
        return sum_ctx(own_rows(values), z)

    first_group = reduce_weights(jnp.concatenate([g_up, g_down], axis=1))

    dq, dk, dv = attention_grads(scalars, queries, attended, grad_att, log_sums, keys_all, values_all)
    dproj = low(
        jnp.concatenate([rotate(dq, cos_own, -sin_own), rotate(dk[:rows], cos_own, -sin_own), dv[:rows]], axis=1)
    )
    dproj_seen = low(jnp.concatenate([rotate(dk[rows:], cos_seen, -sin_seen), dv[rows:]], axis=1))
    share = dot(dproj, full_qkv, 1, 1)
    share_seen = dot(dproj_seen, full_qkv[:, local:], 1, 1)
    share_near, share_far = share_seen[:rows], share_seen[rows:]

    def quarter_of(values):
        mine = values[:half] + wide(swap_core(low(values[half:])))
        return mine[:quarter] + wide(swap_y(low(mine[quarter:])))

    far_q = low(quarter_of(share_far))
    near_q = quarter_of(share_near)
    near_in = wide(hop(low(near_q), [(i, i + half_ctx) for i in range(half_ctx)]))
    far_in = wide(hop(far_q, [(1, 2)])) + wide(hop(far_q, [(3, 2)]))
    da_one = quarter_of(share) + far_in + jnp.where(z >= half_ctx, near_q + near_in, 0.0)
    grad_q = low(dmid[:quarter] + norm_grad(da_one, values[:quarter], gain_one))
    grad_half = jnp.concatenate([grad_q, swap_y(grad_q)], axis=0)
    grad_input = wide(unturned(jnp.concatenate([grad_half, swap_core(grad_half)], axis=0)))

    gb_qkv = jnp.sum(wide(dproj), axis=0)
    gb_seen = jnp.sum(wide(dproj_seen), axis=0)
    gb_qkv = gb_qkv + jnp.concatenate([jnp.zeros((local,), jnp.float32), gb_seen])
    g_qkv_seen = dot(normed_seen, dproj_seen, 0, 0)
    g_qkv = dot(normed, dproj, 0, 0) + jnp.concatenate([jnp.zeros((width, local), jnp.float32), g_qkv_seen], axis=1)
    second_group = reduce_weights(jnp.concatenate([g_out, g_qkv], axis=1))

    def gain_grad(weight, grad, bias_grad, gain, shift):
        full = wide(weight)
        by_shift = jnp.sum(full * bias_grad[None, :], axis=1)
        return (jnp.sum(full * grad, axis=1) - shift * by_shift) / gain, by_shift

    g_gain_one, g_shift_one = gain_grad(full_qkv, g_qkv, gb_qkv, gain_one, shift_one)
    g_gain_two, g_shift_two = gain_grad(full_up, g_up, gb_up, gain_two, shift_two)
    over_tp = jnp.stack([gb_out, gb_down, g_gain_one, g_shift_one, g_gain_two, g_shift_two])
    over_tp = over_tp + swap_core(over_tp)
    over_tp = over_tp + swap_y(over_tp)
    if paired:
        keep = lambda v, shape: lax.dynamic_index_in_dim(v.reshape(shape), f, 1, keepdims=False)
        give = lambda v, shape: lax.dynamic_index_in_dim(v.reshape(shape), 1 - f, 1, keepdims=False)
        shape_qkv, shape_up = (gb_qkv.size // HD, 2, HD // 2), (units // HD, 2, HD // 2)
        mine = jnp.concatenate([over_tp[:, :part].reshape(-1), keep(gb_qkv, shape_qkv).reshape(-1), keep(gb_up, shape_up).reshape(-1)])
        other = jnp.concatenate([over_tp[:, part:].reshape(-1), give(gb_qkv, shape_qkv).reshape(-1), give(gb_up, shape_up).reshape(-1)])
        vectors = mine + lax.ppermute(other, "fsdp", PAIR)
    else:
        scattered = (
            lax.psum_scatter(over_tp, "fsdp", scatter_dimension=1, tiled=True),
            lax.psum_scatter(gb_qkv.reshape(-1, HD), "fsdp", scatter_dimension=1, tiled=True),
            lax.psum_scatter(gb_up.reshape(-1, HD), "fsdp", scatter_dimension=1, tiled=True),
        )
        vectors = jnp.concatenate([v.reshape(-1) for v in scattered])
    vectors = vectors + hop(vectors, [(i, i ^ 1) for i in range(4)])
    vectors = vectors + hop(vectors, [(i, i ^ 2) for i in range(4)])
    own = width // members
    named = vectors[: 6 * own].reshape(6, own)
    n_qkv, n_up = b_qkv.size, b_up.size
    out_b_qkv = vectors[6 * own : 6 * own + n_qkv].reshape(b_qkv.shape)
    out_b_up = vectors[6 * own + n_qkv :].reshape(b_up.shape)
    return (
        result[None],
        grad_input[None],
        second_group[:, local:].reshape(w_qkv.shape),
        out_b_qkv,
        second_group[:, :local].T,
        named[0],
        first_group[:, :units],
        out_b_up,
        first_group[:, units:].T,
        named[1],
        named[2],
        named[3],
        named[4],
        named[5],
    )


def solution(mesh):
    rows = P("fsdp", "ctx", None)
    weights = (P("fsdp", None, "tp"), P(None, "tp", "fsdp"), P("tp", "fsdp"), P("fsdp"), P("fsdp", "tp"), P("tp", "fsdp"), P("tp", "fsdp"))
    vectors = (P("fsdp"),) * 5
    return jax.shard_map(
        body,
        mesh=mesh,
        in_specs=(rows, P("fsdp")) + weights + vectors + (rows,),
        out_specs=(rows, rows) + weights + vectors,
        check_vma=False,
    )
```

```python
import functools
import jax
import jax.numpy as jnp
from jax import lax
from jax.experimental import pallas as pl
from jax.experimental.pallas import tpu as pltpu
from jax.sharding import PartitionSpec as P

HD = 64
BLOCK = 16
TILE = 256
WIDE = 512
LOG2E = 1.4426950408889634
NEG = -1e30
epsilon = 1e-05
BF, F32 = jnp.bfloat16, jnp.float32


def low(values):
    return values.astype(BF)


def wide(values):
    return values.astype(F32)


def dot(a, b, ca=1, cb=0):
    return lax.dot_general(a, b, (((ca,), (cb,)), ((), ())), preferred_element_type=F32)


def shape(dims, kind):
    return jax.ShapeDtypeStruct(dims, kind)


def call(kernel, name, scalars, grid, ins, outs, scratch, args, flops, moved, room=24):
    return pl.pallas_call(
        kernel,
        name=name,
        out_shape=[s for s, _ in outs],
        grid_spec=pltpu.PrefetchScalarGridSpec(
            num_scalar_prefetch=1, grid=grid, in_specs=ins, out_specs=[b for _, b in outs], scratch_shapes=scratch
        ),
        compiler_params=pltpu.CompilerParams(dimension_semantics=("arbitrary",) * len(grid), vmem_limit_bytes=room << 20),
        cost_estimate=pl.CostEstimate(flops=flops, bytes_accessed=moved, transcendentals=0),
    )(scalars, *args)


def whole(values):
    dims = values.shape
    return pl.BlockSpec(dims, lambda i, sc: (0,) * len(dims))


def row_block(values, index):
    return pl.BlockSpec((TILE, values.shape[1]), lambda i, sc: (index(i, sc), 0))


def turn_matrix(width):
    k = lax.broadcasted_iota(jnp.int32, (width, width), 0)
    n = lax.broadcasted_iota(jnp.int32, (width, width), 1)
    first = (n & (HD - 1)) < HD // 2
    return jnp.where(first & (k == n + HD // 2), -1.0, jnp.where((~first) & (k == n - HD // 2), 1.0, 0.0)).astype(BF)


def tile_angles(base_ref, tile_ref, index):
    cos, sin = base_ref[0], base_ref[1]
    cos_t, sin_t = tile_ref[0, pl.ds(index, 1), :], tile_ref[1, pl.ds(index, 1), :]
    return cos * cos_t - sin * sin_t, sin * cos_t + cos * sin_t


def unit_rows(x):
    mean = jnp.mean(x, axis=-1, keepdims=True)
    centered = x - mean
    variance = jnp.mean(centered * centered, axis=-1, keepdims=True)
    scale = lax.rsqrt(variance + epsilon)
    return centered * scale, scale


def project_kernel(parts, with_q, far, tiles, sc_ref, *refs):
    refs = list(refs)
    xs = [refs.pop(0) for _ in range(parts)]
    dy_ref = refs.pop(0) if with_q else None
    vec_ref, wa_ref, wb_ref, bias_ref, base_ref, tile_ref = [refs.pop(0) for _ in range(6)]
    outs = [refs.pop(0) for _ in range(3 if with_q else 2)]
    norm_ref = refs.pop(0)
    if with_q:
        keep_ref, dy_out = refs.pop(0), refs.pop(0)
    w_s, r_s, b_s, x_s, a_s = refs
    j = pl.program_id(0)
    f = sc_ref[5]
    local = outs[0].shape[1]
    part = wa_ref.shape[0]
    skip = 0 if with_q else 1
    count = len(outs)

    @pl.when(j == 0)
    def _():
        turn = turn_matrix(local)
        for n in range(count):
            cols = slice((n + skip) * local, (n + skip + 1) * local)
            w_s[n, :part] = wa_ref[:, cols]
            w_s[n, part:] = wb_ref[:, cols]
            if n < count - 1:
                r_s[n] = low(dot(w_s[n], turn))
                b_s[n] = dot(jnp.broadcast_to(bias_ref[:, cols], (8, local)).astype(BF), turn)

    if parts == 1:
        x = wide(xs[0][...])
    else:
        for n in range(parts):

            @pl.when(j == n)
            def _(n=n):
                x_s[...] = xs[n][...]

        x = wide(x_s[...])
    unit, _ = unit_rows(x)
    a_s[...] = unit * vec_ref[0:1] + vec_ref[1:2]
    first = pl.ds(pl.multiple_of(f * part, 128), part)
    second = pl.ds(pl.multiple_of((1 - f) * part, 128), part)
    a = jnp.concatenate([low(a_s[:, first]), low(a_s[:, second])], axis=1)
    norm_ref[...] = a
    if with_q:
        keep_ref[:, :part] = xs[0][:, first]
        keep_ref[:, part:] = xs[0][:, second]
        dy_out[:, :part] = dy_ref[:, first]
        dy_out[:, part:] = dy_ref[:, second]
    at = j ^ sc_ref[1 if with_q else 2]
    cos, sin = tile_angles(base_ref, tile_ref, at if far else at + lax.rem(sc_ref[0], sc_ref[4]) * tiles)
    for n in range(count):
        cols = slice((n + skip) * local, (n + skip + 1) * local)
        u = dot(a, w_s[n]) + bias_ref[:, cols]
        if n < count - 1:
            u = u * cos + (dot(a, r_s[n]) + b_s[n, 0:1]) * sin
        u = low(u)
        if n == 0 and with_q:
            u = u * jnp.asarray(HD**-0.5, BF)
        outs[n][...] = u


def project(scalars, xs, dy, far, rows, vec, wa, wb, bias, base, turns):
    with_q = dy is not None
    width = wa.shape[0] * 2
    local = wa.shape[1] // 3
    tiles = rows // TILE
    if with_q:
        turned = lambda i, sc: i ^ sc[1]
        ins = [row_block(xs[0], turned), row_block(dy, turned)]
        args = [xs[0], dy]
        parts = 1
    else:
        ins = [pl.BlockSpec((TILE, width), lambda i, sc, n=n: (n, 0)) for _, n in xs]
        args = [v for v, _ in xs]
        parts = len(xs)
    ins += [whole(v) for v in (vec, wa, wb, bias, base, turns)]
    args += [vec, wa, wb, bias, base, turns]
    tile = lambda n: pl.BlockSpec((TILE, n), lambda i, sc: (i, 0))
    count = 3 if with_q else 2
    outs = [(shape((rows, local), BF), tile(local))] * count + [(shape((rows, width), BF), tile(width))] * (3 if with_q else 1)
    scratch = [
        pltpu.VMEM((count, width, local), BF),
        pltpu.VMEM((count - 1, width, local), BF),
        pltpu.VMEM((count - 1, 8, local), F32),
        pltpu.VMEM((TILE, width), BF),
        pltpu.VMEM((TILE, width), F32),
    ]
    return call(
        functools.partial(project_kernel, parts, with_q, far, tiles), "project" if with_q else "project_seen", scalars, (tiles,), ins, outs, scratch, args,
        2 * rows * width * local * 5, 8_000_000,
    )


def stack_heads(rows, heads):
    lane = lax.broadcasted_iota(jnp.int32, rows.shape, 1) // HD
    return jnp.concatenate([jnp.where(lane == h, rows, jnp.zeros_like(rows)) for h in range(heads)], axis=0)


def tile_plan(sc_ref, tile, tiles):
    z, prefix, half = sc_ref[0], sc_ref[3], sc_ref[4]
    noisy = z < half
    late = lax.rem(z, half)
    at = tile ^ sc_ref[1]
    prefix = jnp.where(late == 0, prefix, 0)
    top = jnp.maximum(at + 1, (prefix + TILE - 1) // TILE)
    return noisy, late == 1, at, top, prefix


def near_rows(sc_ref, t):
    return pl.ds(pl.multiple_of((t ^ sc_ref[2]) * TILE, TILE), TILE)


def edge_mask(block_gap, k_pos, t, at, noisy, prefix):
    limit = (at - t) * (TILE // BLOCK) + jnp.where(noisy, 0, 1)
    return (block_gap < limit) | (k_pos < prefix - t * TILE)


def fwd_kernel(first, stride, tiles, sc_ref, q_ref, ko_ref, vo_ref, km_ref, vm_ref, kf_ref, vf_ref, wa_ref, wb_ref, o_ref, lse_ref, share_ref, sbuf, mbuf, lbuf, acc):
    tile = first + stride * pl.program_id(0)
    noisy, late, at, top, prefix = tile_plan(sc_ref, tile, tiles)
    width = q_ref.shape[1]
    heads = width // HD
    qs = stack_heads(q_ref[...], heads)
    mbuf[...] = jnp.full_like(mbuf, NEG)
    lbuf[...] = jnp.zeros_like(lbuf)
    acc[...] = jnp.zeros_like(acc)
    high = heads * TILE
    own = pl.ds(pl.multiple_of(tile * TILE, TILE), TILE)

    def keep(slot, s):
        best = mbuf[...]
        for n in range(s.shape[1] // TILE):
            sbuf[slot + n] = s[:, n * TILE : (n + 1) * TILE]
        for n in range(s.shape[1] // 128):
            best = jnp.maximum(best, s[:, n * 128 : (n + 1) * 128])
        mbuf[...] = best

    def plain_step(t, carry):
        keep(t, dot(qs, km_ref[near_rows(sc_ref, t), :], 1, 1))
        return carry

    lax.fori_loop(0, at, plain_step, 0)
    wides = tiles * TILE // WIDE

    def far_rows(n):
        return pl.ds(pl.multiple_of(n * WIDE, WIDE), WIDE)

    def far_step(n, carry):
        keep(tiles + n * (WIDE // TILE), dot(qs, kf_ref[far_rows(n), :], 1, 1))
        return carry

    lax.fori_loop(0, jnp.where(late, wides, 0), far_step, 0)
    q_block = (lax.broadcasted_iota(jnp.int32, (high, TILE), 0) & (TILE - 1)) >> 4
    k_pos = lax.broadcasted_iota(jnp.int32, (high, TILE), 1)
    gap = (k_pos >> 4) - q_block

    def edge_step(t, carry):
        s = dot(qs, km_ref[near_rows(sc_ref, t), :], 1, 1)
        keep(t, jnp.where(edge_mask(gap, k_pos, t, at, noisy, prefix), s, NEG))
        return carry

    lax.fori_loop(at, top, edge_step, 0)

    @pl.when(noisy)
    def _():
        keep(2 * tiles, jnp.where(gap == 0, dot(qs, ko_ref[own, :], 1, 1), NEG))

    best = jnp.max(mbuf[...], axis=1, keepdims=True) * LOG2E
    mbuf[...] = jnp.broadcast_to(best, mbuf.shape)

    def add(slot, v):
        m = mbuf[...]
        total = lbuf[...]
        cols = []
        for n in range(v.shape[0] // TILE):
            s = sbuf[slot + n]
            for k in range(TILE // 128):
                p = jnp.exp2(s[:, k * 128 : (k + 1) * 128] * LOG2E - m)
                total = total + p
                cols.append(low(p))
        lbuf[...] = total
        acc[...] += dot(jnp.concatenate(cols, axis=1), v)

    def near_sum(t, carry):
        add(t, vm_ref[near_rows(sc_ref, t), :])
        return carry

    lax.fori_loop(0, top, near_sum, 0)

    def far_sum(n, carry):
        add(tiles + n * (WIDE // TILE), vf_ref[far_rows(n), :])
        return carry

    lax.fori_loop(0, jnp.where(late, wides, 0), far_sum, 0)

    @pl.when(noisy)
    def _():
        add(2 * tiles, vo_ref[own, :])

    norm = jnp.sum(lbuf[...], axis=1, keepdims=True)
    out = acc[...] * (1.0 / norm)
    lane = lax.broadcasted_iota(jnp.int32, (TILE, width), 1) // HD
    picked = out[:TILE]
    for h in range(1, heads):
        picked = jnp.where(lane == h, out[h * TILE : (h + 1) * TILE], picked)
    picked = low(picked)
    o_ref[...] = picked
    lse = jnp.broadcast_to(best + jnp.log2(norm), (high, 128))
    lse_ref[0] = jnp.concatenate(
        [lse[h * TILE : (h + 1) * TILE].T[:1] for h in range(heads)] + [jnp.zeros((8 - heads, TILE), F32)], axis=0
    )
    part = wa_ref.shape[1]
    share_ref[:, :part] = low(dot(picked, wa_ref[...]))
    share_ref[:, part:] = low(dot(picked, wb_ref[...]))


def attention(scalars, first, stride, q, keys, values, wa, wb):
    rows, width = q.shape
    tiles, heads = rows // TILE, width // HD
    count = tiles // stride
    flat = [v for pair in zip(keys, values) for v in pair]
    tile = lambda n: pl.BlockSpec((TILE, n), lambda i, sc: (i, 0))
    full = 2 * wa.shape[1]
    return call(
        functools.partial(fwd_kernel, first, stride, tiles), "attn_fwd", scalars, (count,),
        [row_block(q, lambda i, sc: first + stride * i)] + [whole(v) for v in flat + [wa, wb]],
        [
            (shape((count * TILE, width), BF), tile(width)),
            (shape((count, 8, TILE), F32), pl.BlockSpec((1, 8, TILE), lambda i, sc: (i, 0, 0))),
            (shape((count * TILE, full), BF), tile(full)),
        ],
        [
            pltpu.VMEM((2 * tiles + 1, heads * TILE, TILE), F32),
            pltpu.VMEM((heads * TILE, 128), F32),
            pltpu.VMEM((heads * TILE, 128), F32),
            pltpu.VMEM((heads * TILE, width), F32),
        ],
        [q] + flat + [wa, wb], 3_000_000_000 * count, 4_000_000,
    )


def turn_back(grad, cos, sin, turn):
    moved = grad * sin
    high = low(moved)
    rest = low(moved - wide(high))
    return low(grad * cos - (dot(high, turn) + dot(rest, turn)))


def bwd_kernel(first, stride, tiles, sc_ref, q_ref, o_ref, za_ref, zb_ref, lse_ref, ko_ref, vo_ref, km_ref, vm_ref, kf_ref, vf_ref, wa_ref, wb_ref, base_ref, tile_ref,
               dq_ref, dk_ref, dv_ref, dqt, st, gt, lse_s, del_s, qs_s, gs_s, z_s, dk_s, dv_s):
    g_id = pl.program_id(0)
    tile = first + stride * g_id
    noisy, late, at, top, prefix = tile_plan(sc_ref, tile, tiles)
    width = q_ref.shape[1]
    heads = width // HD
    high = heads * TILE
    part = wa_ref.shape[1]
    rows = tiles * TILE
    per = za_ref.shape[0] // TILE

    @pl.when(g_id == 0)
    def _():
        dk_s[...] = jnp.zeros_like(dk_s)
        dv_s[...] = jnp.zeros_like(dv_s)

    for n in range(2 * per):

        @pl.when(g_id == n)
        def _(n=n):
            z_s[...] = (za_ref if n < per else zb_ref)[(n % per) * TILE : (n % per + 1) * TILE, :]

    z = z_s[...]
    g32 = dot(z[:, :part], wa_ref[...], 1, 1) + dot(z[:, part:], wb_ref[...], 1, 1)
    g = low(g32)
    g32 = wide(g)
    q = q_ref[...]
    qs_s[...] = stack_heads(q, heads)
    gs_s[...] = stack_heads(g, heads)
    q_t = wide(q).T
    g_t = g32.T
    prod = (wide(o_ref[...]) * g32).T
    head_of = lax.broadcasted_iota(jnp.int32, (width, TILE), 0) // HD
    for h in range(heads):
        cols = slice(h * TILE, (h + 1) * TILE)
        st[:, cols] = low(jnp.where(head_of == h, q_t, 0.0))
        gt[:, cols] = low(jnp.where(head_of == h, g_t, 0.0))
        del_s[:, cols] = jnp.sum(prod[h * HD : (h + 1) * HD], axis=0, keepdims=True)
        lse_s[:, cols] = lse_ref[0, h : h + 1, :]
    dqt[...] = jnp.zeros_like(dqt)

    def step(k, v, base, mask):
        n = k.shape[0]
        to = pl.ds(base, n)
        s = dot(k, st[...])
        p = jnp.exp2(s * LOG2E - lse_s[...])
        if mask is not None:
            p = jnp.where(mask, p, 0.0)
        dp = dot(v, gt[...])
        ds = low(p * (dp - del_s[...]))
        p = low(p)
        dv_s[to, :] += dot(p, gs_s[...])
        dk_s[to, :] += dot(ds, qs_s[...])
        dqt[...] += dot(k, ds, 0, 0)

    def near_at(t):
        return pl.multiple_of(rows + (t ^ sc_ref[2]) * TILE, TILE)

    def plain_step(t, carry):
        at_t = near_rows(sc_ref, t)
        step(km_ref[at_t, :], vm_ref[at_t, :], near_at(t), None)
        return carry

    lax.fori_loop(0, at, plain_step, 0)
    wides = rows // WIDE

    def far_step(n, carry):
        at_n = pl.ds(pl.multiple_of(n * WIDE, WIDE), WIDE)
        step(kf_ref[at_n, :], vf_ref[at_n, :], pl.multiple_of(2 * rows + n * WIDE, WIDE), None)
        return carry

    lax.fori_loop(0, jnp.where(late, wides, 0), far_step, 0)
    k_pos = lax.broadcasted_iota(jnp.int32, (TILE, high), 0)
    gap = (k_pos >> 4) - ((lax.broadcasted_iota(jnp.int32, (TILE, high), 1) & (TILE - 1)) >> 4)

    def edge_step(t, carry):
        at_t = near_rows(sc_ref, t)
        step(km_ref[at_t, :], vm_ref[at_t, :], near_at(t), edge_mask(gap, k_pos, t, at, noisy, prefix))
        return carry

    lax.fori_loop(at, top, edge_step, 0)

    @pl.when(noisy)
    def _():
        own = pl.ds(pl.multiple_of(tile * TILE, TILE), TILE)
        step(ko_ref[own, :], vo_ref[own, :], pl.multiple_of(tile * TILE, TILE), gap == 0)

    turn = turn_matrix(width)
    dq_t = jnp.where(head_of == 0, dqt[:, :TILE], 0.0)
    for h in range(1, heads):
        dq_t = jnp.where(head_of == h, dqt[:, h * TILE : (h + 1) * TILE], dq_t)
    late_at = late.astype(jnp.int32) * tiles
    dq_ref[...] = turn_back(dq_t.T * (HD**-0.5), *tile_angles(base_ref, tile_ref, at + late_at), turn)

    @pl.when(g_id == pl.num_programs(0) - 1)
    def _():
        dv_ref[...] = low(dv_s[...])

        def finish(base, true_tile):
            to = pl.ds(pl.multiple_of(base, TILE), TILE)
            dk_ref[to, :] = turn_back(dk_s[to, :], *tile_angles(base_ref, tile_ref, true_tile), turn)

        def all_three(j, carry):
            finish(j * TILE, (j ^ sc_ref[1]) + late_at)
            finish(rows + j * TILE, (j ^ sc_ref[2]) + late_at)
            finish(2 * rows + j * TILE, j ^ sc_ref[2])
            return carry

        lax.fori_loop(0, tiles, all_three, 0)


def attention_grads(scalars, first, stride, q, o, za, zb, lse, keys, values, wa, wb, base, turns):
    rows, width = q.shape
    tiles, heads = rows // TILE, width // HD
    count = tiles // stride
    flat = [v for pair in zip(keys, values) for v in pair]
    tile = pl.BlockSpec((TILE, width), lambda i, sc: (i, 0))
    total = pl.BlockSpec((3 * rows, width), lambda i, sc: (0, 0))
    high = heads * TILE
    return call(
        functools.partial(bwd_kernel, first, stride, tiles), "attn_bwd", scalars, (count,),
        [row_block(q, lambda i, sc: first + stride * i), tile, whole(za), whole(zb), pl.BlockSpec((1, 8, TILE), lambda i, sc: (i, 0, 0))]
        + [whole(v) for v in flat + [wa, wb, base, turns]],
        [(shape((count * TILE, width), BF), tile), (shape((3 * rows, width), BF), total), (shape((3 * rows, width), BF), total)],
        [
            pltpu.VMEM((width, high), F32),
            pltpu.VMEM((width, high), BF),
            pltpu.VMEM((width, high), BF),
            pltpu.VMEM((1, high), F32),
            pltpu.VMEM((1, high), F32),
            pltpu.VMEM((high, width), BF),
            pltpu.VMEM((high, width), BF),
            pltpu.VMEM((TILE, za.shape[1]), BF),
            pltpu.VMEM((3 * rows, width), F32),
            pltpu.VMEM((3 * rows, width), F32),
        ],
        [q, o, za, zb, lse] + flat + [wa, wb, base, turns], 8_000_000_000 * count, 10_000_000,
    )


def norm_kernel(sc_ref, x_ref, mine_ref, theirs_ref, vec_ref, mid_ref, a_ref):
    mid = wide(x_ref[...]) + (wide(mine_ref[...]) + wide(theirs_ref[...])) + vec_ref[4:5]
    mid_ref[...] = mid
    unit, _ = unit_rows(mid)
    a_ref[...] = low(unit * vec_ref[5:6] + vec_ref[6:7])


def norm_two(scalars, index, x, mine, theirs, vec):
    rows, width = mine.shape
    block = pl.BlockSpec((rows, width), lambda i, sc: (0, 0))
    return call(
        norm_kernel, "norm_two", scalars, (1,),
        [row_block(x, lambda i, sc: index), block, block, whole(vec)],
        [(shape((rows, width), F32), block), (shape((rows, width), BF), block)], [], [x, mine, theirs, vec], 10 * rows * width, 3_000_000,
    )


def norm_back(grad, x, gain):
    unit, scale = unit_rows(x)
    weighted = grad * gain
    return scale * (weighted - jnp.mean(weighted, axis=-1, keepdims=True) - unit * jnp.mean(weighted * unit, axis=-1, keepdims=True))


def norm_grad_kernel(sc_ref, dy_ref, mid_ref, mine_ref, theirs_ref, vec_ref, dmid_ref, dz_ref):
    dmid = wide(dy_ref[...]) + norm_back(wide(mine_ref[...]) + wide(theirs_ref[...]), mid_ref[...], vec_ref[5:6])
    dmid_ref[...] = dmid
    dz_ref[...] = low(dmid)


def norm_two_grad(scalars, index, dy, mid, mine, theirs, vec):
    rows, width = mid.shape
    block = pl.BlockSpec((rows, width), lambda i, sc: (0, 0))
    return call(
        norm_grad_kernel, "norm_two_grad", scalars, (1,),
        [row_block(dy, lambda i, sc: index), block, block, block, whole(vec)],
        [(shape((rows, width), F32), block), (shape((rows, width), BF), block)], [], [dy, mid, mine, theirs, vec], 20 * rows * width, 3_000_000,
    )


def mlp_kernel(sc_ref, a_ref, b_ref, dy_ref, ua_ref, ub_ref, da_ref, db_ref, bias_ref, share_ref, act_ref, pre_ref, x_s):
    g = pl.program_id(0)
    part = ua_ref.shape[0]

    @pl.when(g == 0)
    def _():
        x_s[...] = a_ref[...]

    @pl.when(g == 1)
    def _():
        x_s[...] = b_ref[...]

    x, dy = x_s[...], dy_ref[...]
    pre = dot(x[:, :part], ua_ref[...]) + dot(x[:, part:], ub_ref[...]) + bias_ref[...]
    cdf = 0.5 + 0.5 * lax.erf(pre * (2.0**-0.5))
    act_ref[...] = low(pre * cdf)
    slope = cdf + pre * (jnp.exp2(pre * pre * (-0.5 * LOG2E)) * 0.3989422804014327)
    grad = dot(dy[:, :part], da_ref[...], 1, 1) + dot(dy[:, part:], db_ref[...], 1, 1)
    dpre = low(grad * slope)
    pre_ref[...] = dpre
    share_ref[:, :part] = low(dot(dpre, ua_ref[...], 1, 1))
    share_ref[:, part:] = low(dot(dpre, ub_ref[...], 1, 1))


def mlp(scalars, first, stride, own, other, dy, ua, ub, da, db, bias):
    width, units = own.shape[1], ua.shape[1]
    tile = lambda n: pl.BlockSpec((TILE, n), lambda i, sc: (i, 0))
    return call(
        mlp_kernel, "mlp", scalars, (2,),
        [whole(own), whole(other), row_block(dy, lambda i, sc: first + stride * i)] + [whole(v) for v in (ua, ub, da, db, bias)],
        [(shape((2 * TILE, width), BF), tile(width)), (shape((2 * TILE, units), BF), tile(units)), (shape((2 * TILE, units), BF), tile(units))],
        [pltpu.VMEM((TILE, width), BF)], [own, other, dy, ua, ub, da, db, bias], 6 * 2 * TILE * width * units, 8_000_000,
    )


def share_kernel(blocks, n_q, tiles, chunks, sc_ref, *refs):
    refs = list(refs)
    dqs = [refs.pop(0) for _ in range(n_q)]
    dks = [refs.pop(0) for _ in range(chunks)]
    dvs = [refs.pop(0) for _ in range(chunks)]
    norms = [refs.pop(0) for _ in range(blocks)]
    wa_ref, wb_ref, share_ref = refs.pop(0), refs.pop(0), refs.pop(0)
    kinds = 3 if n_q else 2
    grads = [refs.pop(0) for _ in range(kinds)]
    sums = refs.pop(0)
    w_s, a_s, t_s, q_s = refs
    j = pl.program_id(0)
    local = dks[0].shape[1]
    part = wa_ref.shape[0]
    skip = 3 - kinds

    @pl.when(j == 0)
    def _():
        t_s[...] = jnp.zeros_like(t_s)
        sums[...] = jnp.zeros_like(sums)
        for n in range(kinds):
            cols = slice((n + skip) * local, (n + skip + 1) * local)
            w_s[n, :part] = wa_ref[:, cols]
            w_s[n, part:] = wb_ref[:, cols]

    for b in range(blocks):

        @pl.when((j >= b * tiles) & (j < (b + 1) * tiles))
        def _(b=b):
            a_s[...] = norms[b][...]

    a = a_s[...]
    parts = []
    if n_q == 1:
        parts.append(dqs[0][...])
    elif n_q:
        for n in range(n_q):

            @pl.when(lax.rem(j, n_q) == n)
            def _(n=n):
                q_s[...] = dqs[n][...]

        parts.append(q_s[...])
    total = lambda group: group[0][...] if chunks == 1 else low(sum(wide(r[...]) for r in group))
    parts += [total(dks), total(dvs)]
    share = sum(dot(p, w_s[n], 1, 1) for n, p in enumerate(parts))
    share_ref[...] = low(share)
    for n, p in enumerate(parts):
        t_s[n] += dot(p, a, 0, 0)
        sums[n : n + 1, :] += jnp.sum(wide(p), axis=0, keepdims=True)

    @pl.when(j == pl.num_programs(0) - 1)
    def _():
        for n in range(kinds):
            grads[n][...] = t_s[n].T


def shares(scalars, start, dqs, dks, dvs, norms, wa, wb):
    rows, width = norms[0].shape
    local = dks[0].shape[1]
    tiles, blocks, chunks = rows // TILE, len(norms), len(dks)
    kinds = 3 if dqs else 2
    ins = [row_block(v, lambda i, sc: i // len(dqs)) for v in dqs]
    ins += [row_block(v, lambda i, sc: i + start) for v in dks + dvs]
    ins += [row_block(v, lambda i, sc, b=b: jnp.clip(i - b * tiles, 0, tiles - 1)) for b, v in enumerate(norms)]
    ins += [whole(wa), whole(wb)]
    fixed = lambda dims: pl.BlockSpec(dims, lambda i, sc: (0,) * len(dims))
    outs = [(shape((blocks * rows, width), BF), pl.BlockSpec((TILE, width), lambda i, sc: (i, 0)))]
    outs += [(shape((width, local), F32), fixed((width, local)))] * kinds + [(shape((8, local), F32), fixed((8, local)))]
    scratch = [
        pltpu.VMEM((kinds, width, local), BF),
        pltpu.VMEM((TILE, width), BF),
        pltpu.VMEM((kinds, local, width), F32),
        pltpu.VMEM((TILE, local), BF),
    ]
    return call(
        functools.partial(share_kernel, blocks, len(dqs), tiles, chunks), "share" if dqs else "share_seen", scalars, (blocks * tiles,), ins, outs, scratch,
        dqs + dks + dvs + norms + [wa, wb], 4 * blocks * rows * width * local * kinds, 8_000_000,
    )


def place_kernel(pieces, which, sc_ref, *refs):
    out_ref, x_s = refs[pieces], refs[pieces + 1]
    j = pl.program_id(0)
    f = sc_ref[5]
    part = out_ref.shape[1] // 2
    for n in range(pieces):

        @pl.when(j == n)
        def _(n=n):
            x_s[...] = refs[n][...].astype(x_s.dtype)

    out_ref[:, pl.ds(pl.multiple_of(f * part, 128), part)] = x_s[:, :part]
    out_ref[:, pl.ds(pl.multiple_of((1 - f) * part, 128), part)] = x_s[:, part:]


def placed(scalars, which, pieces, kind):
    width = pieces[0][0].shape[1]
    ins = [pl.BlockSpec((TILE, width), lambda i, sc, n=n: (n, 0)) for _, n in pieces]
    rows = TILE * len(pieces)
    return call(
        functools.partial(place_kernel, len(pieces), which), "placed", scalars, (len(pieces),), ins,
        [(shape((rows, width), kind), pl.BlockSpec((TILE, width), lambda i, sc: (i ^ sc[which], 0)))],
        [pltpu.VMEM((TILE, width), kind)], [v for v, _ in pieces], 0, 6_000_000,
    )[0]


def pack_kernel(n, *refs):
    out_ref, row_s = refs[-2], refs[-1]
    row_s[...] = jnp.zeros_like(row_s)
    for k in range(n):
        row_s[k : k + 1, :] = wide(refs[k][...])
    top = n
    for ref in refs[n:-2]:
        row_s[top : top + ref.shape[0], : ref.shape[1]] = wide(ref[...])
        top += ref.shape[0]
    out_ref[...] = low(row_s[...])


def packed(vectors, folds):
    part = vectors[0].shape[0]
    args = [v.reshape(1, part) for v in vectors] + [v.reshape(-1, v.shape[-1]) for v in folds]
    rows = len(vectors) + sum(v.shape[0] for v in args[len(vectors) :])
    rows += -rows % 16
    return pl.pallas_call(
        functools.partial(pack_kernel, len(vectors)), name="packed", out_shape=shape((rows, part), BF),
        scratch_shapes=[pltpu.VMEM((rows, part), F32)],
        compiler_params=pltpu.CompilerParams(vmem_limit_bytes=8 << 20),
        cost_estimate=pl.CostEstimate(flops=0, bytes_accessed=100_000, transcendentals=0),
    )(*args)


def unpack_kernel(sizes, sc_ref, a_ref, b_ref, vec_ref, qkv_ref, up_ref):
    f = sc_ref[5]
    a, b = wide(a_ref[...]), wide(b_ref[...])
    lo, hi = jnp.where(f == 0, a, b), jnp.where(f == 0, b, a)
    part = a.shape[1]
    n = 6
    vec_ref[0:2, :part], vec_ref[0:2, part:] = lo[0:2], hi[0:2]
    vec_ref[2:8, :part], vec_ref[2:8, part:] = a[0:6], b[0:6]
    lanes = HD // 2
    for ref, start, count in ((qkv_ref, n, sizes[0]), (up_ref, n + sizes[0], sizes[1])):
        ref[...] = jnp.concatenate([p[start + k : start + k + 1, :lanes] for k in range(count) for p in (lo, hi)], axis=1)


def unpacked(scalars, a, b, sizes):
    outs = [shape((8, 2 * a.shape[1]), F32), shape((1, sizes[0] * HD), F32), shape((1, sizes[1] * HD), F32)]
    fixed = [(o, pl.BlockSpec(o.shape, lambda i, sc: (0, 0))) for o in outs]
    return call(functools.partial(unpack_kernel, sizes), "unpacked", scalars, (1,), [whole(a), whole(b)], fixed, [], [a, b], 0, 100_000, 8)


def weights_kernel(pieces, order, sc_ref, *refs):
    refs = list(refs)
    a_refs = [refs.pop(0) for _ in range(pieces)]
    dy_ref = refs.pop(0)
    pre_refs, act_refs = [refs.pop(0) for _ in range(2)], [refs.pop(0) for _ in range(2)]
    own_ref, other_ref, sum_ref, a_s, d_s, p_s, c_s, g_s = refs
    j = pl.program_id(0)

    @pl.when(j == 0)
    def _():
        for n in range(pieces):
            to = slice(n * TILE, (n + 1) * TILE)
            a_s[to, :] = a_refs[n][...]
            d_s[to, :] = dy_ref[order[n] * TILE : (order[n] + 1) * TILE, :]
        for n in range(2):
            to = slice(n * 2 * TILE, (n + 1) * 2 * TILE)
            p_s[to, :] = pre_refs[n][...]
            c_s[to, :] = act_refs[n][...]
        sum_ref[...] = jnp.zeros_like(sum_ref)
        sum_ref[0:1, :] = jnp.sum(wide(p_s[...]), axis=0, keepdims=True)
        sum_ref[1:2, :] = jnp.sum(wide(d_s[...]), axis=0, keepdims=True)

    part, units = own_ref.shape[0], p_s.shape[1]
    cols = pl.ds(pl.multiple_of((1 - j) * part, 128), part)
    g_s[:, :units] = dot(a_s[:, cols], p_s[...], 0, 0)
    g_s[:, units:] = dot(d_s[:, cols], c_s[...], 0, 0)

    @pl.when(j == 0)
    def _():
        other_ref[...] = low(g_s[...])

    @pl.when(j == 1)
    def _():
        own_ref[...] = g_s[...]


def mlp_weights(scalars, twos, dy, order, pres, acts):
    rows, width = dy.shape
    units = pres[0].shape[1]
    part = width // 2
    outs = [shape((part, 2 * units), F32), shape((part, 2 * units), BF), shape((8, max(width, units)), F32)]
    fixed = [(o, pl.BlockSpec(o.shape, lambda i, sc: (0, 0))) for o in outs]
    args = twos + [dy] + pres + acts
    scratch = [pltpu.VMEM((rows, n), BF) for n in (width, width, units, units)] + [pltpu.VMEM((part, 2 * units), F32)]
    return call(
        functools.partial(weights_kernel, len(twos), order), "mlp_weights", scalars, (2,), [whole(v) for v in args], fixed, scratch, args,
        4 * rows * width * units, 12_000_000, 40,
    )


PAIR = [(0, 1), (1, 0)]


def swap_core(values):
    return lax.ppermute(values, "tp", [(i, i ^ 1) for i in range(4)])


def swap_y(values):
    return lax.ppermute(values, "tp", [(i, i ^ 2) for i in range(4)])


def hop(values, pairs):
    return lax.ppermute(values, "ctx", pairs)


def after(values, *deps):
    return lax.optimization_barrier((values, *deps))[0]


def pick(parts, index):
    return lax.dynamic_index_in_dim(parts, index, 0, keepdims=False)


def ordered(first, second, flip):
    return jnp.where(flip == 0, jnp.stack([first, second]), jnp.stack([second, first]))


def sum_ctx(values, z):
    near, far = z & 1, z >> 1
    near_pairs, far_pairs = [(i, i ^ 1) for i in range(4)], [(i, i ^ 2) for i in range(4)]
    rows, cols = values.shape
    halves = values.reshape(2, rows // 2, cols)
    half = pick(halves, near) + wide(hop(low(pick(halves, 1 - near)), near_pairs))
    quarters = half.reshape(2, rows // 4, cols)
    quarter = low(pick(quarters, far) + wide(hop(low(pick(quarters, 1 - far)), far_pairs)))
    half = ordered(quarter, hop(quarter, far_pairs), far).reshape(rows // 2, cols)
    return wide(ordered(half, hop(half, near_pairs), near).reshape(rows, cols))


def body(
    hidden,
    prefix,
    w_qkv,
    b_qkv,
    w_out,
    b_out,
    w_up,
    b_up,
    w_down,
    b_down,
    ln1_gain,
    ln1_shift,
    ln2_gain,
    ln2_shift,
    cotangent,
):
    members = lax.axis_size("fsdp")
    paired = members == 2
    z = lax.axis_index("ctx")
    t = lax.axis_index("tp")
    half_ctx = lax.axis_size("ctx") // 2
    core, side = t & 1, t >> 1
    turn_q, turn_k = 2 * core, 2 * core + side
    f = lax.axis_index("fsdp") if paired else jnp.int32(0)
    rows, width = hidden.shape[1], hidden.shape[2]
    local, units = w_qkv.shape[2], w_up.shape[1]
    half, quarter, part = rows // 2, rows // 4, width // 2
    tiles = rows // TILE
    scalars = jnp.stack([z, turn_q, turn_k, prefix[0], jnp.int32(half_ctx), f]).astype(jnp.int32)

    def both(values, axis):
        if paired:
            return values, lax.ppermute(values, "fsdp", PAIR)
        return tuple(jnp.split(lax.all_gather(values, "fsdp", axis=axis, tiled=True), 2, axis=axis))

    qkv_a, qkv_b = both(w_qkv.reshape(w_qkv.shape[0], 3 * local), 0)
    own_quarter = lax.dynamic_slice(hidden[0], (turn_k * quarter, 0), (quarter, width))
    near_quarter = hop(own_quarter, [(i + half_ctx, i) for i in range(half_ctx)])
    far_from = after(own_quarter, near_quarter)
    near_quarter = jnp.where(z >= half_ctx, own_quarter, near_quarter)
    far_quarter = hop(far_from, [(2, 1)]) + hop(far_from, [(2, 3)])

    def spread(values):
        other = swap_y(values)
        pair = swap_core(jnp.concatenate([values, other], axis=0))
        return [(values, 0), (other, 0), (pair, 0), (pair, 1)]

    vectors_in = (ln1_gain, ln1_shift, b_out, ln2_gain, ln2_shift, b_down)
    fold_rows = (b_qkv.size // b_qkv.shape[-1], b_up.shape[0])
    if paired:
        small = packed(vectors_in, (b_qkv, b_up))
        vec, bias_qkv, bias_up = unpacked(scalars, small, lax.ppermute(small, "fsdp", PAIR), fold_rows)
    else:
        gather = lambda v: wide(lax.all_gather(v, "fsdp", axis=v.ndim - 1, tiled=True))
        found = [gather(v) for v in vectors_in]
        vec = jnp.stack(found[:2] + found)
        bias_qkv, bias_up = gather(b_qkv).reshape(1, -1), gather(b_up).reshape(1, -1)
    gain_one, shift_one, gain_two, shift_two, bias_down = vec[2], vec[3], vec[5], vec[6], vec[7]
    later = after((w_out, w_up, w_down), qkv_b)
    out_a, out_b = both(later[0], 1)
    up_a, up_b = both(later[1], 0)
    down_a, down_b = both(later[2], 1)

    lane = jnp.arange(local, dtype=jnp.int32) % (HD // 2)
    frequency = jnp.power(jnp.float32(10000.0), -2.0 * wide(lane) / HD)[None, :]
    base = wide(jnp.arange(TILE, dtype=jnp.int32))[:, None] * frequency
    turns = wide(jnp.arange(half_ctx * tiles, dtype=jnp.int32) * TILE)[:, None] * frequency
    base, turns = jnp.stack([jnp.cos(base), jnp.sin(base)]), jnp.stack([jnp.cos(turns), jnp.sin(turns)])

    q, k_own, v_own, norm_own, x_turned, dy = project(
        scalars, [hidden[0]], cotangent[0], False, rows, vec, qkv_a, qkv_b, bias_qkv, base, turns
    )
    k_near, v_near, norm_near = project(scalars, spread(near_quarter), None, False, rows, vec, qkv_a, qkv_b, bias_qkv, base, turns)
    k_far, v_far, norm_far = project(scalars, spread(far_quarter), None, True, rows, vec, qkv_a, qkv_b, bias_qkv, base, turns)
    keys, values = [k_own, k_near, k_far], [v_own, v_near, v_far]

    def core_sum(share):
        return low(wide(share[:TILE]) + wide(swap_core(share[TILE:])))

    o0, lse0, share = attention(scalars, 0, 2, q, keys, values, out_a, out_b)
    mine0 = core_sum(share)
    o1, lse1, share = attention(scalars, 1, 2, after(q, mine0), keys, values, out_a, out_b)
    mine1 = core_sum(share)
    mid0, two0 = norm_two(scalars, 0, x_turned, mine0, swap_y(mine0), vec)
    twos0 = (two0, swap_core(two0))
    share, act0, pre0 = mlp(scalars, 0, 2, after(twos0[0], mine1), twos0[1], dy, up_a, up_b, down_a, down_b, bias_up)
    back0 = core_sum(share)
    mid1, two1 = norm_two(scalars, 1, x_turned, mine1, after(swap_y(mine1), back0), vec)
    twos1 = (two1, swap_core(two1))
    share, act1, pre1 = mlp(scalars, 1, 2, *twos1, dy, up_a, up_b, down_a, down_b, bias_up)
    back1 = core_sum(share)
    back_y0, back_y1 = swap_y(back0), swap_y(back1)

    act0, act1, pre0, pre1 = after((act0, act1, pre0, pre1), back1)
    g_own, g_other, sums_mlp = mlp_weights(scalars, list(twos0) + list(twos1), dy, (0, 2, 1, 3), [pre0, pre1], [act0, act1])
    full_down = jnp.concatenate([down_a, down_b], axis=1)
    down0 = core_sum(low(dot(act0, full_down)))
    down1 = core_sum(low(dot(act1, full_down)))
    down_y0, down_y1 = swap_y(after(down0, back_y0, back_y1)), swap_y(after(down1, back_y0, back_y1))

    def partner_sum(own_part, other_part):
        if paired:
            return own_part + wide(lax.ppermute(other_part, "fsdp", PAIR))
        return lax.psum_scatter(jnp.concatenate([own_part, wide(other_part)], axis=0), "fsdp", scatter_dimension=0, tiled=True)

    if not paired:
        g_own, g_other = g_own, g_other
    group = partner_sum(g_own, g_other)
    near_bit, far_bit = z & 1, z >> 1
    near_pairs, far_pairs = [(i, i ^ 1) for i in range(4)], [(i, i ^ 2) for i in range(4)]

    def split(values, bit):
        grid = values.reshape(2, values.shape[0] // 2, values.shape[1])
        return pick(grid, bit), low(pick(grid, 1 - bit))

    dmid0, dz0 = norm_two_grad(scalars, 0, dy, mid0, back0, back_y0, vec)
    dzs0 = (dz0, swap_core(dz0))
    dmid1, dz1 = norm_two_grad(scalars, 1, dy, mid1, back1, back_y1, vec)
    dzs1 = (dz1, swap_core(dz1))
    dq0, dk0, dv0 = attention_grads(scalars, 0, 2, q, o0, *dzs0, lse0, keys, values, out_a, out_b, base, turns)
    g_keep, g_send = split(group, near_bit)
    dq1, dk1, dv1 = attention_grads(scalars, 1, 2, after(q, dk0, g_send), o1, *dzs1, lse1, keys, values, out_a, out_b, base, turns)
    g_half = g_keep + wide(hop(g_send, near_pairs))
    g_keep, g_send = split(g_half, far_bit)
    g_quarter = low(g_keep + wide(hop(g_send, far_pairs)))
    g_half = ordered(g_quarter, hop(g_quarter, far_pairs), far_bit).reshape(g_half.shape)
    first_group = wide(ordered(g_half, hop(g_half, near_pairs), near_bit).reshape(group.shape))

    result0 = low(mid0 + (wide(down0) + wide(down_y0)) + bias_down)
    result1 = low(mid1 + (wide(down1) + wide(down_y1)) + bias_down)
    other = swap_core(jnp.concatenate([result0, result1], axis=0))
    result = placed(scalars, 1, [(result0, 0), (result1, 0), (other, 0), (other, 1)], BF)

    dks, dvs = [dk0, dk1], [dv0, dv1]
    share_seen, gk_seen, gv_seen, sums_seen = shares(scalars, tiles, [], dks, dvs, [norm_near, norm_far], qkv_a, qkv_b)
    share_own, gq, gk, gv, sums = shares(scalars, 0, after([dq0, dq1], share_seen), dks, dvs, [norm_own], qkv_a, qkv_b)

    def core_half(share):
        return low(wide(share[:half]) + wide(swap_core(share[half:])))

    near_mine = core_half(share_seen[:rows])
    far_mine = core_half(share_seen[rows:])
    near_q = low(wide(near_mine[:quarter]) + wide(swap_y(near_mine[quarter:])))
    near_in = hop(near_q, [(0, 1), (1, 3)])
    far_q = wide(far_mine[:quarter]) + wide(swap_y(far_mine[quarter:]))
    far_q = low(far_q + jnp.where(z == 1, wide(near_in), 0.0))
    far_in = wide(hop(far_q, [(1, 2)])) + wide(hop(far_q, [(3, 2)]))
    own_mine = core_half(share_own).reshape(2, quarter, width)
    da_one = wide(pick(own_mine, side)) + wide(swap_y(pick(own_mine, 1 - side)))
    da_one = da_one + far_in + jnp.where(z >= half_ctx, wide(near_q) + jnp.where(z == 3, wide(near_in), 0.0), 0.0)
    x_q = wide(lax.dynamic_slice(x_turned, (side * quarter, 0), (quarter, width)))
    grad_q = low(jnp.where(side == 0, dmid0, dmid1) + norm_back(da_one, x_q, gain_one))
    grad_y = swap_y(grad_q)
    grad_c = swap_core(jnp.concatenate([grad_q, grad_y], axis=0))
    grad_input = placed(scalars, 2, [(grad_q, 0), (grad_y, 0), (grad_c, 0), (grad_c, 1)], F32)

    dz_all = jnp.concatenate([*dzs0, *dzs1], axis=0)
    g_out = dot(dz_all, jnp.concatenate([o0, o1], axis=0), 0, 0)
    g_qkv = jnp.concatenate([gq, gk + gk_seen, gv + gv_seen], axis=1)
    gb_qkv = jnp.concatenate([sums[0], sums[1] + sums_seen[0], sums[2] + sums_seen[1]])
    g_all = jnp.concatenate([g_out, g_qkv], axis=1)
    second_group = sum_ctx(partner_sum(g_all[:part], low(g_all[part:])), z)

    def gain_grad(weights, grad, bias_grad, gain, shift):
        full = wide(jnp.concatenate(weights, axis=0))
        by_shift = jnp.sum(full * bias_grad[None, :], axis=1)
        return (jnp.sum(full * grad, axis=1) - shift * by_shift) / gain, by_shift

    gb_up, gb_down = sums_mlp[0], sums_mlp[1] * 0.25
    gb_out = (jnp.sum(wide(dz0), axis=0) + jnp.sum(wide(dz1), axis=0)) * 0.5
    g_gain_one, g_shift_one = gain_grad((qkv_a, qkv_b), g_qkv, gb_qkv, gain_one, shift_one)
    g_up = jnp.concatenate([g_own[:, :units], wide(g_other[:, :units])], axis=0)
    g_gain_two, g_shift_two = gain_grad((up_a, up_b), g_up, gb_up, gain_two, shift_two)
    over_tp = after(jnp.stack([gb_out, gb_down, g_gain_one, g_shift_one, g_gain_two, g_shift_two]), near_q)
    over_tp = over_tp + swap_core(over_tp)
    over_tp = over_tp + swap_y(over_tp)
    if paired:
        take = lambda v, n: lax.dynamic_index_in_dim(v.reshape(-1, 2, HD // 2), n, 1, keepdims=False).reshape(-1)
        mine = jnp.concatenate([over_tp[:, :part].reshape(-1), take(gb_qkv, f), take(gb_up, f)])
        other = jnp.concatenate([over_tp[:, part:].reshape(-1), take(gb_qkv, 1 - f), take(gb_up, 1 - f)])
        vectors = mine + lax.ppermute(other, "fsdp", PAIR)
    else:
        scattered = [
            lax.psum_scatter(v, "fsdp", scatter_dimension=1, tiled=True).reshape(-1)
            for v in (over_tp, gb_qkv.reshape(-1, HD), gb_up.reshape(-1, HD))
        ]
        vectors = jnp.concatenate(scattered)
    vectors = vectors + hop(vectors, [(i, i ^ 1) for i in range(4)])
    vectors = vectors + hop(vectors, [(i, i ^ 2) for i in range(4)])
    own = width // members
    named = vectors[: 6 * own].reshape(6, own)
    cut = 6 * own + b_qkv.size
    return (
        result[None],
        grad_input[None],
        second_group[:, local:].reshape(w_qkv.shape),
        vectors[6 * own : cut].reshape(b_qkv.shape),
        second_group[:, :local].T,
        named[0],
        first_group[:, :units],
        vectors[cut:].reshape(b_up.shape),
        first_group[:, units:].T,
        named[1],
        named[2],
        named[3],
        named[4],
        named[5],
    )


def solution(mesh):
    rows = P("fsdp", "ctx", None)
    weights = (P("fsdp", None, "tp"), P(None, "tp", "fsdp"), P("tp", "fsdp"), P("fsdp"), P("fsdp", "tp"), P("tp", "fsdp"), P("tp", "fsdp"))
    vectors = (P("fsdp"),) * 5
    return jax.shard_map(
        body,
        mesh=mesh,
        in_specs=(rows, P("fsdp")) + weights + vectors + (rows,),
        out_specs=(rows, rows) + weights + vectors,
        check_vma=False,
    )
```

```python
import functools
import jax
import jax.numpy as jnp
from jax import lax
from jax.experimental import pallas as pl
from jax.experimental.pallas import tpu as pltpu
from jax.sharding import PartitionSpec as P

HD = 64
BLOCK = 16
TILE = 256
WIDE = 512
LOG2E = 1.4426950408889634
NEG = -1e30
epsilon = 1e-05
BF, F32 = jnp.bfloat16, jnp.float32


def low(values):
    return values.astype(BF)


def wide(values):
    return values.astype(F32)


def dot(a, b, ca=1, cb=0):
    return lax.dot_general(a, b, (((ca,), (cb,)), ((), ())), preferred_element_type=F32)


def shape(dims, kind):
    return jax.ShapeDtypeStruct(dims, kind)


def call(kernel, name, scalars, grid, ins, outs, scratch, args, flops, moved, room=24):
    return pl.pallas_call(
        kernel,
        name=name,
        out_shape=[s for s, _ in outs],
        grid_spec=pltpu.PrefetchScalarGridSpec(
            num_scalar_prefetch=1, grid=grid, in_specs=ins, out_specs=[b for _, b in outs], scratch_shapes=scratch
        ),
        compiler_params=pltpu.CompilerParams(dimension_semantics=("arbitrary",) * len(grid), vmem_limit_bytes=room << 20),
        cost_estimate=pl.CostEstimate(flops=flops, bytes_accessed=moved, transcendentals=0),
    )(scalars, *args)


def whole(values):
    dims = values.shape
    return pl.BlockSpec(dims, lambda i, sc: (0,) * len(dims))


def row_block(values, index):
    return pl.BlockSpec((TILE, values.shape[1]), lambda i, sc: (index(i, sc), 0))


def turn_matrix(width):
    k = lax.broadcasted_iota(jnp.int32, (width, width), 0)
    n = lax.broadcasted_iota(jnp.int32, (width, width), 1)
    first = (n & (HD - 1)) < HD // 2
    return jnp.where(first & (k == n + HD // 2), -1.0, jnp.where((~first) & (k == n - HD // 2), 1.0, 0.0)).astype(BF)


def tile_angles(base_ref, tile_ref, index):
    cos, sin = base_ref[0], base_ref[1]
    cos_t, sin_t = tile_ref[0, pl.ds(index, 1), :], tile_ref[1, pl.ds(index, 1), :]
    return cos * cos_t - sin * sin_t, sin * cos_t + cos * sin_t


def unit_rows(x):
    mean = jnp.mean(x, axis=-1, keepdims=True)
    centered = x - mean
    variance = jnp.mean(centered * centered, axis=-1, keepdims=True)
    scale = lax.rsqrt(variance + epsilon)
    return centered * scale, scale


def project_kernel(parts, with_q, far, tiles, sc_ref, *refs):
    refs = list(refs)
    xs = [refs.pop(0) for _ in range(parts)]
    dy_ref = refs.pop(0) if with_q else None
    vec_ref, wa_ref, wb_ref, bias_ref, base_ref, tile_ref = [refs.pop(0) for _ in range(6)]
    outs = [refs.pop(0) for _ in range(3 if with_q else 2)]
    norm_ref = refs.pop(0)
    if with_q:
        keep_ref, dy_out = refs.pop(0), refs.pop(0)
    w_s, r_s, b_s, x_s, a_s = refs
    j = pl.program_id(0)
    f = sc_ref[5]
    local = outs[0].shape[1]
    part = wa_ref.shape[0]
    skip = 0 if with_q else 1
    count = len(outs)

    @pl.when(j == 0)
    def _():
        turn = turn_matrix(local)
        for n in range(count):
            cols = slice((n + skip) * local, (n + skip + 1) * local)
            w_s[n, :part] = wa_ref[:, cols]
            w_s[n, part:] = wb_ref[:, cols]
            if n < count - 1:
                r_s[n] = low(dot(w_s[n], turn))
                b_s[n] = dot(jnp.broadcast_to(bias_ref[:, cols], (8, local)).astype(BF), turn)

    if parts == 1:
        x = wide(xs[0][...])
    else:
        for n in range(parts):

            @pl.when(j == n)
            def _(n=n):
                x_s[...] = xs[n][...]

        x = wide(x_s[...])
    unit, _ = unit_rows(x)
    a_s[...] = unit * vec_ref[0:1] + vec_ref[1:2]
    first = pl.ds(pl.multiple_of(f * part, 128), part)
    second = pl.ds(pl.multiple_of((1 - f) * part, 128), part)
    a = jnp.concatenate([low(a_s[:, first]), low(a_s[:, second])], axis=1)
    norm_ref[...] = a
    if with_q:
        keep_ref[:, :part] = xs[0][:, first]
        keep_ref[:, part:] = xs[0][:, second]
        dy_out[:, :part] = dy_ref[:, first]
        dy_out[:, part:] = dy_ref[:, second]
    at = j ^ sc_ref[1 if with_q else 2]
    cos, sin = tile_angles(base_ref, tile_ref, at if far else at + lax.rem(sc_ref[0], sc_ref[4]) * tiles)
    for n in range(count):
        cols = slice((n + skip) * local, (n + skip + 1) * local)
        u = dot(a, w_s[n]) + bias_ref[:, cols]
        if n < count - 1:
            u = u * cos + (dot(a, r_s[n]) + b_s[n, 0:1]) * sin
        u = low(u)
        if n == 0 and with_q:
            u = u * jnp.asarray(HD**-0.5, BF)
        outs[n][...] = u


def project(scalars, xs, dy, far, rows, vec, wa, wb, bias, base, turns):
    with_q = dy is not None
    width = wa.shape[0] * 2
    local = wa.shape[1] // 3
    tiles = rows // TILE
    if with_q:
        turned = lambda i, sc: i ^ sc[1]
        ins = [row_block(xs[0], turned), row_block(dy, turned)]
        args = [xs[0], dy]
        parts = 1
    else:
        ins = [pl.BlockSpec((TILE, width), lambda i, sc, n=n: (n, 0)) for _, n in xs]
        args = [v for v, _ in xs]
        parts = len(xs)
    ins += [whole(v) for v in (vec, wa, wb, bias, base, turns)]
    args += [vec, wa, wb, bias, base, turns]
    tile = lambda n: pl.BlockSpec((TILE, n), lambda i, sc: (i, 0))
    count = 3 if with_q else 2
    outs = [(shape((rows, local), BF), tile(local))] * count + [(shape((rows, width), BF), tile(width))] * (3 if with_q else 1)
    scratch = [
        pltpu.VMEM((count, width, local), BF),
        pltpu.VMEM((count - 1, width, local), BF),
        pltpu.VMEM((count - 1, 8, local), F32),
        pltpu.VMEM((TILE, width), BF),
        pltpu.VMEM((TILE, width), F32),
    ]
    return call(
        functools.partial(project_kernel, parts, with_q, far, tiles), "project" if with_q else "project_seen", scalars, (tiles,), ins, outs, scratch, args,
        2 * rows * width * local * 5, 8_000_000,
    )


def stack_heads(rows, heads):
    lane = lax.broadcasted_iota(jnp.int32, rows.shape, 1) // HD
    return jnp.concatenate([jnp.where(lane == h, rows, jnp.zeros_like(rows)) for h in range(heads)], axis=0)


def tile_plan(sc_ref, tile, tiles):
    z, prefix, half = sc_ref[0], sc_ref[3], sc_ref[4]
    noisy = z < half
    late = lax.rem(z, half)
    at = tile ^ sc_ref[1]
    prefix = jnp.where(late == 0, prefix, 0)
    top = jnp.maximum(at + 1, (prefix + TILE - 1) // TILE)
    return noisy, late == 1, at, top, prefix


def near_rows(sc_ref, t):
    return pl.ds(pl.multiple_of((t ^ sc_ref[2]) * TILE, TILE), TILE)


def edge_mask(block_gap, k_pos, t, at, noisy, prefix):
    limit = (at - t) * (TILE // BLOCK) + jnp.where(noisy, 0, 1)
    return (block_gap < limit) | (k_pos < prefix - t * TILE)


def fwd_kernel(first, stride, tiles, sc_ref, q_ref, ko_ref, vo_ref, km_ref, vm_ref, kf_ref, vf_ref, wa_ref, wb_ref, o_ref, lse_ref, keep_ref, send_ref, sbuf, mbuf, lbuf, acc):
    tile = first + stride * pl.program_id(0)
    noisy, late, at, top, prefix = tile_plan(sc_ref, tile, tiles)
    width = q_ref.shape[1]
    heads = width // HD
    qs = stack_heads(q_ref[...], heads)
    mbuf[...] = jnp.full_like(mbuf, NEG)
    lbuf[...] = jnp.zeros_like(lbuf)
    acc[...] = jnp.zeros_like(acc)
    high = heads * TILE
    own = pl.ds(pl.multiple_of(tile * TILE, TILE), TILE)

    def keep(slot, s):
        best = mbuf[...]
        for n in range(s.shape[1] // TILE):
            sbuf[slot + n] = s[:, n * TILE : (n + 1) * TILE]
        for n in range(s.shape[1] // 128):
            best = jnp.maximum(best, s[:, n * 128 : (n + 1) * 128])
        mbuf[...] = best

    def plain_step(t, carry):
        keep(t, dot(qs, km_ref[near_rows(sc_ref, t), :], 1, 1))
        return carry

    lax.fori_loop(0, at, plain_step, 0)
    wides = tiles * TILE // WIDE

    def far_rows(n):
        return pl.ds(pl.multiple_of(n * WIDE, WIDE), WIDE)

    def far_step(n, carry):
        keep(tiles + n * (WIDE // TILE), dot(qs, kf_ref[far_rows(n), :], 1, 1))
        return carry

    lax.fori_loop(0, jnp.where(late, wides, 0), far_step, 0)
    q_block = (lax.broadcasted_iota(jnp.int32, (high, TILE), 0) & (TILE - 1)) >> 4
    k_pos = lax.broadcasted_iota(jnp.int32, (high, TILE), 1)
    gap = (k_pos >> 4) - q_block

    def edge_step(t, carry):
        s = dot(qs, km_ref[near_rows(sc_ref, t), :], 1, 1)
        keep(t, jnp.where(edge_mask(gap, k_pos, t, at, noisy, prefix), s, NEG))
        return carry

    lax.fori_loop(at, top, edge_step, 0)

    @pl.when(noisy)
    def _():
        keep(2 * tiles, jnp.where(gap == 0, dot(qs, ko_ref[own, :], 1, 1), NEG))

    best = jnp.max(mbuf[...], axis=1, keepdims=True) * LOG2E
    mbuf[...] = jnp.broadcast_to(best, mbuf.shape)

    def add(slot, v):
        m = mbuf[...]
        total = lbuf[...]
        cols = []
        for n in range(v.shape[0] // TILE):
            s = sbuf[slot + n]
            for k in range(TILE // 128):
                p = jnp.exp2(s[:, k * 128 : (k + 1) * 128] * LOG2E - m)
                total = total + p
                cols.append(low(p))
        lbuf[...] = total
        acc[...] += dot(jnp.concatenate(cols, axis=1), v)

    def near_sum(t, carry):
        add(t, vm_ref[near_rows(sc_ref, t), :])
        return carry

    lax.fori_loop(0, top, near_sum, 0)

    def far_sum(n, carry):
        add(tiles + n * (WIDE // TILE), vf_ref[far_rows(n), :])
        return carry

    lax.fori_loop(0, jnp.where(late, wides, 0), far_sum, 0)

    @pl.when(noisy)
    def _():
        add(2 * tiles, vo_ref[own, :])

    norm = jnp.sum(lbuf[...], axis=1, keepdims=True)
    out = acc[...] * (1.0 / norm)
    lane = lax.broadcasted_iota(jnp.int32, (TILE, width), 1) // HD
    picked = out[:TILE]
    for h in range(1, heads):
        picked = jnp.where(lane == h, out[h * TILE : (h + 1) * TILE], picked)
    picked = low(picked)
    o_ref[...] = picked
    lse = jnp.broadcast_to(best + jnp.log2(norm), (high, 128))
    lse_ref[0] = jnp.concatenate(
        [lse[h * TILE : (h + 1) * TILE].T[:1] for h in range(heads)] + [jnp.zeros((8 - heads, TILE), F32)], axis=0
    )
    part = wa_ref.shape[1]
    for n, ref in enumerate((keep_ref, send_ref)):

        @pl.when(pl.program_id(0) == n)
        def _(ref=ref):
            ref[:, :part] = low(dot(picked, wa_ref[...]))
            ref[:, part:] = low(dot(picked, wb_ref[...]))


def attention(scalars, first, stride, q, keys, values, wa, wb):
    rows, width = q.shape
    tiles, heads = rows // TILE, width // HD
    count = tiles // stride
    flat = [v for pair in zip(keys, values) for v in pair]
    tile = lambda n: pl.BlockSpec((TILE, n), lambda i, sc: (i, 0))
    full = 2 * wa.shape[1]
    return call(
        functools.partial(fwd_kernel, first, stride, tiles), "attn_fwd", scalars, (count,),
        [row_block(q, lambda i, sc: first + stride * i)] + [whole(v) for v in flat + [wa, wb]],
        [
            (shape((count * TILE, width), BF), tile(width)),
            (shape((count, 8, TILE), F32), pl.BlockSpec((1, 8, TILE), lambda i, sc: (i, 0, 0))),
        ]
        + [(shape((TILE, full), BF), pl.BlockSpec((TILE, full), lambda i, sc: (0, 0)))] * 2,
        [
            pltpu.VMEM((2 * tiles + 1, heads * TILE, TILE), F32),
            pltpu.VMEM((heads * TILE, 128), F32),
            pltpu.VMEM((heads * TILE, 128), F32),
            pltpu.VMEM((heads * TILE, width), F32),
        ],
        [q] + flat + [wa, wb], 3_000_000_000 * count, 4_000_000,
    )


def turn_back(grad, cos, sin, turn):
    moved = grad * sin
    high = low(moved)
    rest = low(moved - wide(high))
    return low(grad * cos - (dot(high, turn) + dot(rest, turn)))


def bwd_kernel(first, stride, tiles, sc_ref, q_ref, o_ref, za_ref, zb_ref, lse_ref, ko_ref, vo_ref, km_ref, vm_ref, kf_ref, vf_ref, wa_ref, wb_ref, base_ref, tile_ref,
               dq_ref, dk_ref, dv_ref, dqt, st, gt, lse_s, del_s, qs_s, gs_s, z_s, dk_s, dv_s):
    g_id = pl.program_id(0)
    tile = first + stride * g_id
    noisy, late, at, top, prefix = tile_plan(sc_ref, tile, tiles)
    width = q_ref.shape[1]
    heads = width // HD
    high = heads * TILE
    part = wa_ref.shape[1]
    rows = tiles * TILE
    per = za_ref.shape[0] // TILE

    @pl.when(g_id == 0)
    def _():
        dk_s[...] = jnp.zeros_like(dk_s)
        dv_s[...] = jnp.zeros_like(dv_s)

    for n in range(2 * per):

        @pl.when(g_id == n)
        def _(n=n):
            z_s[...] = (za_ref if n < per else zb_ref)[(n % per) * TILE : (n % per + 1) * TILE, :]

    z = z_s[...]
    g32 = dot(z[:, :part], wa_ref[...], 1, 1) + dot(z[:, part:], wb_ref[...], 1, 1)
    g = low(g32)
    g32 = wide(g)
    q = q_ref[...]
    qs_s[...] = stack_heads(q, heads)
    gs_s[...] = stack_heads(g, heads)
    q_t = wide(q).T
    g_t = g32.T
    prod = (wide(o_ref[...]) * g32).T
    head_of = lax.broadcasted_iota(jnp.int32, (width, TILE), 0) // HD
    for h in range(heads):
        cols = slice(h * TILE, (h + 1) * TILE)
        st[:, cols] = low(jnp.where(head_of == h, q_t, 0.0))
        gt[:, cols] = low(jnp.where(head_of == h, g_t, 0.0))
        del_s[:, cols] = jnp.sum(prod[h * HD : (h + 1) * HD], axis=0, keepdims=True)
        lse_s[:, cols] = lse_ref[0, h : h + 1, :]
    dqt[...] = jnp.zeros_like(dqt)

    def step(k, v, base, mask):
        n = k.shape[0]
        to = pl.ds(base, n)
        s = dot(k, st[...])
        p = jnp.exp2(s * LOG2E - lse_s[...])
        if mask is not None:
            p = jnp.where(mask, p, 0.0)
        dp = dot(v, gt[...])
        ds = low(p * (dp - del_s[...]))
        p = low(p)
        dv_s[to, :] += dot(p, gs_s[...])
        dk_s[to, :] += dot(ds, qs_s[...])
        dqt[...] += dot(k, ds, 0, 0)

    def near_at(t):
        return pl.multiple_of(rows + (t ^ sc_ref[2]) * TILE, TILE)

    def plain_step(t, carry):
        at_t = near_rows(sc_ref, t)
        step(km_ref[at_t, :], vm_ref[at_t, :], near_at(t), None)
        return carry

    lax.fori_loop(0, at, plain_step, 0)
    wides = rows // WIDE

    def far_step(n, carry):
        at_n = pl.ds(pl.multiple_of(n * WIDE, WIDE), WIDE)
        step(kf_ref[at_n, :], vf_ref[at_n, :], pl.multiple_of(2 * rows + n * WIDE, WIDE), None)
        return carry

    lax.fori_loop(0, jnp.where(late, wides, 0), far_step, 0)
    k_pos = lax.broadcasted_iota(jnp.int32, (TILE, high), 0)
    gap = (k_pos >> 4) - ((lax.broadcasted_iota(jnp.int32, (TILE, high), 1) & (TILE - 1)) >> 4)

    def edge_step(t, carry):
        at_t = near_rows(sc_ref, t)
        step(km_ref[at_t, :], vm_ref[at_t, :], near_at(t), edge_mask(gap, k_pos, t, at, noisy, prefix))
        return carry

    lax.fori_loop(at, top, edge_step, 0)

    @pl.when(noisy)
    def _():
        own = pl.ds(pl.multiple_of(tile * TILE, TILE), TILE)
        step(ko_ref[own, :], vo_ref[own, :], pl.multiple_of(tile * TILE, TILE), gap == 0)

    turn = turn_matrix(width)
    dq_t = jnp.where(head_of == 0, dqt[:, :TILE], 0.0)
    for h in range(1, heads):
        dq_t = jnp.where(head_of == h, dqt[:, h * TILE : (h + 1) * TILE], dq_t)
    late_at = late.astype(jnp.int32) * tiles
    dq_ref[...] = turn_back(dq_t.T * (HD**-0.5), *tile_angles(base_ref, tile_ref, at + late_at), turn)

    @pl.when(g_id == pl.num_programs(0) - 1)
    def _():
        dv_ref[...] = low(dv_s[...])

        def finish(base, true_tile):
            to = pl.ds(pl.multiple_of(base, TILE), TILE)
            dk_ref[to, :] = turn_back(dk_s[to, :], *tile_angles(base_ref, tile_ref, true_tile), turn)

        def all_three(j, carry):
            finish(j * TILE, (j ^ sc_ref[1]) + late_at)
            finish(rows + j * TILE, (j ^ sc_ref[2]) + late_at)
            finish(2 * rows + j * TILE, j ^ sc_ref[2])
            return carry

        lax.fori_loop(0, tiles, all_three, 0)


def attention_grads(scalars, first, stride, q, o, za, zb, lse, keys, values, wa, wb, base, turns):
    rows, width = q.shape
    tiles, heads = rows // TILE, width // HD
    count = tiles // stride
    flat = [v for pair in zip(keys, values) for v in pair]
    tile = pl.BlockSpec((TILE, width), lambda i, sc: (i, 0))
    total = pl.BlockSpec((3 * rows, width), lambda i, sc: (0, 0))
    high = heads * TILE
    return call(
        functools.partial(bwd_kernel, first, stride, tiles), "attn_bwd", scalars, (count,),
        [row_block(q, lambda i, sc: first + stride * i), tile, whole(za), whole(zb), pl.BlockSpec((1, 8, TILE), lambda i, sc: (i, 0, 0))]
        + [whole(v) for v in flat + [wa, wb, base, turns]],
        [(shape((count * TILE, width), BF), tile), (shape((3 * rows, width), BF), total), (shape((3 * rows, width), BF), total)],
        [
            pltpu.VMEM((width, high), F32),
            pltpu.VMEM((width, high), BF),
            pltpu.VMEM((width, high), BF),
            pltpu.VMEM((1, high), F32),
            pltpu.VMEM((1, high), F32),
            pltpu.VMEM((high, width), BF),
            pltpu.VMEM((high, width), BF),
            pltpu.VMEM((TILE, za.shape[1]), BF),
            pltpu.VMEM((3 * rows, width), F32),
            pltpu.VMEM((3 * rows, width), F32),
        ],
        [q, o, za, zb, lse] + flat + [wa, wb, base, turns], 8_000_000_000 * count, 10_000_000,
    )


def norm_kernel(sc_ref, x_ref, mine_ref, theirs_ref, vec_ref, mid_ref, a_ref):
    mid = wide(x_ref[...]) + (wide(mine_ref[...]) + wide(theirs_ref[...])) + vec_ref[4:5]
    mid_ref[...] = mid
    unit, _ = unit_rows(mid)
    a_ref[...] = low(unit * vec_ref[5:6] + vec_ref[6:7])


def norm_two(scalars, index, x, mine, theirs, vec):
    rows, width = mine.shape
    block = pl.BlockSpec((rows, width), lambda i, sc: (0, 0))
    return call(
        norm_kernel, "norm_two", scalars, (1,),
        [row_block(x, lambda i, sc: index), block, block, whole(vec)],
        [(shape((rows, width), F32), block), (shape((rows, width), BF), block)], [], [x, mine, theirs, vec], 10 * rows * width, 3_000_000,
    )


def norm_back(grad, x, gain):
    unit, scale = unit_rows(x)
    weighted = grad * gain
    return scale * (weighted - jnp.mean(weighted, axis=-1, keepdims=True) - unit * jnp.mean(weighted * unit, axis=-1, keepdims=True))


def norm_grad_kernel(sc_ref, dy_ref, mid_ref, mine_ref, theirs_ref, vec_ref, dmid_ref, dz_ref):
    dmid = wide(dy_ref[...]) + norm_back(wide(mine_ref[...]) + wide(theirs_ref[...]), mid_ref[...], vec_ref[5:6])
    dmid_ref[...] = dmid
    dz_ref[...] = low(dmid)


def norm_two_grad(scalars, index, dy, mid, mine, theirs, vec):
    rows, width = mid.shape
    block = pl.BlockSpec((rows, width), lambda i, sc: (0, 0))
    return call(
        norm_grad_kernel, "norm_two_grad", scalars, (1,),
        [row_block(dy, lambda i, sc: index), block, block, block, whole(vec)],
        [(shape((rows, width), F32), block), (shape((rows, width), BF), block)], [], [dy, mid, mine, theirs, vec], 20 * rows * width, 3_000_000,
    )


def mlp_kernel(last, sc_ref, a_ref, b_ref, dy_ref, ua_ref, ub_ref, da_ref, db_ref, bias_ref, *refs):
    refs = list(refs)
    done = [refs.pop(0) for _ in range(2 if last else 0)]
    keep_ref, send_ref, act_ref, pre_ref, down_keep, down_send, x_s = refs
    g = pl.program_id(0)
    part = ua_ref.shape[0]

    @pl.when(g == 0)
    def _():
        x_s[...] = a_ref[...]

    @pl.when(g == 1)
    def _():
        x_s[...] = b_ref[...]

    x, dy = x_s[...], dy_ref[...]
    pre = dot(x[:, :part], ua_ref[...]) + dot(x[:, part:], ub_ref[...]) + bias_ref[...]
    cdf = 0.5 + 0.5 * lax.erf(pre * (2.0**-0.5))
    act = low(pre * cdf)
    act_ref[...] = act
    slope = cdf + pre * (jnp.exp2(pre * pre * (-0.5 * LOG2E)) * 0.3989422804014327)
    grad = dot(dy[:, :part], da_ref[...], 1, 1) + dot(dy[:, part:], db_ref[...], 1, 1)
    dpre = low(grad * slope)
    pre_ref[...] = dpre
    to = slice(TILE, 2 * TILE) if last else slice(0, TILE)
    for n, (ref, down) in enumerate(((keep_ref, down_keep), (send_ref, down_send))):

        @pl.when(g == n)
        def _(n=n, ref=ref, down=down):
            ref[:, :part] = low(dot(dpre, ua_ref[...], 1, 1))
            ref[:, part:] = low(dot(dpre, ub_ref[...], 1, 1))
            if last:
                down[:TILE] = done[n][...]
            down[to, :part] = low(dot(act, da_ref[...]))
            down[to, part:] = low(dot(act, db_ref[...]))


def mlp(scalars, first, stride, own, other, dy, ua, ub, da, db, bias, done):
    width, units = own.shape[1], ua.shape[1]
    tile = lambda n: pl.BlockSpec((TILE, n), lambda i, sc: (i, 0))
    fixed = lambda n: (shape((n, width), BF), pl.BlockSpec((n, width), lambda i, sc: (0, 0)))
    size = 2 * TILE if done else TILE
    weights = [ua, ub, da, db, bias, *done]
    return call(
        functools.partial(mlp_kernel, len(done) > 0), "mlp", scalars, (2,),
        [whole(own), whole(other), row_block(dy, lambda i, sc: first + stride * i)] + [whole(v) for v in weights],
        [fixed(TILE)] * 2 + [(shape((2 * TILE, units), BF), tile(units))] * 2 + [fixed(size)] * 2,
        [pltpu.VMEM((TILE, width), BF)], [own, other, dy, *weights], 8 * 2 * TILE * width * units, 8_000_000,
    )


def share_kernel(blocks, final, tiles, sc_ref, *refs):
    refs = list(refs)
    take = lambda n: [refs.pop(0) for _ in range(n)]
    dqs, outs, dzs, before = (take(2), take(2), take(4), take(2)) if final else ([], [], [], [])
    dks, dvs, norms = take(2), take(2), take(blocks)
    wa_ref, wb_ref = take(2)
    shares_out = take(2 * blocks)
    own_ref, other_ref, sums, rows_ref = take(4) if final else take(2) + [None, None]
    w_s, a_s = take(2)
    t_s, q_s, o_s, z_s = take(4) if final else [own_ref, None, None, None]
    sums = sums if final else other_ref
    j = pl.program_id(0)
    local = dks[0].shape[1]
    part = wa_ref.shape[0]
    kinds = 3 if final else 2
    skip = 3 - kinds
    lead = 2 if final else 0

    @pl.when(j == 0)
    def _():
        if final:
            t_s[: lead * local] = jnp.zeros_like(t_s[: lead * local])
            t_s[lead * local :] = before[0][...]
            sums[...] = before[1][...]
            rows_ref[...] = jnp.zeros_like(rows_ref)
        else:
            t_s[...] = jnp.zeros_like(t_s)
            sums[...] = jnp.zeros_like(sums)
        for n in range(kinds):
            cols = slice((n + skip) * local, (n + skip + 1) * local)
            w_s[n, :part] = wa_ref[:, cols]
            w_s[n, part:] = wb_ref[:, cols]

    for b in range(blocks):

        @pl.when((j >= b * tiles) & (j < (b + 1) * tiles))
        def _(b=b):
            a_s[...] = norms[b][...]

    a = a_s[...]
    parts = []
    if final:
        for n in range(4):

            @pl.when(j == n)
            def _(n=n):
                q_s[...] = dqs[n % 2][...]
                o_s[...] = outs[n % 2][...]
                z_s[...] = dzs[(n % 2) * 2 + n // 2][...]

        parts.append(q_s[...])
        z = z_s[...]
        t_s[:local] += dot(o_s[...], z, 0, 0)
        rows_ref[0:1, :] += jnp.sum(wide(z), axis=0, keepdims=True)
    total = lambda group: low(sum(wide(r[...]) for r in group))
    parts += [total(dks), total(dvs)]
    share = low(sum(dot(p, w_s[n], 1, 1) for n, p in enumerate(parts)))
    half = tiles // 2
    for n, ref in enumerate(shares_out):

        @pl.when((j >= n * half) & (j < (n + 1) * half))
        def _(ref=ref):
            ref[...] = share

    for n, p in enumerate(parts):
        at = (n + (1 if final else 0)) * local
        t_s[at : at + local] += dot(p, a, 0, 0)
        sums[n + skip : n + skip + 1, :] += jnp.sum(wide(p), axis=0, keepdims=True)

    if final:

        @pl.when(j == pl.num_programs(0) - 1)
        def _():
            own_ref[...] = t_s[:, :part].T
            other_ref[...] = low(t_s[:, part:].T)


def shares(scalars, start, dqs, outs, dzs, before, dks, dvs, norms, wa, wb):
    rows, width = norms[0].shape
    local = dks[0].shape[1]
    part = wa.shape[0]
    tiles, blocks, final = rows // TILE, len(norms), len(dqs) > 0
    kinds = 3 if final else 2
    fixed = lambda dims: pl.BlockSpec(dims, lambda i, sc: (0,) * len(dims))
    ins = [row_block(v, lambda i, sc: i // 2) for v in dqs + outs] + [whole(v) for v in dzs + before]
    ins += [row_block(v, lambda i, sc: i + start) for v in dks + dvs]
    ins += [row_block(v, lambda i, sc, b=b: jnp.clip(i - b * tiles, 0, tiles - 1)) for b, v in enumerate(norms)]
    ins += [whole(wa), whole(wb)]
    half = tiles // 2
    results = [
        (shape((rows // 2, width), BF), pl.BlockSpec((TILE, width), lambda i, sc, n=n: (jnp.clip(i - n * half, 0, half - 1), 0)))
        for n in range(2 * blocks)
    ]
    scratch = [pltpu.VMEM((kinds, width, local), BF), pltpu.VMEM((TILE, width), BF)]
    if final:
        results += [(shape((part, 4 * local), F32), fixed((part, 4 * local))), (shape((part, 4 * local), BF), fixed((part, 4 * local)))]
        results += [(shape((8, local), F32), fixed((8, local))), (shape((8, width), F32), fixed((8, width)))]
        scratch += [pltpu.VMEM((4 * local, width), F32), pltpu.VMEM((TILE, local), BF), pltpu.VMEM((TILE, local), BF), pltpu.VMEM((TILE, width), BF)]
    else:
        results += [(shape((2 * local, width), F32), fixed((2 * local, width))), (shape((8, local), F32), fixed((8, local)))]
    return call(
        functools.partial(share_kernel, blocks, final, tiles), "share" if final else "share_seen", scalars, (blocks * tiles,), ins, results, scratch,
        dqs + outs + dzs + before + dks + dvs + norms + [wa, wb], 4 * blocks * rows * width * local * kinds, 8_000_000, 32,
    )


def place_kernel(pieces, which, sc_ref, *refs):
    out_ref, x_s = refs[pieces], refs[pieces + 1]
    j = pl.program_id(0)
    f = sc_ref[5]
    part = out_ref.shape[1] // 2
    for n in range(pieces):

        @pl.when(j == n)
        def _(n=n):
            x_s[...] = refs[n][...].astype(x_s.dtype)

    out_ref[:, pl.ds(pl.multiple_of(f * part, 128), part)] = x_s[:, :part]
    out_ref[:, pl.ds(pl.multiple_of((1 - f) * part, 128), part)] = x_s[:, part:]


def placed(scalars, which, pieces, kind):
    width = pieces[0][0].shape[1]
    ins = [pl.BlockSpec((TILE, width), lambda i, sc, n=n: (n, 0)) for _, n in pieces]
    rows = TILE * len(pieces)
    return call(
        functools.partial(place_kernel, len(pieces), which), "placed", scalars, (len(pieces),), ins,
        [(shape((rows, width), kind), pl.BlockSpec((TILE, width), lambda i, sc: (i ^ sc[which], 0)))],
        [pltpu.VMEM((TILE, width), kind)], [v for v, _ in pieces], 0, 6_000_000,
    )[0]


def pack_kernel(n, *refs):
    out_ref, row_s = refs[-2], refs[-1]
    row_s[...] = jnp.zeros_like(row_s)
    for k in range(n):
        row_s[k : k + 1, :] = wide(refs[k][...])
    top = n
    for ref in refs[n:-2]:
        row_s[top : top + ref.shape[0], : ref.shape[1]] = wide(ref[...])
        top += ref.shape[0]
    out_ref[...] = low(row_s[...])


def packed(vectors, folds):
    part = vectors[0].shape[0]
    args = [v.reshape(1, part) for v in vectors] + [v.reshape(-1, v.shape[-1]) for v in folds]
    rows = len(vectors) + sum(v.shape[0] for v in args[len(vectors) :])
    rows += -rows % 16
    return pl.pallas_call(
        functools.partial(pack_kernel, len(vectors)), name="packed", out_shape=shape((rows, part), BF),
        scratch_shapes=[pltpu.VMEM((rows, part), F32)],
        compiler_params=pltpu.CompilerParams(vmem_limit_bytes=8 << 20),
        cost_estimate=pl.CostEstimate(flops=0, bytes_accessed=100_000, transcendentals=0),
    )(*args)


def unpack_kernel(sizes, sc_ref, a_ref, b_ref, vec_ref, qkv_ref, up_ref):
    f = sc_ref[5]
    a, b = wide(a_ref[...]), wide(b_ref[...])
    lo, hi = jnp.where(f == 0, a, b), jnp.where(f == 0, b, a)
    part = a.shape[1]
    n = 6
    vec_ref[0:2, :part], vec_ref[0:2, part:] = lo[0:2], hi[0:2]
    vec_ref[2:8, :part], vec_ref[2:8, part:] = a[0:6], b[0:6]
    lanes = HD // 2
    for ref, start, count in ((qkv_ref, n, sizes[0]), (up_ref, n + sizes[0], sizes[1])):
        ref[...] = jnp.concatenate([p[start + k : start + k + 1, :lanes] for k in range(count) for p in (lo, hi)], axis=1)


def unpacked(scalars, a, b, sizes):
    outs = [shape((8, 2 * a.shape[1]), F32), shape((1, sizes[0] * HD), F32), shape((1, sizes[1] * HD), F32)]
    fixed = [(o, pl.BlockSpec(o.shape, lambda i, sc: (0, 0))) for o in outs]
    return call(functools.partial(unpack_kernel, sizes), "unpacked", scalars, (1,), [whole(a), whole(b)], fixed, [], [a, b], 0, 100_000, 8)


def weights_kernel(pieces, order, sc_ref, *refs):
    refs = list(refs)
    a_refs = [refs.pop(0) for _ in range(pieces)]
    dy_ref = refs.pop(0)
    pre_refs, act_refs = [refs.pop(0) for _ in range(2)], [refs.pop(0) for _ in range(2)]
    own_ref, other_ref, sum_ref, a_s, d_s, p_s, c_s, g_s = refs
    j = pl.program_id(0)

    @pl.when(j == 0)
    def _():
        for n in range(pieces):
            to = slice(n * TILE, (n + 1) * TILE)
            a_s[to, :] = a_refs[n][...]
            d_s[to, :] = dy_ref[order[n] * TILE : (order[n] + 1) * TILE, :]
        for n in range(2):
            to = slice(n * 2 * TILE, (n + 1) * 2 * TILE)
            p_s[to, :] = pre_refs[n][...]
            c_s[to, :] = act_refs[n][...]
        sum_ref[...] = jnp.zeros_like(sum_ref)
        sum_ref[0:1, :] = jnp.sum(wide(p_s[...]), axis=0, keepdims=True)
        sum_ref[1:2, :] = jnp.sum(wide(d_s[...]), axis=0, keepdims=True)

    part, units = own_ref.shape[0], p_s.shape[1]
    cols = pl.ds(pl.multiple_of((1 - j) * part, 128), part)
    g_s[:, :units] = dot(a_s[:, cols], p_s[...], 0, 0)
    g_s[:, units:] = dot(d_s[:, cols], c_s[...], 0, 0)

    @pl.when(j == 0)
    def _():
        other_ref[...] = low(g_s[...])

    @pl.when(j == 1)
    def _():
        own_ref[...] = g_s[...]


def mlp_weights(scalars, twos, dy, order, pres, acts):
    rows, width = dy.shape
    units = pres[0].shape[1]
    part = width // 2
    outs = [shape((part, 2 * units), F32), shape((part, 2 * units), BF), shape((8, max(width, units)), F32)]
    fixed = [(o, pl.BlockSpec(o.shape, lambda i, sc: (0, 0))) for o in outs]
    args = twos + [dy] + pres + acts
    scratch = [pltpu.VMEM((rows, n), BF) for n in (width, width, units, units)] + [pltpu.VMEM((part, 2 * units), F32)]
    return call(
        functools.partial(weights_kernel, len(twos), order), "mlp_weights", scalars, (2,), [whole(v) for v in args], fixed, scratch, args,
        4 * rows * width * units, 12_000_000, 40,
    )


PAIR = [(0, 1), (1, 0)]


def swap_core(values):
    return lax.ppermute(values, "tp", [(i, i ^ 1) for i in range(4)])


def swap_y(values):
    return lax.ppermute(values, "tp", [(i, i ^ 2) for i in range(4)])


def hop(values, pairs):
    return lax.ppermute(values, "ctx", pairs)


def after(values, *deps):
    return lax.optimization_barrier((values, *deps))[0]


def pick(parts, index):
    return lax.dynamic_index_in_dim(parts, index, 0, keepdims=False)


def ordered(first, second, flip):
    return jnp.where(flip == 0, jnp.stack([first, second]), jnp.stack([second, first]))


def sum_ctx(values, z):
    near, far = z & 1, z >> 1
    near_pairs, far_pairs = [(i, i ^ 1) for i in range(4)], [(i, i ^ 2) for i in range(4)]
    rows, cols = values.shape
    halves = values.reshape(2, rows // 2, cols)
    half = pick(halves, near) + wide(hop(low(pick(halves, 1 - near)), near_pairs))
    quarters = half.reshape(2, rows // 4, cols)
    quarter = low(pick(quarters, far) + wide(hop(low(pick(quarters, 1 - far)), far_pairs)))
    half = ordered(quarter, hop(quarter, far_pairs), far).reshape(rows // 2, cols)
    return wide(ordered(half, hop(half, near_pairs), near).reshape(rows, cols))


def body(
    hidden,
    prefix,
    w_qkv,
    b_qkv,
    w_out,
    b_out,
    w_up,
    b_up,
    w_down,
    b_down,
    ln1_gain,
    ln1_shift,
    ln2_gain,
    ln2_shift,
    cotangent,
):
    members = lax.axis_size("fsdp")
    paired = members == 2
    z = lax.axis_index("ctx")
    t = lax.axis_index("tp")
    half_ctx = lax.axis_size("ctx") // 2
    core, side = t & 1, t >> 1
    turn_q, turn_k = 2 * core, 2 * core + side
    f = lax.axis_index("fsdp") if paired else jnp.int32(0)
    rows, width = hidden.shape[1], hidden.shape[2]
    local, units = w_qkv.shape[2], w_up.shape[1]
    half, quarter, part = rows // 2, rows // 4, width // 2
    tiles = rows // TILE
    scalars = jnp.stack([z, turn_q, turn_k, prefix[0], jnp.int32(half_ctx), f]).astype(jnp.int32)

    def both(values, axis):
        if paired:
            return values, lax.ppermute(values, "fsdp", PAIR)
        return tuple(jnp.split(lax.all_gather(values, "fsdp", axis=axis, tiled=True), 2, axis=axis))

    qkv_a, qkv_b = both(w_qkv.reshape(w_qkv.shape[0], 3 * local), 0)
    own_quarter = lax.dynamic_slice(hidden[0], (turn_k * quarter, 0), (quarter, width))
    first = hop(own_quarter, [(2, 1), (3, 2)])
    aside = hop(own_quarter, [(2, 3)])

    def spread(values):
        other = swap_y(values)
        return [(v, 0) for v in (values, other, swap_core(values), swap_core(other))]

    vectors_in = (ln1_gain, ln1_shift, b_out, ln2_gain, ln2_shift, b_down)
    fold_rows = (b_qkv.size // b_qkv.shape[-1], b_up.shape[0])
    if paired:
        small = packed(vectors_in, (b_qkv, b_up))
        small_b = lax.ppermute(small, "fsdp", PAIR)
        vec, bias_qkv, bias_up = unpacked(scalars, small, small_b, fold_rows)
    else:
        small_b = qkv_b
        gather = lambda v: wide(lax.all_gather(v, "fsdp", axis=v.ndim - 1, tiled=True))
        found = [gather(v) for v in vectors_in]
        vec = jnp.stack(found[:2] + found)
        bias_qkv, bias_up = gather(b_qkv).reshape(1, -1), gather(b_up).reshape(1, -1)
    gain_one, shift_one, gain_two, shift_two, bias_down = vec[2], vec[3], vec[5], vec[6], vec[7]
    far_quarter = first + aside
    second = hop(after(first, qkv_b, small_b), [(1, 0), (2, 1)])
    near_quarter = jnp.where(z >= half_ctx, own_quarter, second)
    far_pieces = spread(far_quarter)
    later = after((w_out, w_up, w_down), small_b)
    out_a, out_b = both(later[0], 1)
    up_a, up_b = both(later[1], 0)
    down_a, down_b = both(later[2], 1)

    lane = jnp.arange(local, dtype=jnp.int32) % (HD // 2)
    frequency = jnp.power(jnp.float32(10000.0), -2.0 * wide(lane) / HD)[None, :]
    base = wide(jnp.arange(TILE, dtype=jnp.int32))[:, None] * frequency
    turns = wide(jnp.arange(half_ctx * tiles, dtype=jnp.int32) * TILE)[:, None] * frequency
    base, turns = jnp.stack([jnp.cos(base), jnp.sin(base)]), jnp.stack([jnp.cos(turns), jnp.sin(turns)])

    q, k_own, v_own, norm_own, x_turned, dy = project(
        scalars, [hidden[0]], cotangent[0], False, rows, vec, qkv_a, qkv_b, bias_qkv, base, turns
    )
    near_pieces = spread(after(near_quarter, far_pieces[1][0]))
    k_far, v_far, norm_far = project(scalars, far_pieces, None, True, rows, vec, qkv_a, qkv_b, after(bias_qkv, q, out_b), base, turns)
    k_near, v_near, norm_near = project(scalars, near_pieces, None, False, rows, vec, qkv_a, qkv_b, after(bias_qkv, k_far, up_b), base, turns)
    keys, values = [k_own, k_near, k_far], [v_own, v_near, v_far]

    def core_sum(kept, sent):
        return low(wide(kept) + wide(swap_core(sent)))

    o0, lse0, *share = attention(scalars, 0, 2, after(q, down_b), keys, values, out_a, out_b)
    mine0 = core_sum(*share)
    o1, lse1, *share = attention(scalars, 1, 2, after(q, mine0), keys, values, out_a, out_b)
    mine1 = core_sum(*share)
    mid0, two0 = norm_two(scalars, 0, x_turned, mine0, swap_y(mine0), vec)
    twos0 = (two0, swap_core(two0))
    *share, act0, pre0, down_keep, down_send = mlp(scalars, 0, 2, after(twos0[0], mine1), twos0[1], dy, up_a, up_b, down_a, down_b, bias_up, [])
    back0 = core_sum(*share)
    mid1, two1 = norm_two(scalars, 1, x_turned, mine1, after(swap_y(mine1), back0), vec)
    twos1 = (two1, swap_core(two1))
    *share, act1, pre1, down_keep, down_send = mlp(scalars, 1, 2, *twos1, dy, up_a, up_b, down_a, down_b, bias_up, [down_keep, down_send])
    back1 = core_sum(*share)
    back_y0, back_y1 = swap_y(back0), swap_y(back1)

    dmid0, dz0 = norm_two_grad(scalars, 0, dy, mid0, back0, back_y0, vec)
    dzs0 = (dz0, swap_core(dz0))
    act0, act1, pre0, pre1 = after((act0, act1, pre0, pre1), back1, dz0)
    g_own, g_other, sums_mlp = mlp_weights(scalars, list(twos0) + list(twos1), dy, (0, 2, 1, 3), [pre0, pre1], [act0, act1])

    def partner_sum(own_part, other_part):
        if paired:
            return own_part + wide(lax.ppermute(other_part, "fsdp", PAIR))
        return lax.psum_scatter(jnp.concatenate([own_part, wide(other_part)], axis=0), "fsdp", scatter_dimension=0, tiled=True)

    group = partner_sum(g_own, g_other)
    near_bit, far_bit = z & 1, z >> 1
    near_pairs, far_pairs = [(i, i ^ 1) for i in range(4)], [(i, i ^ 2) for i in range(4)]

    def split(values, bit):
        grid = values.reshape(2, values.shape[0] // 2, values.shape[1])
        return pick(grid, bit), low(pick(grid, 1 - bit))

    dmid1, dz1 = norm_two_grad(scalars, 1, dy, mid1, back1, back_y1, vec)
    dzs1 = (dz1, swap_core(dz1))
    dq0, dk0, dv0 = attention_grads(scalars, 0, 2, after(q, g_other), o0, *dzs0, lse0, keys, values, out_a, out_b, base, turns)
    g_keep, g_send = split(group, near_bit)
    dq1, dk1, dv1 = attention_grads(scalars, 1, 2, after(q, dk0, g_send), o1, *dzs1, lse1, keys, values, out_a, out_b, base, turns)
    g_half = g_keep + wide(hop(g_send, near_pairs))
    down = core_sum(down_keep, after(down_send, dk0))
    down_y = swap_y(down)
    g_keep, g_send = split(g_half, far_bit)
    dk1, g_send = after((dk1, g_send), g_send)
    g_quarter = low(g_keep + wide(hop(g_send, far_pairs)))
    g_half = ordered(g_quarter, hop(g_quarter, far_pairs), far_bit).reshape(g_half.shape)
    first_group = wide(ordered(g_half, hop(g_half, near_pairs), near_bit).reshape(group.shape))

    result_half = low(jnp.concatenate([mid0, mid1], axis=0) + (wide(down) + wide(down_y)) + bias_down)
    other = swap_core(result_half)
    result = placed(scalars, 1, [(result_half, 0), (result_half, 1), (other, 0), (other, 1)], BF)

    dks, dvs = [dk0, dk1], [dv0, dv1]
    *seen, t_seen, sums_seen = shares(scalars, tiles, [], [], [], [], dks, dvs, [norm_near, norm_far], qkv_a, qkv_b)
    *share_own, g_two, g_two_other, sums, sums_out = shares(
        scalars, 0, after([dq0, dq1], g_quarter, t_seen), [o0, o1], [*dzs0, *dzs1], [t_seen, sums_seen], dks, dvs, [norm_own], qkv_a, qkv_b
    )
    second_part = partner_sum(g_two, g_two_other)

    def core_halves(kept, sent):
        got = swap_core(sent)
        return [low(wide(kept[n : n + quarter]) + wide(got[n : n + quarter])) for n in (0, quarter)]

    near_keep, near_send = core_halves(*seen[:2])
    far_keep, far_send = core_halves(*seen[2:])
    near_q = low(wide(near_keep) + wide(swap_y(near_send)))
    near_in = hop(near_q, [(0, 1), (1, 3)])
    far_q = wide(far_keep) + wide(swap_y(after(far_send, near_q)))
    far_q = low(far_q + jnp.where(z == 1, wide(near_in), 0.0))
    far_in = wide(hop(far_q, [(1, 2)])) + wide(hop(far_q, [(3, 2)]))
    own_low, own_high = core_halves(*share_own)
    own_send = jnp.where(side == 0, own_high, own_low)
    da_one = wide(jnp.where(side == 0, own_low, own_high)) + wide(swap_y(after(own_send, far_q)))
    da_one = da_one + far_in + jnp.where(z >= half_ctx, wide(near_q) + jnp.where(z == 3, wide(near_in), 0.0), 0.0)
    x_q = wide(lax.dynamic_slice(x_turned, (side * quarter, 0), (quarter, width)))
    grad_q = low(jnp.where(side == 0, dmid0, dmid1) + norm_back(da_one, x_q, gain_one))
    grad_y = swap_y(grad_q)
    grad_input = placed(scalars, 2, [(v, 0) for v in (grad_q, grad_y, swap_core(grad_q), swap_core(grad_y))], F32)

    second_group = sum_ctx(second_part, z)

    def gain_grad(weights, grad, bias_grad, gain, shift):
        full = wide(jnp.concatenate(weights, axis=0))
        by_shift = jnp.sum(full * bias_grad[None, :], axis=1)
        return (jnp.sum(full * grad, axis=1) - shift * by_shift) / gain, by_shift

    g_own, g_two, sums_mlp, sums, sums_out = after((g_own, g_two, sums_mlp, sums, sums_out), near_q)
    joined = lambda own, other, cols: jnp.concatenate([own[:, cols], wide(other[:, cols])], axis=0)
    gb_up, gb_down, gb_out, gb_qkv = sums_mlp[0], sums_mlp[1] * 0.25, sums_out[0] * 0.25, sums[:3].reshape(-1)
    g_gain_one, g_shift_one = gain_grad((qkv_a, qkv_b), joined(g_two, g_two_other, slice(local, None)), gb_qkv, gain_one, shift_one)
    g_gain_two, g_shift_two = gain_grad((up_a, up_b), joined(g_own, g_other, slice(0, units)), gb_up, gain_two, shift_two)
    over_tp = after(jnp.stack([gb_out, gb_down, g_gain_one, g_shift_one, g_gain_two, g_shift_two]), near_q)
    over_tp = over_tp + swap_core(over_tp)
    over_tp = over_tp + swap_y(over_tp)
    if paired:
        take = lambda v, n: lax.dynamic_index_in_dim(v.reshape(-1, 2, HD // 2), n, 1, keepdims=False).reshape(-1)
        mine = jnp.concatenate([over_tp[:, :part].reshape(-1), take(gb_qkv, f), take(gb_up, f)])
        other = jnp.concatenate([over_tp[:, part:].reshape(-1), take(gb_qkv, 1 - f), take(gb_up, 1 - f)])
        vectors = mine + lax.ppermute(other, "fsdp", PAIR)
    else:
        scattered = [
            lax.psum_scatter(v, "fsdp", scatter_dimension=1, tiled=True).reshape(-1)
            for v in (over_tp, gb_qkv.reshape(-1, HD), gb_up.reshape(-1, HD))
        ]
        vectors = jnp.concatenate(scattered)
    vectors = vectors + hop(vectors, [(i, i ^ 1) for i in range(4)])
    vectors = vectors + hop(vectors, [(i, i ^ 2) for i in range(4)])
    own = width // members
    named = vectors[: 6 * own].reshape(6, own)
    cut = 6 * own + b_qkv.size
    return (
        result[None],
        grad_input[None],
        second_group[:, local:].reshape(w_qkv.shape),
        vectors[6 * own : cut].reshape(b_qkv.shape),
        second_group[:, :local].T,
        named[0],
        first_group[:, :units],
        vectors[cut:].reshape(b_up.shape),
        first_group[:, units:].T,
        named[1],
        named[2],
        named[3],
        named[4],
        named[5],
    )


def solution(mesh):
    rows = P("fsdp", "ctx", None)
    weights = (P("fsdp", None, "tp"), P(None, "tp", "fsdp"), P("tp", "fsdp"), P("fsdp"), P("fsdp", "tp"), P("tp", "fsdp"), P("tp", "fsdp"))
    vectors = (P("fsdp"),) * 5
    return jax.shard_map(
        body,
        mesh=mesh,
        in_specs=(rows, P("fsdp")) + weights + vectors + (rows,),
        out_specs=(rows, rows) + weights + vectors,
        check_vma=False,
    )
```

```python
import functools
import jax
import jax.numpy as jnp
from jax import lax
from jax.experimental import pallas as pl
from jax.experimental.pallas import tpu as pltpu
from jax.sharding import PartitionSpec as P

HD = 64
BLOCK = 16
TILE = 256
WIDE = 512
LOG2E = 1.4426950408889634
NEG = -1e30
epsilon = 1e-05
BF, F32 = jnp.bfloat16, jnp.float32


def low(values):
    return values.astype(BF)


def wide(values):
    return values.astype(F32)


def dot(a, b, ca=1, cb=0):
    return lax.dot_general(a, b, (((ca,), (cb,)), ((), ())), preferred_element_type=F32)


def shape(dims, kind):
    return jax.ShapeDtypeStruct(dims, kind)


def in_hbm(values):
    return pltpu.with_memory_space_constraint(values, pltpu.HBM) if values.size >= 65536 else values


def call(kernel, name, scalars, grid, ins, outs, scratch, args, flops, moved, room=24):
    return pl.pallas_call(
        kernel,
        name=name,
        out_shape=[s for s, _ in outs],
        grid_spec=pltpu.PrefetchScalarGridSpec(
            num_scalar_prefetch=1, grid=grid, in_specs=ins, out_specs=[b for _, b in outs], scratch_shapes=scratch
        ),
        compiler_params=pltpu.CompilerParams(dimension_semantics=("arbitrary",) * len(grid), vmem_limit_bytes=room << 20),
        cost_estimate=pl.CostEstimate(flops=flops, bytes_accessed=moved, transcendentals=0),
    )(scalars, *args)


def whole(values):
    dims = values.shape
    return pl.BlockSpec(dims, lambda i, sc: (0,) * len(dims))


def row_block(values, index):
    return pl.BlockSpec((TILE, values.shape[1]), lambda i, sc: (index(i, sc), 0))


def turn_matrix(width):
    k = lax.broadcasted_iota(jnp.int32, (width, width), 0)
    n = lax.broadcasted_iota(jnp.int32, (width, width), 1)
    first = (n & (HD - 1)) < HD // 2
    return jnp.where(first & (k == n + HD // 2), -1.0, jnp.where((~first) & (k == n - HD // 2), 1.0, 0.0)).astype(BF)


def tile_angles(base_ref, tile_ref, index):
    cos, sin = base_ref[0], base_ref[1]
    cos_t, sin_t = tile_ref[0, pl.ds(index, 1), :], tile_ref[1, pl.ds(index, 1), :]
    return cos * cos_t - sin * sin_t, sin * cos_t + cos * sin_t


def unit_rows(x):
    mean = jnp.mean(x, axis=-1, keepdims=True)
    centered = x - mean
    variance = jnp.mean(centered * centered, axis=-1, keepdims=True)
    scale = lax.rsqrt(variance + epsilon)
    return centered * scale, scale


def project_kernel(parts, with_q, far, tiles, sc_ref, *refs):
    refs = list(refs)
    xs = [refs.pop(0) for _ in range(parts)]
    dy_ref = refs.pop(0) if with_q else None
    vec_ref, wa_ref, wb_ref, bias_ref, base_ref, tile_ref = [refs.pop(0) for _ in range(6)]
    outs = [refs.pop(0) for _ in range(3 if with_q else 2)]
    norm_ref = refs.pop(0)
    if with_q:
        keep_ref, dy_out = refs.pop(0), refs.pop(0)
    w_s, r_s, b_s, x_s, a_s = refs
    j = pl.program_id(0)
    f = sc_ref[5]
    local = outs[0].shape[1]
    part = wa_ref.shape[0]
    skip = 0 if with_q else 1
    count = len(outs)

    @pl.when(j == 0)
    def _():
        turn = turn_matrix(local)
        for n in range(count):
            cols = slice((n + skip) * local, (n + skip + 1) * local)
            w_s[n, :part] = wa_ref[:, cols]
            w_s[n, part:] = wb_ref[:, cols]
            if n < count - 1:
                r_s[n] = low(dot(w_s[n], turn))
                b_s[n] = dot(jnp.broadcast_to(bias_ref[:, cols], (8, local)).astype(BF), turn)

    if parts == 1:
        x = wide(xs[0][...])
    else:
        for n in range(parts):

            @pl.when(j == n)
            def _(n=n):
                x_s[...] = xs[n][...]

        x = wide(x_s[...])
    unit, _ = unit_rows(x)
    a_s[...] = unit * vec_ref[0:1] + vec_ref[1:2]
    first = pl.ds(pl.multiple_of(f * part, 128), part)
    second = pl.ds(pl.multiple_of((1 - f) * part, 128), part)
    a = jnp.concatenate([low(a_s[:, first]), low(a_s[:, second])], axis=1)
    norm_ref[...] = a
    if with_q:
        keep_ref[:, :part] = xs[0][:, first]
        keep_ref[:, part:] = xs[0][:, second]
        dy_out[:, :part] = dy_ref[:, first]
        dy_out[:, part:] = dy_ref[:, second]
    at = j ^ sc_ref[1 if with_q else 2]
    cos, sin = tile_angles(base_ref, tile_ref, at if far else at + lax.rem(sc_ref[0], sc_ref[4]) * tiles)
    for n in range(count):
        cols = slice((n + skip) * local, (n + skip + 1) * local)
        u = dot(a, w_s[n]) + bias_ref[:, cols]
        if n < count - 1:
            u = u * cos + (dot(a, r_s[n]) + b_s[n, 0:1]) * sin
        u = low(u)
        if n == 0 and with_q:
            u = u * jnp.asarray(HD**-0.5, BF)
        outs[n][...] = u


def project(scalars, xs, dy, far, rows, vec, wa, wb, bias, base, turns):
    with_q = dy is not None
    width = wa.shape[0] * 2
    local = wa.shape[1] // 3
    tiles = rows // TILE
    if with_q:
        turned = lambda i, sc: i ^ sc[1]
        ins = [row_block(xs[0], turned), row_block(dy, turned)]
        args = [xs[0], dy]
        parts = 1
    else:
        ins = [pl.BlockSpec((TILE, width), lambda i, sc, n=n: (n, 0)) for _, n in xs]
        args = [v for v, _ in xs]
        parts = len(xs)
    ins += [whole(v) for v in (vec, wa, wb, bias, base, turns)]
    args += [vec, wa, wb, bias, base, turns]
    tile = lambda n: pl.BlockSpec((TILE, n), lambda i, sc: (i, 0))
    count = 3 if with_q else 2
    outs = [(shape((rows, local), BF), tile(local))] * count + [(shape((rows, width), BF), tile(width))] * (3 if with_q else 1)
    scratch = [
        pltpu.VMEM((count, width, local), BF),
        pltpu.VMEM((count - 1, width, local), BF),
        pltpu.VMEM((count - 1, 8, local), F32),
        pltpu.VMEM((TILE, width), BF),
        pltpu.VMEM((TILE, width), F32),
    ]
    return call(
        functools.partial(project_kernel, parts, with_q, far, tiles), "project" if with_q else "project_seen", scalars, (tiles,), ins, outs, scratch, args,
        2 * rows * width * local * 5, 8_000_000,
    )


def stack_heads(rows, heads):
    lane = lax.broadcasted_iota(jnp.int32, rows.shape, 1) // HD
    return jnp.concatenate([jnp.where(lane == h, rows, jnp.zeros_like(rows)) for h in range(heads)], axis=0)


def tile_plan(sc_ref, tile, tiles):
    z, prefix, half = sc_ref[0], sc_ref[3], sc_ref[4]
    noisy = z < half
    late = lax.rem(z, half)
    at = tile ^ sc_ref[1]
    prefix = jnp.where(late == 0, prefix, 0)
    top = jnp.maximum(at + 1, (prefix + TILE - 1) // TILE)
    return noisy, late == 1, at, top, prefix


def near_rows(sc_ref, t):
    return pl.ds(pl.multiple_of((t ^ sc_ref[2]) * TILE, TILE), TILE)


def edge_mask(block_gap, k_pos, t, at, noisy, prefix):
    limit = (at - t) * (TILE // BLOCK) + jnp.where(noisy, 0, 1)
    return (block_gap < limit) | (k_pos < prefix - t * TILE)


def fwd_kernel(first, stride, tiles, sc_ref, q_ref, ko_ref, vo_ref, km_ref, vm_ref, kf_ref, vf_ref, wa_ref, wb_ref, o_ref, lse_ref, keep_ref, send_ref, sbuf, mbuf, lbuf, acc):
    tile = first + stride * pl.program_id(0)
    noisy, late, at, top, prefix = tile_plan(sc_ref, tile, tiles)
    width = q_ref.shape[1]
    heads = width // HD
    qs = stack_heads(q_ref[...], heads)
    mbuf[...] = jnp.full_like(mbuf, NEG)
    lbuf[...] = jnp.zeros_like(lbuf)
    acc[...] = jnp.zeros_like(acc)
    high = heads * TILE
    own = pl.ds(pl.multiple_of(tile * TILE, TILE), TILE)

    def keep(slot, s):
        best = mbuf[...]
        for n in range(s.shape[1] // TILE):
            sbuf[slot + n] = s[:, n * TILE : (n + 1) * TILE]
        for n in range(s.shape[1] // 128):
            best = jnp.maximum(best, s[:, n * 128 : (n + 1) * 128])
        mbuf[...] = best

    def plain_step(t, carry):
        keep(t, dot(qs, km_ref[near_rows(sc_ref, t), :], 1, 1))
        return carry

    lax.fori_loop(0, at, plain_step, 0)
    wides = tiles * TILE // WIDE

    def far_rows(n):
        return pl.ds(pl.multiple_of(n * WIDE, WIDE), WIDE)

    def far_step(n, carry):
        keep(tiles + n * (WIDE // TILE), dot(qs, kf_ref[far_rows(n), :], 1, 1))
        return carry

    lax.fori_loop(0, jnp.where(late, wides, 0), far_step, 0)
    q_block = (lax.broadcasted_iota(jnp.int32, (high, TILE), 0) & (TILE - 1)) >> 4
    k_pos = lax.broadcasted_iota(jnp.int32, (high, TILE), 1)
    gap = (k_pos >> 4) - q_block

    def edge_step(t, carry):
        s = dot(qs, km_ref[near_rows(sc_ref, t), :], 1, 1)
        keep(t, jnp.where(edge_mask(gap, k_pos, t, at, noisy, prefix), s, NEG))
        return carry

    lax.fori_loop(at, top, edge_step, 0)

    @pl.when(noisy)
    def _():
        keep(2 * tiles, jnp.where(gap == 0, dot(qs, ko_ref[own, :], 1, 1), NEG))

    best = jnp.max(mbuf[...], axis=1, keepdims=True) * LOG2E
    mbuf[...] = jnp.broadcast_to(best, mbuf.shape)

    def add(slot, v):
        m = mbuf[...]
        total = lbuf[...]
        cols = []
        for n in range(v.shape[0] // TILE):
            s = sbuf[slot + n]
            for k in range(TILE // 128):
                p = jnp.exp2(s[:, k * 128 : (k + 1) * 128] * LOG2E - m)
                total = total + p
                cols.append(low(p))
        lbuf[...] = total
        acc[...] += dot(jnp.concatenate(cols, axis=1), v)

    def near_sum(t, carry):
        add(t, vm_ref[near_rows(sc_ref, t), :])
        return carry

    lax.fori_loop(0, top, near_sum, 0)

    def far_sum(n, carry):
        add(tiles + n * (WIDE // TILE), vf_ref[far_rows(n), :])
        return carry

    lax.fori_loop(0, jnp.where(late, wides, 0), far_sum, 0)

    @pl.when(noisy)
    def _():
        add(2 * tiles, vo_ref[own, :])

    norm = jnp.sum(lbuf[...], axis=1, keepdims=True)
    out = acc[...] * (1.0 / norm)
    lane = lax.broadcasted_iota(jnp.int32, (TILE, width), 1) // HD
    picked = out[:TILE]
    for h in range(1, heads):
        picked = jnp.where(lane == h, out[h * TILE : (h + 1) * TILE], picked)
    picked = low(picked)
    o_ref[...] = picked
    lse = jnp.broadcast_to(best + jnp.log2(norm), (high, 128))
    lse_ref[0] = jnp.concatenate(
        [lse[h * TILE : (h + 1) * TILE].T[:1] for h in range(heads)] + [jnp.zeros((8 - heads, TILE), F32)], axis=0
    )
    part = wa_ref.shape[1]
    for n, ref in enumerate((keep_ref, send_ref)):

        @pl.when(pl.program_id(0) == n)
        def _(ref=ref):
            ref[:, :part] = low(dot(picked, wa_ref[...]))
            ref[:, part:] = low(dot(picked, wb_ref[...]))


def attention(scalars, first, stride, q, keys, values, wa, wb):
    rows, width = q.shape
    tiles, heads = rows // TILE, width // HD
    count = tiles // stride
    flat = [v for pair in zip(keys, values) for v in pair]
    tile = lambda n: pl.BlockSpec((TILE, n), lambda i, sc: (i, 0))
    full = 2 * wa.shape[1]
    return call(
        functools.partial(fwd_kernel, first, stride, tiles), "attn_fwd", scalars, (count,),
        [row_block(q, lambda i, sc: first + stride * i)] + [whole(v) for v in flat + [wa, wb]],
        [
            (shape((count * TILE, width), BF), tile(width)),
            (shape((count, 8, TILE), F32), pl.BlockSpec((1, 8, TILE), lambda i, sc: (i, 0, 0))),
        ]
        + [(shape((TILE, full), BF), pl.BlockSpec((TILE, full), lambda i, sc: (0, 0)))] * 2,
        [
            pltpu.VMEM((2 * tiles + 1, heads * TILE, TILE), F32),
            pltpu.VMEM((heads * TILE, 128), F32),
            pltpu.VMEM((heads * TILE, 128), F32),
            pltpu.VMEM((heads * TILE, width), F32),
        ],
        [q] + flat + [wa, wb], 3_000_000_000 * count, 4_000_000,
    )


def turn_back(grad, cos, sin, turn):
    moved = grad * sin
    high = low(moved)
    rest = low(moved - wide(high))
    return low(grad * cos - (dot(high, turn) + dot(rest, turn)))


def bwd_kernel(first, stride, tiles, sc_ref, q_ref, o_ref, za_ref, zb_ref, lse_ref, ko_ref, vo_ref, km_ref, vm_ref, kf_ref, vf_ref, wa_ref, wb_ref, base_ref, tile_ref,
               dq_ref, dk_ref, dv_ref, dqt, st, gt, lse_s, del_s, qs_s, gs_s, z_s, dk_s, dv_s):
    g_id = pl.program_id(0)
    tile = first + stride * g_id
    noisy, late, at, top, prefix = tile_plan(sc_ref, tile, tiles)
    width = q_ref.shape[1]
    heads = width // HD
    high = heads * TILE
    part = wa_ref.shape[1]
    rows = tiles * TILE
    per = za_ref.shape[0] // TILE

    @pl.when(g_id == 0)
    def _():
        dk_s[...] = jnp.zeros_like(dk_s)
        dv_s[...] = jnp.zeros_like(dv_s)

    for n in range(2 * per):

        @pl.when(g_id == n)
        def _(n=n):
            z_s[...] = (za_ref if n < per else zb_ref)[(n % per) * TILE : (n % per + 1) * TILE, :]

    z = z_s[...]
    g32 = dot(z[:, :part], wa_ref[...], 1, 1) + dot(z[:, part:], wb_ref[...], 1, 1)
    g = low(g32)
    g32 = wide(g)
    q = q_ref[...]
    qs_s[...] = stack_heads(q, heads)
    gs_s[...] = stack_heads(g, heads)
    q_t = wide(q).T
    g_t = g32.T
    prod = (wide(o_ref[...]) * g32).T
    head_of = lax.broadcasted_iota(jnp.int32, (width, TILE), 0) // HD
    for h in range(heads):
        cols = slice(h * TILE, (h + 1) * TILE)
        st[:, cols] = low(jnp.where(head_of == h, q_t, 0.0))
        gt[:, cols] = low(jnp.where(head_of == h, g_t, 0.0))
        del_s[:, cols] = jnp.sum(prod[h * HD : (h + 1) * HD], axis=0, keepdims=True)
        lse_s[:, cols] = lse_ref[0, h : h + 1, :]
    dqt[...] = jnp.zeros_like(dqt)

    def step(k, v, base, mask):
        n = k.shape[0]
        to = pl.ds(base, n)
        s = dot(k, st[...])
        p = jnp.exp2(s * LOG2E - lse_s[...])
        if mask is not None:
            p = jnp.where(mask, p, 0.0)
        dp = dot(v, gt[...])
        ds = low(p * (dp - del_s[...]))
        p = low(p)
        dv_s[to, :] += dot(p, gs_s[...])
        dk_s[to, :] += dot(ds, qs_s[...])
        dqt[...] += dot(k, ds, 0, 0)

    def near_at(t):
        return pl.multiple_of(rows + (t ^ sc_ref[2]) * TILE, TILE)

    def plain_step(t, carry):
        at_t = near_rows(sc_ref, t)
        step(km_ref[at_t, :], vm_ref[at_t, :], near_at(t), None)
        return carry

    lax.fori_loop(0, at, plain_step, 0)
    wides = rows // WIDE

    def far_step(n, carry):
        at_n = pl.ds(pl.multiple_of(n * WIDE, WIDE), WIDE)
        step(kf_ref[at_n, :], vf_ref[at_n, :], pl.multiple_of(2 * rows + n * WIDE, WIDE), None)
        return carry

    lax.fori_loop(0, jnp.where(late, wides, 0), far_step, 0)
    k_pos = lax.broadcasted_iota(jnp.int32, (TILE, high), 0)
    gap = (k_pos >> 4) - ((lax.broadcasted_iota(jnp.int32, (TILE, high), 1) & (TILE - 1)) >> 4)

    def edge_step(t, carry):
        at_t = near_rows(sc_ref, t)
        step(km_ref[at_t, :], vm_ref[at_t, :], near_at(t), edge_mask(gap, k_pos, t, at, noisy, prefix))
        return carry

    lax.fori_loop(at, top, edge_step, 0)

    @pl.when(noisy)
    def _():
        own = pl.ds(pl.multiple_of(tile * TILE, TILE), TILE)
        step(ko_ref[own, :], vo_ref[own, :], pl.multiple_of(tile * TILE, TILE), gap == 0)

    turn = turn_matrix(width)
    dq_t = jnp.where(head_of == 0, dqt[:, :TILE], 0.0)
    for h in range(1, heads):
        dq_t = jnp.where(head_of == h, dqt[:, h * TILE : (h + 1) * TILE], dq_t)
    late_at = late.astype(jnp.int32) * tiles
    dq_ref[...] = turn_back(dq_t.T * (HD**-0.5), *tile_angles(base_ref, tile_ref, at + late_at), turn)

    @pl.when(g_id == pl.num_programs(0) - 1)
    def _():
        dv_ref[...] = low(dv_s[...])

        def finish(base, true_tile):
            to = pl.ds(pl.multiple_of(base, TILE), TILE)
            dk_ref[to, :] = turn_back(dk_s[to, :], *tile_angles(base_ref, tile_ref, true_tile), turn)

        def all_three(j, carry):
            finish(j * TILE, (j ^ sc_ref[1]) + late_at)
            finish(rows + j * TILE, (j ^ sc_ref[2]) + late_at)
            finish(2 * rows + j * TILE, j ^ sc_ref[2])
            return carry

        lax.fori_loop(0, tiles, all_three, 0)


def attention_grads(scalars, first, stride, q, o, za, zb, lse, keys, values, wa, wb, base, turns):
    rows, width = q.shape
    tiles, heads = rows // TILE, width // HD
    count = tiles // stride
    flat = [v for pair in zip(keys, values) for v in pair]
    tile = pl.BlockSpec((TILE, width), lambda i, sc: (i, 0))
    total = pl.BlockSpec((3 * rows, width), lambda i, sc: (0, 0))
    high = heads * TILE
    return call(
        functools.partial(bwd_kernel, first, stride, tiles), "attn_bwd", scalars, (count,),
        [row_block(q, lambda i, sc: first + stride * i), tile, whole(za), whole(zb), pl.BlockSpec((1, 8, TILE), lambda i, sc: (i, 0, 0))]
        + [whole(v) for v in flat + [wa, wb, base, turns]],
        [(shape((count * TILE, width), BF), tile), (shape((3 * rows, width), BF), total), (shape((3 * rows, width), BF), total)],
        [
            pltpu.VMEM((width, high), F32),
            pltpu.VMEM((width, high), BF),
            pltpu.VMEM((width, high), BF),
            pltpu.VMEM((1, high), F32),
            pltpu.VMEM((1, high), F32),
            pltpu.VMEM((high, width), BF),
            pltpu.VMEM((high, width), BF),
            pltpu.VMEM((TILE, za.shape[1]), BF),
            pltpu.VMEM((3 * rows, width), F32),
            pltpu.VMEM((3 * rows, width), F32),
        ],
        [q, o, za, zb, lse] + flat + [wa, wb, base, turns], 8_000_000_000 * count, 10_000_000,
    )


def norm_kernel(sc_ref, x_ref, mine_ref, theirs_ref, vec_ref, mid_ref, a_ref):
    mid = wide(x_ref[...]) + (wide(mine_ref[...]) + wide(theirs_ref[...])) + vec_ref[4:5]
    mid_ref[...] = mid
    unit, _ = unit_rows(mid)
    a_ref[...] = low(unit * vec_ref[5:6] + vec_ref[6:7])


def norm_two(scalars, index, x, mine, theirs, vec):
    rows, width = mine.shape
    block = pl.BlockSpec((rows, width), lambda i, sc: (0, 0))
    return call(
        norm_kernel, "norm_two", scalars, (1,),
        [row_block(x, lambda i, sc: index), block, block, whole(vec)],
        [(shape((rows, width), F32), block), (shape((rows, width), BF), block)], [], [x, mine, theirs, vec], 10 * rows * width, 3_000_000,
    )


def norm_back(grad, x, gain):
    unit, scale = unit_rows(x)
    weighted = grad * gain
    return scale * (weighted - jnp.mean(weighted, axis=-1, keepdims=True) - unit * jnp.mean(weighted * unit, axis=-1, keepdims=True))


def norm_grad_kernel(sc_ref, dy_ref, mid_ref, mine_ref, theirs_ref, vec_ref, dmid_ref, dz_ref):
    dmid = wide(dy_ref[...]) + norm_back(wide(mine_ref[...]) + wide(theirs_ref[...]), mid_ref[...], vec_ref[5:6])
    dmid_ref[...] = dmid
    dz_ref[...] = low(dmid)


def norm_two_grad(scalars, index, dy, mid, mine, theirs, vec):
    rows, width = mid.shape
    block = pl.BlockSpec((rows, width), lambda i, sc: (0, 0))
    return call(
        norm_grad_kernel, "norm_two_grad", scalars, (1,),
        [row_block(dy, lambda i, sc: index), block, block, block, whole(vec)],
        [(shape((rows, width), F32), block), (shape((rows, width), BF), block)], [], [dy, mid, mine, theirs, vec], 20 * rows * width, 3_000_000,
    )


def mlp_kernel(last, sc_ref, a_ref, b_ref, dy_ref, ua_ref, ub_ref, da_ref, db_ref, bias_ref, *refs):
    refs = list(refs)
    done = [refs.pop(0) for _ in range(2 if last else 0)]
    keep_ref, send_ref, act_ref, pre_ref, down_keep, down_send, x_s = refs
    g = pl.program_id(0)
    part = ua_ref.shape[0]

    @pl.when(g == 0)
    def _():
        x_s[...] = a_ref[...]

    @pl.when(g == 1)
    def _():
        x_s[...] = b_ref[...]

    x, dy = x_s[...], dy_ref[...]
    pre = dot(x[:, :part], ua_ref[...]) + dot(x[:, part:], ub_ref[...]) + bias_ref[...]
    cdf = 0.5 + 0.5 * lax.erf(pre * (2.0**-0.5))
    act = low(pre * cdf)
    act_ref[...] = act
    slope = cdf + pre * (jnp.exp2(pre * pre * (-0.5 * LOG2E)) * 0.3989422804014327)
    grad = dot(dy[:, :part], da_ref[...], 1, 1) + dot(dy[:, part:], db_ref[...], 1, 1)
    dpre = low(grad * slope)
    pre_ref[...] = dpre
    to = slice(TILE, 2 * TILE) if last else slice(0, TILE)
    for n, (ref, down) in enumerate(((keep_ref, down_keep), (send_ref, down_send))):

        @pl.when(g == n)
        def _(n=n, ref=ref, down=down):
            ref[:, :part] = low(dot(dpre, ua_ref[...], 1, 1))
            ref[:, part:] = low(dot(dpre, ub_ref[...], 1, 1))
            if last:
                down[:TILE] = done[n][...]
            down[to, :part] = low(dot(act, da_ref[...]))
            down[to, part:] = low(dot(act, db_ref[...]))


def mlp(scalars, first, stride, own, other, dy, ua, ub, da, db, bias, done):
    width, units = own.shape[1], ua.shape[1]
    tile = lambda n: pl.BlockSpec((TILE, n), lambda i, sc: (i, 0))
    fixed = lambda n: (shape((n, width), BF), pl.BlockSpec((n, width), lambda i, sc: (0, 0)))
    size = 2 * TILE if done else TILE
    weights = [ua, ub, da, db, bias, *done]
    return call(
        functools.partial(mlp_kernel, len(done) > 0), "mlp", scalars, (2,),
        [whole(own), whole(other), row_block(dy, lambda i, sc: first + stride * i)] + [whole(v) for v in weights],
        [fixed(TILE)] * 2 + [(shape((2 * TILE, units), BF), tile(units))] * 2 + [fixed(size)] * 2,
        [pltpu.VMEM((TILE, width), BF)], [own, other, dy, *weights], 8 * 2 * TILE * width * units, 8_000_000,
    )


def share_kernel(blocks, final, tiles, sc_ref, *refs):
    refs = list(refs)
    take = lambda n: [refs.pop(0) for _ in range(n)]
    dqs, outs, dzs, before = (take(2), take(2), take(4), take(2)) if final else ([], [], [], [])
    dks, dvs, norms = take(2), take(2), take(blocks)
    wa_ref, wb_ref = take(2)
    shares_out = take(2 * blocks)
    own_ref, other_ref, sums, rows_ref = take(4) if final else take(2) + [None, None]
    w_s, a_s = take(2)
    t_s, q_s, o_s, z_s = take(4) if final else [own_ref, None, None, None]
    sums = sums if final else other_ref
    j = pl.program_id(0)
    local = dks[0].shape[1]
    part = wa_ref.shape[0]
    kinds = 3 if final else 2
    skip = 3 - kinds
    lead = 2 if final else 0

    @pl.when(j == 0)
    def _():
        if final:
            t_s[: lead * local] = jnp.zeros_like(t_s[: lead * local])
            t_s[lead * local :] = before[0][...]
            sums[...] = before[1][...]
            rows_ref[...] = jnp.zeros_like(rows_ref)
        else:
            t_s[...] = jnp.zeros_like(t_s)
            sums[...] = jnp.zeros_like(sums)
        for n in range(kinds):
            cols = slice((n + skip) * local, (n + skip + 1) * local)
            w_s[n, :part] = wa_ref[:, cols]
            w_s[n, part:] = wb_ref[:, cols]

    for b in range(blocks):

        @pl.when((j >= b * tiles) & (j < (b + 1) * tiles))
        def _(b=b):
            a_s[...] = norms[b][...]

    a = a_s[...]
    parts = []
    if final:
        for n in range(4):

            @pl.when(j == n)
            def _(n=n):
                q_s[...] = dqs[n % 2][...]
                o_s[...] = outs[n % 2][...]
                z_s[...] = dzs[(n % 2) * 2 + n // 2][...]

        parts.append(q_s[...])
        z = z_s[...]
        t_s[:local] += dot(o_s[...], z, 0, 0)
        rows_ref[0:1, :] += jnp.sum(wide(z), axis=0, keepdims=True)
    total = lambda group: low(sum(wide(r[...]) for r in group))
    parts += [total(dks), total(dvs)]
    share = low(sum(dot(p, w_s[n], 1, 1) for n, p in enumerate(parts)))
    half = tiles // 2
    for n, ref in enumerate(shares_out):

        @pl.when((j >= n * half) & (j < (n + 1) * half))
        def _(ref=ref):
            ref[...] = share

    for n, p in enumerate(parts):
        at = (n + (1 if final else 0)) * local
        t_s[at : at + local] += dot(p, a, 0, 0)
        sums[n + skip : n + skip + 1, :] += jnp.sum(wide(p), axis=0, keepdims=True)

    if final:

        @pl.when(j == pl.num_programs(0) - 1)
        def _():
            own_ref[...] = t_s[:, :part].T
            other_ref[...] = low(t_s[:, part:].T)


def shares(scalars, start, dqs, outs, dzs, before, dks, dvs, norms, wa, wb):
    rows, width = norms[0].shape
    local = dks[0].shape[1]
    part = wa.shape[0]
    tiles, blocks, final = rows // TILE, len(norms), len(dqs) > 0
    kinds = 3 if final else 2
    fixed = lambda dims: pl.BlockSpec(dims, lambda i, sc: (0,) * len(dims))
    ins = [row_block(v, lambda i, sc: i // 2) for v in dqs + outs] + [whole(v) for v in dzs + before]
    ins += [row_block(v, lambda i, sc: i + start) for v in dks + dvs]
    ins += [row_block(v, lambda i, sc, b=b: jnp.clip(i - b * tiles, 0, tiles - 1)) for b, v in enumerate(norms)]
    ins += [whole(wa), whole(wb)]
    half = tiles // 2
    results = [
        (shape((rows // 2, width), BF), pl.BlockSpec((TILE, width), lambda i, sc, n=n: (jnp.clip(i - n * half, 0, half - 1), 0)))
        for n in range(2 * blocks)
    ]
    scratch = [pltpu.VMEM((kinds, width, local), BF), pltpu.VMEM((TILE, width), BF)]
    if final:
        results += [(shape((part, 4 * local), F32), fixed((part, 4 * local))), (shape((part, 4 * local), BF), fixed((part, 4 * local)))]
        results += [(shape((8, local), F32), fixed((8, local))), (shape((8, width), F32), fixed((8, width)))]
        scratch += [pltpu.VMEM((4 * local, width), F32), pltpu.VMEM((TILE, local), BF), pltpu.VMEM((TILE, local), BF), pltpu.VMEM((TILE, width), BF)]
    else:
        results += [(shape((2 * local, width), F32), fixed((2 * local, width))), (shape((8, local), F32), fixed((8, local)))]
    return call(
        functools.partial(share_kernel, blocks, final, tiles), "share" if final else "share_seen", scalars, (blocks * tiles,), ins, results, scratch,
        [in_hbm(v) if final else v for v in dqs + outs + dzs + before + dks + dvs + norms] + [wa, wb], 4 * blocks * rows * width * local * kinds, 8_000_000, 32,
    )


def place_kernel(pieces, which, sc_ref, *refs):
    out_ref, x_s = refs[pieces], refs[pieces + 1]
    j = pl.program_id(0)
    f = sc_ref[5]
    part = out_ref.shape[1] // 2
    for n in range(pieces):

        @pl.when(j == n)
        def _(n=n):
            x_s[...] = refs[n][...].astype(x_s.dtype)

    out_ref[:, pl.ds(pl.multiple_of(f * part, 128), part)] = x_s[:, :part]
    out_ref[:, pl.ds(pl.multiple_of((1 - f) * part, 128), part)] = x_s[:, part:]


def placed(scalars, which, pieces, kind):
    width = pieces[0][0].shape[1]
    ins = [pl.BlockSpec((TILE, width), lambda i, sc, n=n: (n, 0)) for _, n in pieces]
    rows = TILE * len(pieces)
    return call(
        functools.partial(place_kernel, len(pieces), which), "placed", scalars, (len(pieces),), ins,
        [(shape((rows, width), kind), pl.BlockSpec((TILE, width), lambda i, sc: (i ^ sc[which], 0)))],
        [pltpu.VMEM((TILE, width), kind)], [v for v, _ in pieces], 0, 6_000_000,
    )[0]


def pack_kernel(n, *refs):
    out_ref, row_s = refs[-2], refs[-1]
    row_s[...] = jnp.zeros_like(row_s)
    for k in range(n):
        row_s[k : k + 1, :] = wide(refs[k][...])
    top = n
    for ref in refs[n:-2]:
        row_s[top : top + ref.shape[0], : ref.shape[1]] = wide(ref[...])
        top += ref.shape[0]
    out_ref[...] = low(row_s[...])


def packed(vectors, folds):
    part = vectors[0].shape[0]
    args = [v.reshape(1, part) for v in vectors] + [v.reshape(-1, v.shape[-1]) for v in folds]
    rows = len(vectors) + sum(v.shape[0] for v in args[len(vectors) :])
    rows += -rows % 16
    return pl.pallas_call(
        functools.partial(pack_kernel, len(vectors)), name="packed", out_shape=shape((rows, part), BF),
        scratch_shapes=[pltpu.VMEM((rows, part), F32)],
        compiler_params=pltpu.CompilerParams(vmem_limit_bytes=8 << 20),
        cost_estimate=pl.CostEstimate(flops=0, bytes_accessed=100_000, transcendentals=0),
    )(*args)


def unpack_kernel(sizes, sc_ref, a_ref, b_ref, vec_ref, qkv_ref, up_ref):
    f = sc_ref[5]
    a, b = wide(a_ref[...]), wide(b_ref[...])
    lo, hi = jnp.where(f == 0, a, b), jnp.where(f == 0, b, a)
    part = a.shape[1]
    n = 6
    vec_ref[0:2, :part], vec_ref[0:2, part:] = lo[0:2], hi[0:2]
    vec_ref[2:8, :part], vec_ref[2:8, part:] = a[0:6], b[0:6]
    lanes = HD // 2
    for ref, start, count in ((qkv_ref, n, sizes[0]), (up_ref, n + sizes[0], sizes[1])):
        ref[...] = jnp.concatenate([p[start + k : start + k + 1, :lanes] for k in range(count) for p in (lo, hi)], axis=1)


def unpacked(scalars, a, b, sizes):
    outs = [shape((8, 2 * a.shape[1]), F32), shape((1, sizes[0] * HD), F32), shape((1, sizes[1] * HD), F32)]
    fixed = [(o, pl.BlockSpec(o.shape, lambda i, sc: (0, 0))) for o in outs]
    return call(functools.partial(unpack_kernel, sizes), "unpacked", scalars, (1,), [whole(a), whole(b)], fixed, [], [a, b], 0, 100_000, 8)


def weights_kernel(pieces, order, sc_ref, *refs):
    refs = list(refs)
    a_refs = [refs.pop(0) for _ in range(pieces)]
    dy_ref = refs.pop(0)
    pre_refs, act_refs = [refs.pop(0) for _ in range(2)], [refs.pop(0) for _ in range(2)]
    own_up, other_up, own_down, other_down, sum_ref, a_s, d_s, p_s, c_s = refs
    j = pl.program_id(0)

    @pl.when(j == 0)
    def _():
        for n in range(pieces):
            to = slice(n * TILE, (n + 1) * TILE)
            a_s[to, :] = a_refs[n][...]
            d_s[to, :] = dy_ref[order[n] * TILE : (order[n] + 1) * TILE, :]
        for n in range(2):
            to = slice(n * 2 * TILE, (n + 1) * 2 * TILE)
            p_s[to, :] = pre_refs[n][...]
            c_s[to, :] = act_refs[n][...]
        sum_ref[...] = jnp.zeros_like(sum_ref)
        sum_ref[0:1, :] = jnp.sum(wide(p_s[...]), axis=0, keepdims=True)
        sum_ref[1:2, :] = jnp.sum(wide(d_s[...]), axis=0, keepdims=True)

    part = own_up.shape[0]
    cols = pl.ds(pl.multiple_of((1 - j) * part, 128), part)
    up = dot(a_s[:, cols], p_s[...], 0, 0)
    down = dot(c_s[...], d_s[:, cols], 0, 0)

    @pl.when(j == 0)
    def _():
        other_up[...] = low(up)
        other_down[...] = low(down)

    @pl.when(j == 1)
    def _():
        own_up[...] = up
        own_down[...] = down


def mlp_weights(scalars, twos, dy, order, pres, acts):
    rows, width = dy.shape
    units = pres[0].shape[1]
    part = width // 2
    outs = [shape(dims, kind) for dims in ((part, units), (units, part)) for kind in (F32, BF)] + [shape((8, max(width, units)), F32)]
    fixed = [(o, pl.BlockSpec(o.shape, lambda i, sc: (0, 0))) for o in outs]
    args = [in_hbm(v) for v in twos + [dy] + pres + acts]
    scratch = [pltpu.VMEM((rows, n), BF) for n in (width, width, units, units)]
    return call(
        functools.partial(weights_kernel, len(twos), order), "mlp_weights", scalars, (2,), [whole(v) for v in args], fixed, scratch, args,
        4 * rows * width * units, 12_000_000, 40,
    )


PAIR = [(0, 1), (1, 0)]


def swap_core(values):
    return lax.ppermute(values, "tp", [(i, i ^ 1) for i in range(4)])


def swap_y(values):
    return lax.ppermute(values, "tp", [(i, i ^ 2) for i in range(4)])


def hop(values, pairs):
    return lax.ppermute(values, "ctx", pairs)


def after(values, *deps):
    return lax.optimization_barrier((values, *deps))[0]


def pick(parts, index):
    return lax.dynamic_index_in_dim(parts, index, 0, keepdims=False)


def ordered(first, second, flip):
    return jnp.where(flip == 0, jnp.stack([first, second]), jnp.stack([second, first]))


def body(
    hidden,
    prefix,
    w_qkv,
    b_qkv,
    w_out,
    b_out,
    w_up,
    b_up,
    w_down,
    b_down,
    ln1_gain,
    ln1_shift,
    ln2_gain,
    ln2_shift,
    cotangent,
):
    members = lax.axis_size("fsdp")
    paired = members == 2
    z = lax.axis_index("ctx")
    t = lax.axis_index("tp")
    half_ctx = lax.axis_size("ctx") // 2
    core, side = t & 1, t >> 1
    turn_q, turn_k = 2 * core, 2 * core + side
    f = lax.axis_index("fsdp") if paired else jnp.int32(0)
    rows, width = hidden.shape[1], hidden.shape[2]
    local, units = w_qkv.shape[2], w_up.shape[1]
    half, quarter, part = rows // 2, rows // 4, width // 2
    tiles = rows // TILE
    scalars = jnp.stack([z, turn_q, turn_k, prefix[0], jnp.int32(half_ctx), f]).astype(jnp.int32)

    def both(values, axis):
        if paired:
            return values, lax.ppermute(values, "fsdp", PAIR)
        return tuple(jnp.split(lax.all_gather(values, "fsdp", axis=axis, tiled=True), 2, axis=axis))

    qkv_own = w_qkv.reshape(w_qkv.shape[0], 3 * local)
    qkv_a, qkv_b = both(qkv_own, 0)
    own_quarter = lax.dynamic_slice(hidden[0], (turn_k * quarter, 0), (quarter, width))
    first = hop(own_quarter, [(2, 1), (3, 2)])
    aside = hop(own_quarter, [(2, 3)])

    def spread(values, *deps):
        other = swap_y(values)
        ours = after((values, other), *deps)
        return [(v, 0) for v in (values, other, swap_core(ours[0]), swap_core(ours[1]))]

    vectors_in = (ln1_gain, ln1_shift, b_out, ln2_gain, ln2_shift, b_down)
    fold_rows = (b_qkv.size // b_qkv.shape[-1], b_up.shape[0])
    if paired:
        small = packed(vectors_in, (b_qkv, b_up))
        small_b = lax.ppermute(after(small, qkv_b), "fsdp", PAIR)
        vec, bias_qkv, bias_up = unpacked(scalars, small, small_b, fold_rows)
    else:
        small_b = qkv_b
        gather = lambda v: wide(lax.all_gather(v, "fsdp", axis=v.ndim - 1, tiled=True))
        found = [gather(v) for v in vectors_in]
        vec = jnp.stack(found[:2] + found)
        bias_qkv, bias_up = gather(b_qkv).reshape(1, -1), gather(b_up).reshape(1, -1)
    gain_one, shift_one, gain_two, shift_two, bias_down = vec[2], vec[3], vec[5], vec[6], vec[7]
    far_quarter = first + aside
    second = hop(after(first, qkv_b), [(1, 0), (2, 1)])
    far_pieces = spread(far_quarter)
    later = after((w_out, w_up, w_down), small_b)
    out_a, out_b = both(later[0], 1)
    up_a, up_b = both(later[1], 0)
    down_a, down_b = both(after(later[2], out_b), 1)

    lane = jnp.arange(local, dtype=jnp.int32) % (HD // 2)
    frequency = jnp.power(jnp.float32(10000.0), -2.0 * wide(lane) / HD)[None, :]
    base = wide(jnp.arange(TILE, dtype=jnp.int32))[:, None] * frequency
    turns = wide(jnp.arange(half_ctx * tiles, dtype=jnp.int32) * TILE)[:, None] * frequency
    base, turns = jnp.stack([jnp.cos(base), jnp.sin(base)]), jnp.stack([jnp.cos(turns), jnp.sin(turns)])

    q, k_own, v_own, norm_own, x_turned, dy = project(
        scalars, [hidden[0]], cotangent[0], False, rows, vec, qkv_a, qkv_b, bias_qkv, base, turns
    )
    near_quarter = jnp.where(z >= half_ctx, own_quarter, after(second, q))
    k_far, v_far, norm_far = project(scalars, far_pieces, None, True, rows, vec, qkv_a, qkv_b, after(bias_qkv, q, up_b), base, turns)
    near_pieces = spread(after(near_quarter, far_pieces[1][0]), k_far)
    k_near, v_near, norm_near = project(scalars, near_pieces, None, False, rows, vec, qkv_a, qkv_b, after(bias_qkv, k_far, out_b, down_b), base, turns)
    keys, values = [k_own, k_near, k_far], [v_own, v_near, v_far]

    def core_sum(kept, sent):
        return low(wide(kept) + wide(swap_core(sent)))

    o0, lse0, *share = attention(scalars, 0, 2, q, keys, values, out_a, out_b)
    mine0 = core_sum(*share)
    o1, lse1, *share = attention(scalars, 1, 2, after(q, mine0, up_b), keys, values, out_a, out_b)
    mine1 = core_sum(*share)
    mid0, two0 = norm_two(scalars, 0, x_turned, mine0, swap_y(mine0), vec)
    twos0 = (two0, swap_core(two0))
    *share, act0, pre0, down_keep, down_send = mlp(scalars, 0, 2, after(twos0[0], mine1), twos0[1], dy, up_a, up_b, down_a, down_b, bias_up, [])
    back0 = core_sum(*share)
    mid1, two1 = norm_two(scalars, 1, x_turned, mine1, swap_y(mine1), vec)
    twos1 = (two1, swap_core(two1))
    *share, act1, pre1, down_keep, down_send = mlp(scalars, 1, 2, *twos1, dy, up_a, up_b, down_a, down_b, bias_up, [down_keep, down_send])
    back1 = core_sum(*share)
    back_y0, back_y1 = swap_y(back0), swap_y(back1)

    dmid0, dz0 = norm_two_grad(scalars, 0, dy, mid0, back0, back_y0, vec)
    dzs0 = (dz0, swap_core(dz0))
    act0, act1, pre0, pre1 = after((act0, act1, pre0, pre1), back1, dz0)
    *g_mlp, sums_mlp = mlp_weights(scalars, list(twos0) + list(twos1), dy, (0, 2, 1, 3), [pre0, pre1], [act0, act1])

    def partner_sum(own_part, other_part, dim=0):
        if paired:
            return own_part + wide(lax.ppermute(other_part, "fsdp", PAIR))
        return lax.psum_scatter(jnp.concatenate([own_part, wide(other_part)], axis=dim), "fsdp", scatter_dimension=dim, tiled=True)

    near_bit, far_bit = z & 1, z >> 1
    near_pairs, far_pairs = [(i, i ^ 1) for i in range(4)], [(i, i ^ 2) for i in range(4)]

    def split(values, bit):
        grid = values.reshape(2, values.shape[0] // 2, values.shape[1])
        return pick(grid, bit), low(pick(grid, 1 - bit))

    def join(values, sent, pairs, bit):
        return ordered(values, hop(sent, pairs), bit).reshape(2 * values.shape[0], values.shape[1])

    down = core_sum(down_keep, after(down_send, dz0))
    dmid1, dz1 = norm_two_grad(scalars, 1, dy, mid1, back1, back_y1, vec)
    dzs1 = (dz1, swap_core(dz1))
    dq0, dk0, dv0 = attention_grads(scalars, 0, 2, after(q, g_mlp[1], down), o0, *dzs0, lse0, keys, values, out_a, out_b, base, turns)
    down_y = swap_y(down)
    up_sum = partner_sum(after(g_mlp[0], dk0), g_mlp[1])
    up_keep, up_send = split(up_sum, near_bit)
    dq1, dk1, dv1 = attention_grads(scalars, 1, 2, after(q, dk0, up_send, down_y), o1, *dzs1, lse1, keys, values, out_a, out_b, base, turns)
    up_half = after(up_keep, dk1) + wide(hop(up_send, near_pairs))
    up_keep, up_send = split(up_half, far_bit)
    down_sum = partner_sum(after(g_mlp[2], dk1), after(g_mlp[3], up_sum), 1)
    down_part, down_send = split(down_sum, near_bit)
    result_half = low(jnp.concatenate([after(mid0, dk1), mid1], axis=0) + (wide(down) + wide(down_y)) + bias_down)
    other = swap_core(result_half)
    dk1 = after(dk1, up_send, down_send, result_half)
    result = placed(scalars, 1, [(result_half, 0), (result_half, 1), (other, 0), (other, 1)], BF)

    dks, dvs = [dk0, dk1], [dv0, dv1]
    *seen, t_seen, sums_seen = shares(scalars, tiles, [], [], [], [], dks, dvs, [norm_near, norm_far], qkv_a, qkv_b)
    def core_halves(kept, sent):
        got = swap_core(sent)
        return [low(wide(kept[n : n + quarter]) + wide(got[n : n + quarter])) for n in (0, quarter)]

    near_got, far_got = swap_core(seen[1]), swap_core(seen[3])
    seen_pairs = ((seen[0], near_got), (seen[2], far_got))
    near_keep, far_keep = (low(wide(k[:quarter]) + wide(g[:quarter])) for k, g in seen_pairs)
    seen_send = low(jnp.concatenate([wide(k[quarter:]) + wide(g[quarter:]) for k, g in seen_pairs], axis=0))
    seen_y = swap_y(seen_send)
    *share_own, g_two, g_two_other, sums, sums_out = shares(
        scalars, 0, after([dq0, dq1], seen_send), [o0, o1], [*dzs0, *dzs1], [t_seen, sums_seen], dks, dvs, [norm_own], qkv_a, qkv_b
    )
    near_q = low(wide(after(near_keep, g_two_other)) + wide(seen_y[:quarter]))
    up_quarter = low(after(up_keep, near_q) + wide(hop(up_send, far_pairs)))
    down_half = after(down_part, near_q) + wide(hop(down_send, near_pairs))
    down_part, down_send = split(down_half, far_bit)
    near_in = hop(near_q, [(0, 1), (1, 3)])
    two_sum = partner_sum(after(g_two, near_in), g_two_other)
    far_q = wide(after(far_keep, two_sum)) + wide(seen_y[quarter:])
    far_q = low(far_q + jnp.where(z == 1, wide(near_in), 0.0))
    far_in = wide(hop(far_q, [(1, 2)])) + wide(hop(far_q, [(3, 2)]))
    own_low, own_high = core_halves(*share_own)
    own_send = jnp.where(side == 0, own_high, own_low)
    da_one = wide(jnp.where(side == 0, own_low, own_high)) + wide(swap_y(after(own_send, far_q)))
    da_one = da_one + far_in + jnp.where(z >= half_ctx, wide(near_q) + jnp.where(z == 3, wide(near_in), 0.0), 0.0)
    x_q = wide(lax.dynamic_slice(x_turned, (side * quarter, 0), (quarter, width)))
    grad_q = low(jnp.where(side == 0, dmid0, dmid1) + norm_back(da_one, x_q, gain_one))
    grad_y = swap_y(grad_q)
    grad_input = placed(scalars, 2, [(v, 0) for v in (grad_q, grad_y, swap_core(grad_q), swap_core(grad_y))], F32)

    up_half = join(up_quarter, up_quarter, far_pairs, far_bit)
    up_total = wide(join(up_half, after(up_half, near_q), near_pairs, near_bit))
    down_quarter = low(down_part + wide(hop(down_send, far_pairs)))
    down_half = join(down_quarter, after(down_quarter, near_q), far_pairs, far_bit)
    down_total = wide(join(down_half, after(down_half, far_q), near_pairs, near_bit))
    two_keep, two_send = split(two_sum, near_bit)
    two_half = two_keep + wide(hop(two_send, near_pairs))
    two_keep, two_send = split(two_half, far_bit)
    two_quarter = low(two_keep + wide(hop(two_send, far_pairs)))
    two_back = join(two_quarter, two_quarter, far_pairs, far_bit)
    second_group = wide(join(two_back, two_back, near_pairs, near_bit))

    def gain_grad(weights, grad, bias_grad, gain, shift):
        full = wide(jnp.concatenate(weights, axis=0))
        by_shift = jnp.sum(full * bias_grad[None, :], axis=1)
        return (jnp.sum(full * grad, axis=1) - shift * by_shift) / gain, by_shift

    g_own, g_two, sums_mlp, sums, sums_out = after((g_mlp[0], g_two, sums_mlp, sums, sums_out), two_half)
    joined = lambda own, other, cols: jnp.concatenate([own[:, cols], wide(other[:, cols])], axis=0)
    gb_up, gb_down, gb_out, gb_qkv = sums_mlp[0], sums_mlp[1] * 0.25, sums_out[0] * 0.25, sums[:3].reshape(-1)
    g_gain_one, g_shift_one = gain_grad((qkv_a, qkv_b), joined(g_two, g_two_other, slice(local, None)), gb_qkv, gain_one, shift_one)
    g_gain_two, g_shift_two = gain_grad((up_a, up_b), joined(g_own, g_mlp[1], slice(None)), gb_up, gain_two, shift_two)
    over_tp = after(jnp.stack([gb_out, gb_down, g_gain_one, g_shift_one, g_gain_two, g_shift_two]), near_q)
    over_tp = over_tp + swap_core(over_tp)
    over_tp = over_tp + swap_y(over_tp)
    if paired:
        take = lambda v, n: lax.dynamic_index_in_dim(v.reshape(-1, 2, HD // 2), n, 1, keepdims=False).reshape(-1)
        mine = jnp.concatenate([over_tp[:, :part].reshape(-1), take(gb_qkv, f), take(gb_up, f)])
        other = jnp.concatenate([over_tp[:, part:].reshape(-1), take(gb_qkv, 1 - f), take(gb_up, 1 - f)])
        vectors = mine + lax.ppermute(other, "fsdp", PAIR)
    else:
        scattered = [
            lax.psum_scatter(v, "fsdp", scatter_dimension=1, tiled=True).reshape(-1)
            for v in (over_tp, gb_qkv.reshape(-1, HD), gb_up.reshape(-1, HD))
        ]
        vectors = jnp.concatenate(scattered)
    vectors = vectors + hop(vectors, [(i, i ^ 1) for i in range(4)])
    vectors = vectors + hop(vectors, [(i, i ^ 2) for i in range(4)])
    own = width // members
    named = vectors[: 6 * own].reshape(6, own)
    cut = 6 * own + b_qkv.size
    return (
        result[None],
        grad_input[None],
        second_group[:, local:].reshape(w_qkv.shape),
        vectors[6 * own : cut].reshape(b_qkv.shape),
        second_group[:, :local].T,
        named[0],
        up_total,
        vectors[cut:].reshape(b_up.shape),
        down_total,
        named[1],
        named[2],
        named[3],
        named[4],
        named[5],
    )


def solution(mesh):
    rows = P("fsdp", "ctx", None)
    weights = (P("fsdp", None, "tp"), P(None, "tp", "fsdp"), P("tp", "fsdp"), P("fsdp"), P("fsdp", "tp"), P("tp", "fsdp"), P("tp", "fsdp"))
    vectors = (P("fsdp"),) * 5
    return jax.shard_map(
        body,
        mesh=mesh,
        in_specs=(rows, P("fsdp")) + weights + vectors + (rows,),
        out_specs=(rows, rows) + weights + vectors,
        check_vma=False,
    )
```

```python
import functools
import jax
import jax.numpy as jnp
from jax import lax
from jax.experimental import pallas as pl
from jax.experimental.pallas import tpu as pltpu
from jax.sharding import PartitionSpec as P

HD = 64
BLOCK = 16
TILE = 256
WIDE = 512
LOG2E = 1.4426950408889634
NEG = -1e30
epsilon = 1e-05
BF, F32 = jnp.bfloat16, jnp.float32


def low(values):
    return values.astype(BF)


def wide(values):
    return values.astype(F32)


def dot(a, b, ca=1, cb=0):
    return lax.dot_general(a, b, (((ca,), (cb,)), ((), ())), preferred_element_type=F32)


def shape(dims, kind):
    return jax.ShapeDtypeStruct(dims, kind)


def in_hbm(values):
    return pltpu.with_memory_space_constraint(values, pltpu.HBM) if values.size >= 65536 else values


def call(kernel, name, scalars, grid, ins, outs, scratch, args, flops, moved, room=24):
    return pl.pallas_call(
        kernel,
        name=name,
        out_shape=[s for s, _ in outs],
        grid_spec=pltpu.PrefetchScalarGridSpec(
            num_scalar_prefetch=1, grid=grid, in_specs=ins, out_specs=[b for _, b in outs], scratch_shapes=scratch
        ),
        compiler_params=pltpu.CompilerParams(dimension_semantics=("arbitrary",) * len(grid), vmem_limit_bytes=room << 20),
        cost_estimate=pl.CostEstimate(flops=flops, bytes_accessed=moved, transcendentals=0),
    )(scalars, *args)


def whole(values):
    dims = values.shape
    return pl.BlockSpec(dims, lambda i, sc: (0,) * len(dims))


def row_block(values, index):
    return pl.BlockSpec((TILE, values.shape[1]), lambda i, sc: (index(i, sc), 0))


def turn_matrix(width):
    k = lax.broadcasted_iota(jnp.int32, (width, width), 0)
    n = lax.broadcasted_iota(jnp.int32, (width, width), 1)
    first = (n & (HD - 1)) < HD // 2
    return jnp.where(first & (k == n + HD // 2), -1.0, jnp.where((~first) & (k == n - HD // 2), 1.0, 0.0)).astype(BF)


def tile_angles(base_ref, tile_ref, index):
    cos, sin = base_ref[0], base_ref[1]
    cos_t, sin_t = tile_ref[0, pl.ds(index, 1), :], tile_ref[1, pl.ds(index, 1), :]
    return cos * cos_t - sin * sin_t, sin * cos_t + cos * sin_t


def unit_rows(x):
    mean = jnp.mean(x, axis=-1, keepdims=True)
    centered = x - mean
    variance = jnp.mean(centered * centered, axis=-1, keepdims=True)
    scale = lax.rsqrt(variance + epsilon)
    return centered * scale, scale


def project_kernel(parts, with_q, far, tiles, sc_ref, *refs):
    refs = list(refs)
    xs = [refs.pop(0) for _ in range(parts)]
    dy_ref = refs.pop(0) if with_q else None
    vec_ref, wa_ref, wb_ref, bias_ref, base_ref, tile_ref = [refs.pop(0) for _ in range(6)]
    outs = [refs.pop(0) for _ in range(3 if with_q else 2)]
    norm_ref = refs.pop(0)
    if with_q:
        keep_ref, dy_out = refs.pop(0), refs.pop(0)
    w_s, r_s, b_s, x_s, a_s = refs
    j = pl.program_id(0)
    f = sc_ref[5]
    local = outs[0].shape[1]
    part = wa_ref.shape[0]
    skip = 0 if with_q else 1
    count = len(outs)

    @pl.when(j == 0)
    def _():
        turn = turn_matrix(local)
        for n in range(count):
            cols = slice((n + skip) * local, (n + skip + 1) * local)
            w_s[n, :part] = wa_ref[:, cols]
            w_s[n, part:] = wb_ref[:, cols]
            if n < count - 1:
                r_s[n] = low(dot(w_s[n], turn))
                b_s[n] = dot(jnp.broadcast_to(bias_ref[:, cols], (8, local)).astype(BF), turn)

    if parts == 1:
        x = wide(xs[0][...])
    else:
        for n in range(parts):

            @pl.when(j == n)
            def _(n=n):
                x_s[...] = xs[n][...]

        x = wide(x_s[...])
    unit, _ = unit_rows(x)
    a_s[...] = unit * vec_ref[0:1] + vec_ref[1:2]
    first = pl.ds(pl.multiple_of(f * part, 128), part)
    second = pl.ds(pl.multiple_of((1 - f) * part, 128), part)
    a = jnp.concatenate([low(a_s[:, first]), low(a_s[:, second])], axis=1)
    norm_ref[...] = a
    if with_q:
        keep_ref[:, :part] = xs[0][:, first]
        keep_ref[:, part:] = xs[0][:, second]
        dy_out[:, :part] = dy_ref[:, first]
        dy_out[:, part:] = dy_ref[:, second]
    at = j ^ sc_ref[1 if with_q else 2]
    cos, sin = tile_angles(base_ref, tile_ref, at if far else at + lax.rem(sc_ref[0], sc_ref[4]) * tiles)
    for n in range(count):
        cols = slice((n + skip) * local, (n + skip + 1) * local)
        u = dot(a, w_s[n]) + bias_ref[:, cols]
        if n < count - 1:
            u = u * cos + (dot(a, r_s[n]) + b_s[n, 0:1]) * sin
        u = low(u)
        if n == 0 and with_q:
            u = u * jnp.asarray(HD**-0.5, BF)
        outs[n][...] = u


def project(scalars, xs, dy, far, rows, vec, wa, wb, bias, base, turns):
    with_q = dy is not None
    width = wa.shape[0] * 2
    local = wa.shape[1] // 3
    tiles = rows // TILE
    if with_q:
        turned = lambda i, sc: i ^ sc[1]
        ins = [row_block(xs[0], turned), row_block(dy, turned)]
        args = [xs[0], dy]
        parts = 1
    else:
        ins = [pl.BlockSpec((TILE, width), lambda i, sc, n=n: (n, 0)) for _, n in xs]
        args = [v for v, _ in xs]
        parts = len(xs)
    ins += [whole(v) for v in (vec, wa, wb, bias, base, turns)]
    args += [vec, wa, wb, bias, base, turns]
    tile = lambda n: pl.BlockSpec((TILE, n), lambda i, sc: (i, 0))
    count = 3 if with_q else 2
    outs = [(shape((rows, local), BF), tile(local))] * count + [(shape((rows, width), BF), tile(width))] * (3 if with_q else 1)
    scratch = [
        pltpu.VMEM((count, width, local), BF),
        pltpu.VMEM((count - 1, width, local), BF),
        pltpu.VMEM((count - 1, 8, local), F32),
        pltpu.VMEM((TILE, width), BF),
        pltpu.VMEM((TILE, width), F32),
    ]
    return call(
        functools.partial(project_kernel, parts, with_q, far, tiles), "project" if with_q else "project_seen", scalars, (tiles,), ins, outs, scratch, args,
        2 * rows * width * local * 5, 8_000_000,
    )


def stack_heads(rows, heads):
    lane = lax.broadcasted_iota(jnp.int32, rows.shape, 1) // HD
    return jnp.concatenate([jnp.where(lane == h, rows, jnp.zeros_like(rows)) for h in range(heads)], axis=0)


def tile_plan(sc_ref, tile, tiles):
    z, prefix, half = sc_ref[0], sc_ref[3], sc_ref[4]
    noisy = z < half
    late = lax.rem(z, half)
    at = tile ^ sc_ref[1]
    prefix = jnp.where(late == 0, prefix, 0)
    top = jnp.maximum(at + 1, (prefix + TILE - 1) // TILE)
    return noisy, late == 1, at, top, prefix


def near_rows(sc_ref, t):
    return pl.ds(pl.multiple_of((t ^ sc_ref[2]) * TILE, TILE), TILE)


def edge_mask(block_gap, k_pos, t, at, noisy, prefix):
    limit = (at - t) * (TILE // BLOCK) + jnp.where(noisy, 0, 1)
    return (block_gap < limit) | (k_pos < prefix - t * TILE)


def fwd_kernel(first, stride, tiles, sc_ref, q_ref, ko_ref, vo_ref, km_ref, vm_ref, kf_ref, vf_ref, wa_ref, wb_ref, o_ref, lse_ref, keep_ref, send_ref, sbuf, mbuf, lbuf, acc):
    tile = first + stride * pl.program_id(0)
    noisy, late, at, top, prefix = tile_plan(sc_ref, tile, tiles)
    width = q_ref.shape[1]
    heads = width // HD
    qs = stack_heads(q_ref[...], heads)
    mbuf[...] = jnp.full_like(mbuf, NEG)
    lbuf[...] = jnp.zeros_like(lbuf)
    acc[...] = jnp.zeros_like(acc)
    high = heads * TILE
    own = pl.ds(pl.multiple_of(tile * TILE, TILE), TILE)

    def keep(slot, s):
        best = mbuf[...]
        for n in range(s.shape[1] // TILE):
            sbuf[slot + n] = s[:, n * TILE : (n + 1) * TILE]
        for n in range(s.shape[1] // 128):
            best = jnp.maximum(best, s[:, n * 128 : (n + 1) * 128])
        mbuf[...] = best

    def plain_step(t, carry):
        keep(t, dot(qs, km_ref[near_rows(sc_ref, t), :], 1, 1))
        return carry

    lax.fori_loop(0, at, plain_step, 0)
    wides = tiles * TILE // WIDE

    def far_rows(n):
        return pl.ds(pl.multiple_of(n * WIDE, WIDE), WIDE)

    def far_step(n, carry):
        keep(tiles + n * (WIDE // TILE), dot(qs, kf_ref[far_rows(n), :], 1, 1))
        return carry

    lax.fori_loop(0, jnp.where(late, wides, 0), far_step, 0)
    q_block = (lax.broadcasted_iota(jnp.int32, (high, TILE), 0) & (TILE - 1)) >> 4
    k_pos = lax.broadcasted_iota(jnp.int32, (high, TILE), 1)
    gap = (k_pos >> 4) - q_block

    def edge_step(t, carry):
        s = dot(qs, km_ref[near_rows(sc_ref, t), :], 1, 1)
        keep(t, jnp.where(edge_mask(gap, k_pos, t, at, noisy, prefix), s, NEG))
        return carry

    lax.fori_loop(at, top, edge_step, 0)

    @pl.when(noisy)
    def _():
        keep(2 * tiles, jnp.where(gap == 0, dot(qs, ko_ref[own, :], 1, 1), NEG))

    best = jnp.max(mbuf[...], axis=1, keepdims=True) * LOG2E
    mbuf[...] = jnp.broadcast_to(best, mbuf.shape)

    def add(slot, v):
        m = mbuf[...]
        total = lbuf[...]
        cols = []
        for n in range(v.shape[0] // TILE):
            s = sbuf[slot + n]
            for k in range(TILE // 128):
                p = jnp.exp2(s[:, k * 128 : (k + 1) * 128] * LOG2E - m)
                total = total + p
                cols.append(low(p))
        lbuf[...] = total
        acc[...] += dot(jnp.concatenate(cols, axis=1), v)

    def near_sum(t, carry):
        add(t, vm_ref[near_rows(sc_ref, t), :])
        return carry

    lax.fori_loop(0, top, near_sum, 0)

    def far_sum(n, carry):
        add(tiles + n * (WIDE // TILE), vf_ref[far_rows(n), :])
        return carry

    lax.fori_loop(0, jnp.where(late, wides, 0), far_sum, 0)

    @pl.when(noisy)
    def _():
        add(2 * tiles, vo_ref[own, :])

    norm = jnp.sum(lbuf[...], axis=1, keepdims=True)
    out = acc[...] * (1.0 / norm)
    lane = lax.broadcasted_iota(jnp.int32, (TILE, width), 1) // HD
    picked = out[:TILE]
    for h in range(1, heads):
        picked = jnp.where(lane == h, out[h * TILE : (h + 1) * TILE], picked)
    picked = low(picked)
    o_ref[...] = picked
    lse = jnp.broadcast_to(best + jnp.log2(norm), (high, 128))
    lse_ref[0] = jnp.concatenate(
        [lse[h * TILE : (h + 1) * TILE].T[:1] for h in range(heads)] + [jnp.zeros((8 - heads, TILE), F32)], axis=0
    )
    part = wa_ref.shape[1]
    for n, ref in enumerate((keep_ref, send_ref)):

        @pl.when(pl.program_id(0) == n)
        def _(ref=ref):
            ref[:, :part] = low(dot(picked, wa_ref[...]))
            ref[:, part:] = low(dot(picked, wb_ref[...]))


def attention(scalars, first, stride, q, keys, values, wa, wb):
    rows, width = q.shape
    tiles, heads = rows // TILE, width // HD
    count = tiles // stride
    flat = [v for pair in zip(keys, values) for v in pair]
    tile = lambda n: pl.BlockSpec((TILE, n), lambda i, sc: (i, 0))
    full = 2 * wa.shape[1]
    return call(
        functools.partial(fwd_kernel, first, stride, tiles), "attn_fwd", scalars, (count,),
        [row_block(q, lambda i, sc: first + stride * i)] + [whole(v) for v in flat + [wa, wb]],
        [
            (shape((count * TILE, width), BF), tile(width)),
            (shape((count, 8, TILE), F32), pl.BlockSpec((1, 8, TILE), lambda i, sc: (i, 0, 0))),
        ]
        + [(shape((TILE, full), BF), pl.BlockSpec((TILE, full), lambda i, sc: (0, 0)))] * 2,
        [
            pltpu.VMEM((2 * tiles + 1, heads * TILE, TILE), F32),
            pltpu.VMEM((heads * TILE, 128), F32),
            pltpu.VMEM((heads * TILE, 128), F32),
            pltpu.VMEM((heads * TILE, width), F32),
        ],
        [q] + flat + [wa, wb], 3_000_000_000 * count, 4_000_000,
    )


def turn_back(grad, cos, sin, turn):
    moved = grad * sin
    high = low(moved)
    rest = low(moved - wide(high))
    return low(grad * cos - (dot(high, turn) + dot(rest, turn)))


def bwd_kernel(first, stride, tiles, sc_ref, q_ref, o_ref, za_ref, zb_ref, lse_ref, ko_ref, vo_ref, km_ref, vm_ref, kf_ref, vf_ref, wa_ref, wb_ref, base_ref, tile_ref,
               dq_ref, dk_ref, dv_ref, dqt, st, gt, lse_s, del_s, qs_s, gs_s, z_s, dk_s, dv_s):
    g_id = pl.program_id(0)
    tile = first + stride * g_id
    noisy, late, at, top, prefix = tile_plan(sc_ref, tile, tiles)
    width = q_ref.shape[1]
    heads = width // HD
    high = heads * TILE
    part = wa_ref.shape[1]
    rows = tiles * TILE
    per = za_ref.shape[0] // TILE

    @pl.when(g_id == 0)
    def _():
        dk_s[...] = jnp.zeros_like(dk_s)
        dv_s[...] = jnp.zeros_like(dv_s)

    for n in range(2 * per):

        @pl.when(g_id == n)
        def _(n=n):
            z_s[...] = (za_ref if n < per else zb_ref)[(n % per) * TILE : (n % per + 1) * TILE, :]

    z = z_s[...]
    g32 = dot(z[:, :part], wa_ref[...], 1, 1) + dot(z[:, part:], wb_ref[...], 1, 1)
    g = low(g32)
    g32 = wide(g)
    q = q_ref[...]
    qs_s[...] = stack_heads(q, heads)
    gs_s[...] = stack_heads(g, heads)
    q_t = wide(q).T
    g_t = g32.T
    prod = (wide(o_ref[...]) * g32).T
    head_of = lax.broadcasted_iota(jnp.int32, (width, TILE), 0) // HD
    for h in range(heads):
        cols = slice(h * TILE, (h + 1) * TILE)
        st[:, cols] = low(jnp.where(head_of == h, q_t, 0.0))
        gt[:, cols] = low(jnp.where(head_of == h, g_t, 0.0))
        del_s[:, cols] = jnp.sum(prod[h * HD : (h + 1) * HD], axis=0, keepdims=True)
        lse_s[:, cols] = lse_ref[0, h : h + 1, :]
    dqt[...] = jnp.zeros_like(dqt)

    def step(k, v, base, mask):
        n = k.shape[0]
        to = pl.ds(base, n)
        s = dot(k, st[...])
        p = jnp.exp2(s * LOG2E - lse_s[...])
        if mask is not None:
            p = jnp.where(mask, p, 0.0)
        dp = dot(v, gt[...])
        ds = low(p * (dp - del_s[...]))
        p = low(p)
        dv_s[to, :] += dot(p, gs_s[...])
        dk_s[to, :] += dot(ds, qs_s[...])
        dqt[...] += dot(k, ds, 0, 0)

    def near_at(t):
        return pl.multiple_of(rows + (t ^ sc_ref[2]) * TILE, TILE)

    def plain_step(t, carry):
        at_t = near_rows(sc_ref, t)
        step(km_ref[at_t, :], vm_ref[at_t, :], near_at(t), None)
        return carry

    lax.fori_loop(0, at, plain_step, 0)
    wides = rows // WIDE

    def far_step(n, carry):
        at_n = pl.ds(pl.multiple_of(n * WIDE, WIDE), WIDE)
        step(kf_ref[at_n, :], vf_ref[at_n, :], pl.multiple_of(2 * rows + n * WIDE, WIDE), None)
        return carry

    lax.fori_loop(0, jnp.where(late, wides, 0), far_step, 0)
    k_pos = lax.broadcasted_iota(jnp.int32, (TILE, high), 0)
    gap = (k_pos >> 4) - ((lax.broadcasted_iota(jnp.int32, (TILE, high), 1) & (TILE - 1)) >> 4)

    def edge_step(t, carry):
        at_t = near_rows(sc_ref, t)
        step(km_ref[at_t, :], vm_ref[at_t, :], near_at(t), edge_mask(gap, k_pos, t, at, noisy, prefix))
        return carry

    lax.fori_loop(at, top, edge_step, 0)

    @pl.when(noisy)
    def _():
        own = pl.ds(pl.multiple_of(tile * TILE, TILE), TILE)
        step(ko_ref[own, :], vo_ref[own, :], pl.multiple_of(tile * TILE, TILE), gap == 0)

    turn = turn_matrix(width)
    dq_t = jnp.where(head_of == 0, dqt[:, :TILE], 0.0)
    for h in range(1, heads):
        dq_t = jnp.where(head_of == h, dqt[:, h * TILE : (h + 1) * TILE], dq_t)
    late_at = late.astype(jnp.int32) * tiles
    dq_ref[...] = turn_back(dq_t.T * (HD**-0.5), *tile_angles(base_ref, tile_ref, at + late_at), turn)

    @pl.when(g_id == pl.num_programs(0) - 1)
    def _():
        dv_ref[...] = low(dv_s[...])

        def finish(base, true_tile):
            to = pl.ds(pl.multiple_of(base, TILE), TILE)
            dk_ref[to, :] = turn_back(dk_s[to, :], *tile_angles(base_ref, tile_ref, true_tile), turn)

        def all_three(j, carry):
            finish(j * TILE, (j ^ sc_ref[1]) + late_at)
            finish(rows + j * TILE, (j ^ sc_ref[2]) + late_at)
            finish(2 * rows + j * TILE, j ^ sc_ref[2])
            return carry

        lax.fori_loop(0, tiles, all_three, 0)


def attention_grads(scalars, first, stride, q, o, za, zb, lse, keys, values, wa, wb, base, turns):
    rows, width = q.shape
    tiles, heads = rows // TILE, width // HD
    count = tiles // stride
    flat = [v for pair in zip(keys, values) for v in pair]
    tile = pl.BlockSpec((TILE, width), lambda i, sc: (i, 0))
    total = pl.BlockSpec((3 * rows, width), lambda i, sc: (0, 0))
    high = heads * TILE
    return call(
        functools.partial(bwd_kernel, first, stride, tiles), "attn_bwd", scalars, (count,),
        [row_block(q, lambda i, sc: first + stride * i), tile, whole(za), whole(zb), pl.BlockSpec((1, 8, TILE), lambda i, sc: (i, 0, 0))]
        + [whole(v) for v in flat + [wa, wb, base, turns]],
        [(shape((count * TILE, width), BF), tile), (shape((3 * rows, width), BF), total), (shape((3 * rows, width), BF), total)],
        [
            pltpu.VMEM((width, high), F32),
            pltpu.VMEM((width, high), BF),
            pltpu.VMEM((width, high), BF),
            pltpu.VMEM((1, high), F32),
            pltpu.VMEM((1, high), F32),
            pltpu.VMEM((high, width), BF),
            pltpu.VMEM((high, width), BF),
            pltpu.VMEM((TILE, za.shape[1]), BF),
            pltpu.VMEM((3 * rows, width), F32),
            pltpu.VMEM((3 * rows, width), F32),
        ],
        [q, o, za, zb, lse] + flat + [wa, wb, base, turns], 8_000_000_000 * count, 10_000_000,
    )


def norm_kernel(sc_ref, x_ref, mine_ref, theirs_ref, vec_ref, mid_ref, a_ref):
    mid = wide(x_ref[...]) + (wide(mine_ref[...]) + wide(theirs_ref[...])) + vec_ref[4:5]
    mid_ref[...] = mid
    unit, _ = unit_rows(mid)
    a_ref[...] = low(unit * vec_ref[5:6] + vec_ref[6:7])


def norm_two(scalars, index, x, mine, theirs, vec):
    rows, width = mine.shape
    block = pl.BlockSpec((rows, width), lambda i, sc: (0, 0))
    return call(
        norm_kernel, "norm_two", scalars, (1,),
        [row_block(x, lambda i, sc: index), block, block, whole(vec)],
        [(shape((rows, width), F32), block), (shape((rows, width), BF), block)], [], [x, mine, theirs, vec], 10 * rows * width, 3_000_000,
    )


def norm_back(grad, x, gain):
    unit, scale = unit_rows(x)
    weighted = grad * gain
    return scale * (weighted - jnp.mean(weighted, axis=-1, keepdims=True) - unit * jnp.mean(weighted * unit, axis=-1, keepdims=True))


def norm_grad_kernel(sc_ref, dy_ref, mid_ref, mine_ref, theirs_ref, vec_ref, dmid_ref, dz_ref):
    dmid = wide(dy_ref[...]) + norm_back(wide(mine_ref[...]) + wide(theirs_ref[...]), mid_ref[...], vec_ref[5:6])
    dmid_ref[...] = dmid
    dz_ref[...] = low(dmid)


def norm_two_grad(scalars, index, dy, mid, mine, theirs, vec):
    rows, width = mid.shape
    block = pl.BlockSpec((rows, width), lambda i, sc: (0, 0))
    return call(
        norm_grad_kernel, "norm_two_grad", scalars, (1,),
        [row_block(dy, lambda i, sc: index), block, block, block, whole(vec)],
        [(shape((rows, width), F32), block), (shape((rows, width), BF), block)], [], [dy, mid, mine, theirs, vec], 20 * rows * width, 3_000_000,
    )


def mlp_kernel(last, sc_ref, a_ref, b_ref, dy_ref, ua_ref, ub_ref, da_ref, db_ref, bias_ref, *refs):
    refs = list(refs)
    done = [refs.pop(0) for _ in range(2 if last else 0)]
    keep_ref, send_ref, act_ref, pre_ref, down_keep, down_send, x_s = refs
    g = pl.program_id(0)
    part = ua_ref.shape[0]

    @pl.when(g == 0)
    def _():
        x_s[...] = a_ref[...]

    @pl.when(g == 1)
    def _():
        x_s[...] = b_ref[...]

    x, dy = x_s[...], dy_ref[...]
    pre = dot(x[:, :part], ua_ref[...]) + dot(x[:, part:], ub_ref[...]) + bias_ref[...]
    cdf = 0.5 + 0.5 * lax.erf(pre * (2.0**-0.5))
    act = low(pre * cdf)
    act_ref[...] = act
    slope = cdf + pre * (jnp.exp2(pre * pre * (-0.5 * LOG2E)) * 0.3989422804014327)
    grad = dot(dy[:, :part], da_ref[...], 1, 1) + dot(dy[:, part:], db_ref[...], 1, 1)
    dpre = low(grad * slope)
    pre_ref[...] = dpre
    to = slice(TILE, 2 * TILE) if last else slice(0, TILE)
    for n, (ref, down) in enumerate(((keep_ref, down_keep), (send_ref, down_send))):

        @pl.when(g == n)
        def _(n=n, ref=ref, down=down):
            ref[:, :part] = low(dot(dpre, ua_ref[...], 1, 1))
            ref[:, part:] = low(dot(dpre, ub_ref[...], 1, 1))
            if last:
                down[:TILE] = done[n][...]
            down[to, :part] = low(dot(act, da_ref[...]))
            down[to, part:] = low(dot(act, db_ref[...]))


def mlp(scalars, first, stride, own, other, dy, ua, ub, da, db, bias, done):
    width, units = own.shape[1], ua.shape[1]
    tile = lambda n: pl.BlockSpec((TILE, n), lambda i, sc: (i, 0))
    fixed = lambda n: (shape((n, width), BF), pl.BlockSpec((n, width), lambda i, sc: (0, 0)))
    size = 2 * TILE if done else TILE
    weights = [ua, ub, da, db, bias, *done]
    return call(
        functools.partial(mlp_kernel, len(done) > 0), "mlp", scalars, (2,),
        [whole(own), whole(other), row_block(dy, lambda i, sc: first + stride * i)] + [whole(v) for v in weights],
        [fixed(TILE)] * 2 + [(shape((2 * TILE, units), BF), tile(units))] * 2 + [fixed(size)] * 2,
        [pltpu.VMEM((TILE, width), BF)], [own, other, dy, *weights], 8 * 2 * TILE * width * units, 8_000_000,
    )


def share_kernel(blocks, final, tiles, sc_ref, *refs):
    refs = list(refs)
    take = lambda n: [refs.pop(0) for _ in range(n)]
    dqs, outs, dzs, before = (take(2), take(2), take(4), take(2)) if final else ([], [], [], [])
    dks, dvs, norms = take(2), take(2), take(blocks)
    wa_ref, wb_ref = take(2)
    share_ref = take(1)[0]
    own_ref, other_ref, sums, rows_ref = take(4) if final else take(2) + [None, None]
    w_s, a_s = take(2)
    t_s, q_s, o_s, z_s = take(4) if final else [own_ref, None, None, None]
    sums = sums if final else other_ref
    j = pl.program_id(0)
    local = dks[0].shape[1]
    part = wa_ref.shape[0]
    kinds = 3 if final else 2
    skip = 3 - kinds
    lead = 2 if final else 0

    @pl.when(j == 0)
    def _():
        if final:
            t_s[: lead * local] = jnp.zeros_like(t_s[: lead * local])
            t_s[lead * local :] = before[0][...]
            sums[...] = before[1][...]
            rows_ref[...] = jnp.zeros_like(rows_ref)
        else:
            t_s[...] = jnp.zeros_like(t_s)
            sums[...] = jnp.zeros_like(sums)
        for n in range(kinds):
            cols = slice((n + skip) * local, (n + skip + 1) * local)
            w_s[n, :part] = wa_ref[:, cols]
            w_s[n, part:] = wb_ref[:, cols]

    for b in range(blocks):

        @pl.when((j >= b * tiles) & (j < (b + 1) * tiles))
        def _(b=b):
            a_s[...] = norms[b][...]

    a = a_s[...]
    parts = []
    if final:
        for n in range(4):

            @pl.when(j == n)
            def _(n=n):
                q_s[...] = dqs[n % 2][...]
                o_s[...] = outs[n % 2][...]
                z_s[...] = dzs[(n % 2) * 2 + n // 2][...]

        parts.append(q_s[...])
        z = z_s[...]
        t_s[:local] += dot(o_s[...], z, 0, 0)
        rows_ref[0:1, :] += jnp.sum(wide(z), axis=0, keepdims=True)
    total = lambda group: low(sum(wide(r[...]) for r in group))
    parts += [total(dks), total(dvs)]
    share_ref[...] = low(sum(dot(p, w_s[n], 1, 1) for n, p in enumerate(parts)))
    for n, p in enumerate(parts):
        at = (n + (1 if final else 0)) * local
        t_s[at : at + local] += dot(p, a, 0, 0)
        sums[n + skip : n + skip + 1, :] += jnp.sum(wide(p), axis=0, keepdims=True)

    if final:

        @pl.when(j == pl.num_programs(0) - 1)
        def _():
            own_ref[...] = t_s[:, :part].T
            other_ref[...] = low(t_s[:, part:].T)


def shares(scalars, start, dqs, outs, dzs, before, dks, dvs, norms, wa, wb):
    rows, width = norms[0].shape
    local = dks[0].shape[1]
    part = wa.shape[0]
    tiles, blocks, final = rows // TILE, len(norms), len(dqs) > 0
    kinds = 3 if final else 2
    fixed = lambda dims: pl.BlockSpec(dims, lambda i, sc: (0,) * len(dims))
    ins = [row_block(v, lambda i, sc: i // 2) for v in dqs + outs] + [whole(v) for v in dzs + before]
    ins += [row_block(v, lambda i, sc: i + start) for v in dks + dvs]
    ins += [row_block(v, lambda i, sc, b=b: jnp.clip(i - b * tiles, 0, tiles - 1)) for b, v in enumerate(norms)]
    ins += [whole(wa), whole(wb)]
    results = [(shape((blocks * rows, width), BF), pl.BlockSpec((TILE, width), lambda i, sc: (i % tiles * blocks + i // tiles, 0)))]
    scratch = [pltpu.VMEM((kinds, width, local), BF), pltpu.VMEM((TILE, width), BF)]
    if final:
        results += [(shape((part, 4 * local), F32), fixed((part, 4 * local))), (shape((part, 4 * local), BF), fixed((part, 4 * local)))]
        results += [(shape((8, local), F32), fixed((8, local))), (shape((8, width), F32), fixed((8, width)))]
        scratch += [pltpu.VMEM((4 * local, width), F32), pltpu.VMEM((TILE, local), BF), pltpu.VMEM((TILE, local), BF), pltpu.VMEM((TILE, width), BF)]
    else:
        results += [(shape((2 * local, width), F32), fixed((2 * local, width))), (shape((8, local), F32), fixed((8, local)))]
    return call(
        functools.partial(share_kernel, blocks, final, tiles), "share" if final else "share_seen", scalars, (blocks * tiles,), ins, results, scratch,
        [in_hbm(v) if final else v for v in dqs + outs + dzs + before + dks + dvs + norms] + [wa, wb], 4 * blocks * rows * width * local * kinds, 8_000_000, 32,
    )


def place_kernel(pieces, which, sc_ref, *refs):
    out_ref, x_s = refs[pieces], refs[pieces + 1]
    j = pl.program_id(0)
    f = sc_ref[5]
    part = out_ref.shape[1] // 2
    for n in range(pieces):

        @pl.when(j == n)
        def _(n=n):
            x_s[...] = refs[n][...].astype(x_s.dtype)

    out_ref[:, pl.ds(pl.multiple_of(f * part, 128), part)] = x_s[:, :part]
    out_ref[:, pl.ds(pl.multiple_of((1 - f) * part, 128), part)] = x_s[:, part:]


def placed(scalars, which, pieces, kind):
    width = pieces[0][0].shape[1]
    ins = [pl.BlockSpec((TILE, width), lambda i, sc, n=n: (n, 0)) for _, n in pieces]
    rows = TILE * len(pieces)
    return call(
        functools.partial(place_kernel, len(pieces), which), "placed", scalars, (len(pieces),), ins,
        [(shape((rows, width), kind), pl.BlockSpec((TILE, width), lambda i, sc: (i ^ sc[which], 0)))],
        [pltpu.VMEM((TILE, width), kind)], [v for v, _ in pieces], 0, 6_000_000,
    )[0]


def pack_kernel(n, *refs):
    out_ref, row_s = refs[-2], refs[-1]
    row_s[...] = jnp.zeros_like(row_s)
    for k in range(n):
        row_s[k : k + 1, :] = wide(refs[k][...])
    top = n
    for ref in refs[n:-2]:
        row_s[top : top + ref.shape[0], : ref.shape[1]] = wide(ref[...])
        top += ref.shape[0]
    out_ref[...] = low(row_s[...])


def packed(vectors, folds):
    part = vectors[0].shape[0]
    args = [v.reshape(1, part) for v in vectors] + [v.reshape(-1, v.shape[-1]) for v in folds]
    rows = len(vectors) + sum(v.shape[0] for v in args[len(vectors) :])
    rows += -rows % 16
    return pl.pallas_call(
        functools.partial(pack_kernel, len(vectors)), name="packed", out_shape=shape((rows, part), BF),
        scratch_shapes=[pltpu.VMEM((rows, part), F32)],
        compiler_params=pltpu.CompilerParams(vmem_limit_bytes=8 << 20),
        cost_estimate=pl.CostEstimate(flops=0, bytes_accessed=100_000, transcendentals=0),
    )(*args)


def unpack_kernel(sizes, sc_ref, a_ref, b_ref, vec_ref, qkv_ref, up_ref):
    f = sc_ref[5]
    a, b = wide(a_ref[...]), wide(b_ref[...])
    lo, hi = jnp.where(f == 0, a, b), jnp.where(f == 0, b, a)
    part = a.shape[1]
    n = 6
    vec_ref[0:2, :part], vec_ref[0:2, part:] = lo[0:2], hi[0:2]
    vec_ref[2:8, :part], vec_ref[2:8, part:] = a[0:6], b[0:6]
    lanes = HD // 2
    for ref, start, count in ((qkv_ref, n, sizes[0]), (up_ref, n + sizes[0], sizes[1])):
        ref[...] = jnp.concatenate([p[start + k : start + k + 1, :lanes] for k in range(count) for p in (lo, hi)], axis=1)


def unpacked(scalars, a, b, sizes):
    outs = [shape((8, 2 * a.shape[1]), F32), shape((1, sizes[0] * HD), F32), shape((1, sizes[1] * HD), F32)]
    fixed = [(o, pl.BlockSpec(o.shape, lambda i, sc: (0, 0))) for o in outs]
    return call(functools.partial(unpack_kernel, sizes), "unpacked", scalars, (1,), [whole(a), whole(b)], fixed, [], [a, b], 0, 100_000, 8)


def weights_kernel(pieces, order, sc_ref, *refs):
    refs = list(refs)
    a_refs = [refs.pop(0) for _ in range(pieces)]
    dy_ref = refs.pop(0)
    pre_refs, act_refs = [refs.pop(0) for _ in range(2)], [refs.pop(0) for _ in range(2)]
    own_up, other_up, own_down, other_down, sum_ref, a_s, d_s, p_s, c_s = refs
    j = pl.program_id(0)

    @pl.when(j == 0)
    def _():
        for n in range(pieces):
            to = slice(n * TILE, (n + 1) * TILE)
            a_s[to, :] = a_refs[n][...]
            d_s[to, :] = dy_ref[order[n] * TILE : (order[n] + 1) * TILE, :]
        for n in range(2):
            to = slice(n * 2 * TILE, (n + 1) * 2 * TILE)
            p_s[to, :] = pre_refs[n][...]
            c_s[to, :] = act_refs[n][...]
        sum_ref[...] = jnp.zeros_like(sum_ref)
        sum_ref[0:1, :] = jnp.sum(wide(p_s[...]), axis=0, keepdims=True)
        sum_ref[1:2, :] = jnp.sum(wide(d_s[...]), axis=0, keepdims=True)

    part = own_up.shape[0]
    cols = pl.ds(pl.multiple_of((1 - j) * part, 128), part)
    up = dot(a_s[:, cols], p_s[...], 0, 0)
    down = dot(c_s[...], d_s[:, cols], 0, 0)

    @pl.when(j == 0)
    def _():
        other_up[...] = low(up)
        other_down[...] = low(down)

    @pl.when(j == 1)
    def _():
        own_up[...] = up
        own_down[...] = down


def mlp_weights(scalars, twos, dy, order, pres, acts):
    rows, width = dy.shape
    units = pres[0].shape[1]
    part = width // 2
    outs = [shape(dims, kind) for dims in ((part, units), (units, part)) for kind in (F32, BF)] + [shape((8, max(width, units)), F32)]
    fixed = [(o, pl.BlockSpec(o.shape, lambda i, sc: (0, 0))) for o in outs]
    args = [in_hbm(v) for v in twos + [dy] + pres + acts]
    scratch = [pltpu.VMEM((rows, n), BF) for n in (width, width, units, units)]
    return call(
        functools.partial(weights_kernel, len(twos), order), "mlp_weights", scalars, (2,), [whole(v) for v in args], fixed, scratch, args,
        4 * rows * width * units, 12_000_000, 40,
    )


PAIR = [(0, 1), (1, 0)]


def swap_core(values):
    return lax.ppermute(values, "tp", [(i, i ^ 1) for i in range(4)])


def swap_y(values):
    return lax.ppermute(values, "tp", [(i, i ^ 2) for i in range(4)])


def hop(values, pairs):
    return lax.ppermute(values, "ctx", pairs)


def after(values, *deps):
    return lax.optimization_barrier((values, *deps))[0]


def pick(parts, index):
    return lax.dynamic_index_in_dim(parts, index, 0, keepdims=False)


def ordered(first, second, flip):
    return jnp.where(flip == 0, jnp.stack([first, second]), jnp.stack([second, first]))


def body(
    hidden,
    prefix,
    w_qkv,
    b_qkv,
    w_out,
    b_out,
    w_up,
    b_up,
    w_down,
    b_down,
    ln1_gain,
    ln1_shift,
    ln2_gain,
    ln2_shift,
    cotangent,
):
    members = lax.axis_size("fsdp")
    paired = members == 2
    z = lax.axis_index("ctx")
    t = lax.axis_index("tp")
    half_ctx = lax.axis_size("ctx") // 2
    core, side = t & 1, t >> 1
    turn_q, turn_k = 2 * core, 2 * core + side
    f = lax.axis_index("fsdp") if paired else jnp.int32(0)
    rows, width = hidden.shape[1], hidden.shape[2]
    local, units = w_qkv.shape[2], w_up.shape[1]
    half, quarter, part = rows // 2, rows // 4, width // 2
    tiles = rows // TILE
    scalars = jnp.stack([z, turn_q, turn_k, prefix[0], jnp.int32(half_ctx), f]).astype(jnp.int32)

    def both(values, axis):
        if paired:
            return values, lax.ppermute(values, "fsdp", PAIR)
        return tuple(jnp.split(lax.all_gather(values, "fsdp", axis=axis, tiled=True), 2, axis=axis))

    qkv_own = w_qkv.reshape(w_qkv.shape[0], 3 * local)
    qkv_a, qkv_b = both(qkv_own, 0)
    own_quarter = lax.dynamic_slice(hidden[0], (turn_k * quarter, 0), (quarter, width))
    first = hop(own_quarter, [(2, 1), (3, 2)])
    aside = hop(own_quarter, [(2, 3)])

    def spread(values, *deps):
        other = swap_y(values)
        ours = after((values, other), *deps)
        return [(v, 0) for v in (values, other, swap_core(ours[0]), swap_core(ours[1]))]

    vectors_in = (ln1_gain, ln1_shift, b_out, ln2_gain, ln2_shift, b_down)
    fold_rows = (b_qkv.size // b_qkv.shape[-1], b_up.shape[0])
    if paired:
        small = packed(vectors_in, (b_qkv, b_up))
        small_b = lax.ppermute(after(small, qkv_b), "fsdp", PAIR)
        vec, bias_qkv, bias_up = unpacked(scalars, small, small_b, fold_rows)
    else:
        small_b = qkv_b
        gather = lambda v: wide(lax.all_gather(v, "fsdp", axis=v.ndim - 1, tiled=True))
        found = [gather(v) for v in vectors_in]
        vec = jnp.stack(found[:2] + found)
        bias_qkv, bias_up = gather(b_qkv).reshape(1, -1), gather(b_up).reshape(1, -1)
    gain_one, shift_one, gain_two, shift_two, bias_down = vec[2], vec[3], vec[5], vec[6], vec[7]
    far_quarter = first + aside
    second = hop(after(first, qkv_b), [(1, 0), (2, 1)])
    far_pieces = spread(far_quarter)
    later = after((w_out, w_up, w_down), qkv_b)
    out_a, out_b = both(later[0], 1)
    up_a, up_b = both(later[1], 0)
    down_a, down_b = both(after(later[2], out_b), 1)

    lane = jnp.arange(local, dtype=jnp.int32) % (HD // 2)
    frequency = jnp.power(jnp.float32(10000.0), -2.0 * wide(lane) / HD)[None, :]
    base = wide(jnp.arange(TILE, dtype=jnp.int32))[:, None] * frequency
    turns = wide(jnp.arange(half_ctx * tiles, dtype=jnp.int32) * TILE)[:, None] * frequency
    base, turns = jnp.stack([jnp.cos(base), jnp.sin(base)]), jnp.stack([jnp.cos(turns), jnp.sin(turns)])

    q, k_own, v_own, norm_own, x_turned, dy = project(
        scalars, [hidden[0]], cotangent[0], False, rows, vec, qkv_a, qkv_b, bias_qkv, base, turns
    )
    near_quarter = jnp.where(z >= half_ctx, own_quarter, after(second, q))
    k_far, v_far, norm_far = project(scalars, far_pieces, None, True, rows, vec, qkv_a, qkv_b, after(bias_qkv, q, up_b), base, turns)
    near_pieces = spread(after(near_quarter, far_pieces[1][0]), k_far)
    k_near, v_near, norm_near = project(scalars, near_pieces, None, False, rows, vec, qkv_a, qkv_b, after(bias_qkv, k_far, out_b, down_b), base, turns)
    keys, values = [k_own, k_near, k_far], [v_own, v_near, v_far]

    def core_sum(kept, sent):
        return low(wide(kept) + wide(swap_core(sent)))

    o0, lse0, *share = attention(scalars, 0, 2, q, keys, values, out_a, out_b)
    mine0 = core_sum(*share)
    o1, lse1, *share = attention(scalars, 1, 2, after(q, mine0, up_b), keys, values, out_a, out_b)
    mine1 = core_sum(*share)
    mid0, two0 = norm_two(scalars, 0, x_turned, mine0, swap_y(mine0), vec)
    twos0 = (two0, swap_core(two0))
    *share, act0, pre0, down_keep, down_send = mlp(scalars, 0, 2, after(twos0[0], mine1), twos0[1], dy, up_a, up_b, down_a, down_b, bias_up, [])
    back0 = core_sum(*share)
    mid1, two1 = norm_two(scalars, 1, x_turned, mine1, swap_y(mine1), vec)
    twos1 = (two1, swap_core(two1))
    *share, act1, pre1, down_keep, down_send = mlp(scalars, 1, 2, *twos1, dy, up_a, up_b, down_a, down_b, bias_up, [down_keep, down_send])
    back1 = core_sum(*share)
    back_y0, back_y1 = swap_y(back0), swap_y(back1)

    dmid0, dz0 = norm_two_grad(scalars, 0, dy, mid0, back0, back_y0, vec)
    dzs0 = (dz0, swap_core(dz0))
    act0, act1, pre0, pre1 = after((act0, act1, pre0, pre1), back1, dz0)
    *g_mlp, sums_mlp = mlp_weights(scalars, list(twos0) + list(twos1), dy, (0, 2, 1, 3), [pre0, pre1], [act0, act1])

    def partner_sum(own_part, other_part, dim=0):
        if paired:
            return own_part + wide(lax.ppermute(other_part, "fsdp", PAIR))
        return lax.psum_scatter(jnp.concatenate([own_part, wide(other_part)], axis=dim), "fsdp", scatter_dimension=dim, tiled=True)

    near_bit, far_bit = z & 1, z >> 1
    near_pairs, far_pairs = [(i, i ^ 1) for i in range(4)], [(i, i ^ 2) for i in range(4)]

    def split(values, bit):
        grid = values.reshape(2, values.shape[0] // 2, values.shape[1])
        return pick(grid, bit), low(pick(grid, 1 - bit))

    def join(values, sent, pairs, bit):
        return ordered(values, hop(sent, pairs), bit).reshape(2 * values.shape[0], values.shape[1])

    down = core_sum(down_keep, after(down_send, dz0))
    dmid1, dz1 = norm_two_grad(scalars, 1, dy, mid1, back1, back_y1, vec)
    dzs1 = (dz1, swap_core(dz1))
    dq0, dk0, dv0 = attention_grads(scalars, 0, 2, after(q, g_mlp[1], down), o0, *dzs0, lse0, keys, values, out_a, out_b, base, turns)
    down_y = swap_y(down)
    up_sum = partner_sum(after(g_mlp[0], dk0), g_mlp[1])
    up_keep, up_send = split(up_sum, near_bit)
    dq1, dk1, dv1 = attention_grads(scalars, 1, 2, after(q, dk0, up_send, down_y), o1, *dzs1, lse1, keys, values, out_a, out_b, base, turns)
    up_half = after(up_keep, dk1) + wide(hop(up_send, near_pairs))
    up_keep, up_send = split(up_half, far_bit)
    down_sum = partner_sum(after(g_mlp[2], dk1), after(g_mlp[3], up_sum), 1)
    down_part, down_send = split(down_sum, near_bit)
    result_half = low(jnp.concatenate([after(mid0, dk1), mid1], axis=0) + (wide(down) + wide(down_y)) + bias_down)
    other = swap_core(result_half)
    dk1 = after(dk1, up_send, down_send, result_half)
    result = placed(scalars, 1, [(result_half, 0), (result_half, 1), (other, 0), (other, 1)], BF)

    dks, dvs = [dk0, dk1], [dv0, dv1]
    seen, t_seen, sums_seen = shares(scalars, tiles, [], [], [], [], dks, dvs, [norm_near, norm_far], qkv_a, qkv_b)
    def core_halves(kept, sent):
        got = swap_core(sent)
        return [low(wide(kept[n : n + quarter]) + wide(got[n : n + quarter])) for n in (0, quarter)]

    seen_got = swap_core(seen[rows:])
    near_keep, far_keep, seen_send = (
        low(wide(seen[to]) + wide(seen_got[to])) for to in (slice(quarter), slice(quarter, half), slice(half, rows))
    )
    seen_y = swap_y(seen_send)
    share_own, g_two, g_two_other, sums, sums_out = shares(
        scalars, 0, after([dq0, dq1], seen_send), [o0, o1], [*dzs0, *dzs1], [t_seen, sums_seen], dks, dvs, [norm_own], qkv_a, qkv_b
    )
    near_q = low(wide(after(near_keep, g_two_other)) + wide(seen_y[:quarter]))
    up_quarter = low(after(up_keep, near_q) + wide(hop(up_send, far_pairs)))
    down_half = after(down_part, near_q) + wide(hop(down_send, near_pairs))
    down_part, down_send = split(down_half, far_bit)
    near_in = hop(near_q, [(0, 1), (1, 3)])
    two_sum = partner_sum(after(g_two, near_in), g_two_other)
    far_q = wide(after(far_keep, two_sum)) + wide(seen_y[quarter:])
    far_q = low(far_q + jnp.where(z == 1, wide(near_in), 0.0))
    far_in = wide(hop(far_q, [(1, 2)])) + wide(hop(far_q, [(3, 2)]))
    own_low, own_high = core_halves(share_own[:half], share_own[half:])
    own_send = jnp.where(side == 0, own_high, own_low)
    da_one = wide(jnp.where(side == 0, own_low, own_high)) + wide(swap_y(after(own_send, far_q)))
    da_one = da_one + far_in + jnp.where(z >= half_ctx, wide(near_q) + jnp.where(z == 3, wide(near_in), 0.0), 0.0)
    x_q = wide(lax.dynamic_slice(x_turned, (side * quarter, 0), (quarter, width)))
    grad_q = low(jnp.where(side == 0, dmid0, dmid1) + norm_back(da_one, x_q, gain_one))
    grad_y = swap_y(grad_q)
    grad_input = placed(scalars, 2, [(v, 0) for v in (grad_q, grad_y, swap_core(grad_q), swap_core(grad_y))], F32)

    up_half = join(up_quarter, up_quarter, far_pairs, far_bit)
    up_total = wide(join(up_half, after(up_half, near_q), near_pairs, near_bit))
    down_quarter = low(down_part + wide(hop(down_send, far_pairs)))
    down_half = join(down_quarter, after(down_quarter, near_q), far_pairs, far_bit)
    down_total = wide(join(down_half, after(down_half, far_q), near_pairs, near_bit))
    two_keep, two_send = split(two_sum, near_bit)
    two_half = two_keep + wide(hop(two_send, near_pairs))
    two_keep, two_send = split(two_half, far_bit)
    two_quarter = low(two_keep + wide(hop(two_send, far_pairs)))
    two_back = join(two_quarter, two_quarter, far_pairs, far_bit)
    second_group = wide(join(two_back, two_back, near_pairs, near_bit))

    def gain_grad(weights, grad, bias_grad, gain, shift):
        full = wide(jnp.concatenate(weights, axis=0))
        by_shift = jnp.sum(full * bias_grad[None, :], axis=1)
        return (jnp.sum(full * grad, axis=1) - shift * by_shift) / gain, by_shift

    g_own, g_two, sums_mlp, sums, sums_out = after((g_mlp[0], g_two, sums_mlp, sums, sums_out), two_half)
    joined = lambda own, other, cols: jnp.concatenate([own[:, cols], wide(other[:, cols])], axis=0)
    gb_up, gb_down, gb_out, gb_qkv = sums_mlp[0], sums_mlp[1] * 0.25, sums_out[0] * 0.25, sums[:3].reshape(-1)
    g_gain_one, g_shift_one = gain_grad((qkv_a, qkv_b), joined(g_two, g_two_other, slice(local, None)), gb_qkv, gain_one, shift_one)
    g_gain_two, g_shift_two = gain_grad((up_a, up_b), joined(g_own, g_mlp[1], slice(None)), gb_up, gain_two, shift_two)
    over_tp = after(jnp.stack([gb_out, gb_down, g_gain_one, g_shift_one, g_gain_two, g_shift_two]), near_q)
    over_tp = over_tp + swap_core(over_tp)
    over_tp = over_tp + swap_y(over_tp)
    if paired:
        take = lambda v, n: lax.dynamic_index_in_dim(v.reshape(-1, 2, HD // 2), n, 1, keepdims=False).reshape(-1)
        mine = jnp.concatenate([over_tp[:, :part].reshape(-1), take(gb_qkv, f), take(gb_up, f)])
        other = jnp.concatenate([over_tp[:, part:].reshape(-1), take(gb_qkv, 1 - f), take(gb_up, 1 - f)])
        vectors = mine + lax.ppermute(other, "fsdp", PAIR)
    else:
        scattered = [
            lax.psum_scatter(v, "fsdp", scatter_dimension=1, tiled=True).reshape(-1)
            for v in (over_tp, gb_qkv.reshape(-1, HD), gb_up.reshape(-1, HD))
        ]
        vectors = jnp.concatenate(scattered)
    vectors = vectors + hop(vectors, [(i, i ^ 1) for i in range(4)])
    vectors = vectors + hop(vectors, [(i, i ^ 2) for i in range(4)])
    own = width // members
    named = vectors[: 6 * own].reshape(6, own)
    cut = 6 * own + b_qkv.size
    return (
        result[None],
        grad_input[None],
        second_group[:, local:].reshape(w_qkv.shape),
        vectors[6 * own : cut].reshape(b_qkv.shape),
        second_group[:, :local].T,
        named[0],
        up_total,
        vectors[cut:].reshape(b_up.shape),
        down_total,
        named[1],
        named[2],
        named[3],
        named[4],
        named[5],
    )


def solution(mesh):
    rows = P("fsdp", "ctx", None)
    weights = (P("fsdp", None, "tp"), P(None, "tp", "fsdp"), P("tp", "fsdp"), P("fsdp"), P("fsdp", "tp"), P("tp", "fsdp"), P("tp", "fsdp"))
    vectors = (P("fsdp"),) * 5
    return jax.shard_map(
        body,
        mesh=mesh,
        in_specs=(rows, P("fsdp")) + weights + vectors + (rows,),
        out_specs=(rows, rows) + weights + vectors,
        check_vma=False,
    )
```
